32 devices in a mesh: slab: 16 (over z, y, x), col: 2 (over core).
Axes of the slice: x: 2, y: 2, z: 4, core: 2. Of those that a mesh axis runs over, the one named last changes fastest.
Arguments:
- direction: float32 [2048, 4096], P('slab', 'col'), may hold values from -6 to 6
- kappa: float32 [2048, 4096], P('slab', 'col'), may hold values from 0.04 to 0.24
- land_mask: int32 [2048, 4096], P('slab', 'col'), may hold values 0 or 1
- owned_segments: int32 [256], replicated, may hold values from -1 to 127, as said below
- seg_anchor: int32 [128, 2], replicated, may hold values from 0 to 31, as said below
- interp_index: int32 [128, 32], replicated, may hold values from 0 to 15
- interp_table: bfloat16 [16, 64, 64], replicated, may hold values from -0.75 to 0.75
- precision: bfloat16 [2048, 2048], replicated, as said below
- obs_scale: float32 [256, 2048], P(('slab', 'col')), may hold values from 0.4 to 2
Outputs:
- product: float32 [2048, 4096], P('slab', 'col')
The draws below stay inside these ranges and needn't reach their ends.
Inputs may be any that keep to these rules, and one draw needn't show every extreme that they name: `owned_segments`: slots d * 8 to (d + 1) * 8 - 1 belong to device d = slab index * 2 + col index, used slots first; each segment stands in exactly one slot, empty slots hold -1; a device's segments have column tiles held by devices of its own col index; the two devices of one col index at slab indices 2t and 2t + 1 hold 8 segments together; some device fills all 8 slots; at most 8 segments of one device share a first row tile, and some device has that many. `seg_anchor`: number the used slots of one col index in order of slab index, then slot, as ranks r = 0, 1, ...; the segment at rank r has first row tile 32 * ((r + r // (the number of slab indices)) % 1). `precision`: Symmetric.
All inputs are finite; a program needn't handle non-finite values. No bound on the sum of `land_mask` on one device may be relied on, other than what follows from the above.
Results may differ from the reference program's by a relative error of at most 0.0019.
Values may be sent and summed in bfloat16 or wider, within the bound.
No kernel may reach another device: no remote copies, remote signals or barrier semaphores. Data moves between devices by JAX's collectives and lax.ppermute only.
A program may use at most 128 MiB of HBM per device.

```python
import math
import jax
import jax.numpy as jnp
from jax import lax

SEG_DEV = 4
TILE_R = 64
TILE_C = 128
SEG_ROWS = 2048
SWEEPS = 4
NB = 16
NR = 2048
NC = 4096
SEG_TILES = 32
NCTL = 16
LANES = 1
SEGS = 128
SEG_MAX = 8
SLOTS = 256
N_SLAB = 16
N_COL = 2
DEVICES = 32


def layout_tables(key):
    base = jax.random.fold_in(key, 7)
    key_load, key_perm, key_cols = jax.random.split(base, 3)
    pairs = N_SLAB // 2
    spread = jax.random.randint(key_load, (pairs, N_COL), -SEG_DEV, SEG_DEV + 1)
    spread = spread.at[0, 0].set(SEG_DEV)
    loads = jnp.stack([SEG_DEV + spread, SEG_DEV - spread], axis=1).reshape(N_SLAB, N_COL).astype(jnp.int32)
    col_offsets = (jnp.cumsum(loads, axis=0) - loads).reshape(DEVICES)
    flat_loads = loads.reshape(DEVICES)
    offsets = jnp.cumsum(flat_loads) - flat_loads
    slot_index = jnp.arange(SEG_MAX, dtype=jnp.int32)
    is_used = slot_index[None, :] < flat_loads[:, None]
    shuffled = jax.random.permutation(key_perm, SEGS).astype(jnp.int32)
    position = jnp.minimum(offsets[:, None] + slot_index[None, :], SEGS - 1)
    segment = jnp.where(is_used, shuffled[position], -1)
    col_rank = col_offsets[:, None] + slot_index[None, :]
    lane_of = (col_rank + col_rank // N_SLAB) % LANES
    device_col = jnp.arange(DEVICES, dtype=jnp.int32) % N_COL
    col_tile = device_col[:, None] * NCTL + jax.random.randint(key_cols, (DEVICES, SEG_MAX), 0, NCTL)
    values = jnp.stack([lane_of * SEG_TILES, col_tile], axis=-1).astype(jnp.int32)
    target = jnp.where(is_used, segment, SEGS).reshape(-1)
    anchor = jnp.zeros((SEGS, 2), jnp.int32).at[target].set(values.reshape(-1, 2), mode='drop')
    return (segment.reshape(SLOTS).astype(jnp.int32), anchor)


def draw_owned_segments(key, part):
    return layout_tables(key)[0]


def draw_seg_anchor(key, part):
    return layout_tables(key)[1]


def draw_precision(key, part):
    order = SEG_ROWS
    noise = jax.random.normal(key, (order, order), jnp.float32)
    symmetric = (noise + noise.T) * (0.35 / jnp.sqrt(2.0 * order))
    return (jnp.eye(order, dtype=jnp.float32) + symmetric).astype(jnp.bfloat16)


def with_ends(array, stream_key, low, largest):
    dims = array.shape
    index_at = [jax.random.randint(jax.random.fold_in(stream_key, axis), (), 0, dims[axis]) for axis in range(len(dims))]
    array = array.at[tuple(index_at)].set(low)
    longest = dims.index(max(dims))
    index_at[longest] = (index_at[longest] + 1) % dims[longest]
    return array.at[tuple(index_at)].set(largest)


def steps_of(rng, dims, cuts, smallest, largest):
    level = 1.0
    for dim, shards_of in cuts:
        draws = jax.random.uniform(jax.random.fold_in(jax.random.fold_in(rng, 6), dim), (shards_of,), jnp.float32, smallest / len(cuts), largest / len(cuts))
        level = level * jnp.repeat(jnp.exp(draws), dims[dim] // shards_of).reshape((-1,) + (1,) * (len(dims) - 1 - dim))
    return level


def gaussian(rng, dims, width, limit, cuts=(), kind=jnp.bfloat16):
    level = steps_of(rng, dims, cuts, -0.22, 0.18) if cuts else 1.0
    values = jax.random.normal(rng, dims, jnp.float32) * width * level
    return jnp.minimum(jnp.maximum(values, -limit), limit).astype(kind)


def setup_inputs(seed: int = 0) -> dict:
    streams_of = jax.random.split(jax.random.key(seed), 10)
    return {
        "direction": gaussian(streams_of[0], (NR, NC), 1.0, 6.0, ((0, 16), (1, 2)), jnp.float32),
        "kappa": jnp.clip(jnp.exp(math.log(0.24) - 1.7917595 * jax.random.uniform(streams_of[1], (NR, NC), jnp.float32) ** steps_of(streams_of[1], (NR, NC), ((0, 16), (1, 2)), -0.2, 0.2)), 0.04, 0.24),
        "land_mask": with_ends((jax.random.randint(streams_of[2], (NR, NC), 0, 8) < 7).astype(jnp.int32), jax.random.fold_in(streams_of[2], 1), 0, 1),
        "owned_segments": draw_owned_segments(jax.random.fold_in(streams_of[9], 71), 0),
        "seg_anchor": draw_seg_anchor(jax.random.fold_in(streams_of[9], 71), 0),
        "interp_index": with_ends(jax.random.randint(streams_of[5], (SEGS, SEG_TILES), 0, NB), jax.random.fold_in(streams_of[5], 1), 0, NB - 1).astype(jnp.int32),
        "interp_table": gaussian(streams_of[6], (NB, TILE_R, TILE_R), TILE_R ** -0.5, 0.75),
        "precision": draw_precision(jax.random.fold_in(streams_of[9], 71), 0),
        "obs_scale": jnp.clip(jnp.exp(math.log(2.0) - 1.609438 * jax.random.uniform(streams_of[8], (SLOTS, SEG_ROWS), jnp.float32) ** steps_of(streams_of[8], (SLOTS, SEG_ROWS), ((0, 32),), -0.2, 0.2)), 0.4, 2.0),
    }


def diffuse_once(field, coeff):
    center_k = coeff[1:-1, 1:-1]
    center_u = field[1:-1, 1:-1]

    def face_weight(other_k):
        return jnp.where((center_k > 0) & (other_k > 0), 0.5 * (center_k + other_k), 0.0)

    result = center_u + face_weight(coeff[:-2, 1:-1]) * (field[:-2, 1:-1] - center_u)
    result = result + face_weight(coeff[2:, 1:-1]) * (field[2:, 1:-1] - center_u)
    result = result + face_weight(coeff[1:-1, :-2]) * (field[1:-1, :-2] - center_u)
    result = result + face_weight(coeff[1:-1, 2:]) * (field[1:-1, 2:] - center_u)
    return result


def smoothing(field, coeff):
    padded_k = jnp.pad(coeff, 1)
    current = field
    for sweep_index in range(SWEEPS):
        current = diffuse_once(jnp.pad(current, 1), padded_k)
    return current


def reference(direction, kappa, land_mask, owned_segments, seg_anchor, interp_index, interp_table, precision, obs_scale):
    maskf = land_mask.astype(jnp.float32)
    keff = kappa * maskf
    moved = direction * maskf
    smoothed = smoothing(moved, keff).astype(jnp.bfloat16)
    slot_ids = jnp.where(owned_segments >= 0, owned_segments, SEGS).astype(jnp.int32)
    slot_of = jnp.zeros((SEGS,), jnp.int32).at[slot_ids].set(jnp.arange(SLOTS, dtype=jnp.int32), mode="drop")

    def one_segment(grid, segment):
        row_start = (seg_anchor[segment, 0] * TILE_R).astype(jnp.int32)
        col_start = (seg_anchor[segment, 1] * TILE_C).astype(jnp.int32)
        tiles = lax.dynamic_slice(smoothed, (row_start, col_start), (SEG_ROWS, TILE_C))
        tiles = tiles.reshape(SEG_TILES, TILE_R, TILE_C).astype(jnp.float32)
        blocks = interp_table[interp_index[segment]].astype(jnp.float32)
        seg_rows = jnp.einsum("ktr,krc->ktc", blocks, tiles).astype(jnp.bfloat16).reshape(SEG_ROWS, TILE_C)
        scale = obs_scale[slot_of[segment]]
        weighted = (seg_rows.astype(jnp.float32) * scale[:, None]).astype(jnp.bfloat16)
        prod = jnp.dot(precision, weighted, preferred_element_type=jnp.float32)
        zvals = (prod * scale[:, None]).astype(jnp.bfloat16).reshape(SEG_TILES, TILE_R, TILE_C)
        back = jnp.einsum("ktr,ktc->krc", blocks, zvals.astype(jnp.float32)).astype(jnp.bfloat16)
        back = back.reshape(SEG_ROWS, TILE_C).astype(jnp.float32)
        old = lax.dynamic_slice(grid, (row_start, col_start), (SEG_ROWS, TILE_C))
        grid = lax.dynamic_update_slice(grid, old + back, (row_start, col_start))
        return grid, None

    adjoint, unused = lax.scan(one_segment, jnp.zeros((NR, NC), jnp.float32), jnp.arange(SEGS, dtype=jnp.int32))
    return maskf * (moved + smoothing(adjoint, keff))
```

```python
import functools

import jax
import jax.numpy as jnp
from jax import lax
from jax.experimental import pallas as pl
from jax.experimental.pallas import tpu as pltpu
from jax.sharding import PartitionSpec as P

TILE_C = 128
SWEEPS = 4
HALO = 8
PAD = 16
CAP = 3


def lane_iota(shape):
    return lax.broadcasted_iota(jnp.int32, shape, len(shape) - 1)


def row_iota(shape):
    return lax.broadcasted_iota(jnp.int32, shape, len(shape) - 2)


def from_left(own, left):
    lanes = own.shape[-1]
    return pltpu.roll(jnp.where(lane_iota(own.shape) == lanes - 1, left, own), 1, 1)


def from_right(own, right):
    lanes = own.shape[-1]
    return pltpu.roll(jnp.where(lane_iota(own.shape) == 0, right, own), lanes - 1, 1)


def face(own, other):
    return jnp.where((own > 0) & (other > 0), 0.5 * (own + other), 0.0)


def sweep_tile(c, tiles, rows, u_ref, fn_ref, fw_ref, fe_ref):
    left = lax.rem(c + tiles - 1, tiles)
    right = lax.rem(c + 1, tiles)
    body = pl.ds(HALO, rows)
    up = pl.ds(HALO - 1, rows)
    down = pl.ds(HALO + 1, rows)
    u = u_ref[c, body, :]
    west = from_left(u, u_ref[left, body, :])
    east = from_right(u, u_ref[right, body, :])
    out = u + fn_ref[c, body, :] * (u_ref[c, up, :] - u)
    out = out + fn_ref[c, down, :] * (u_ref[c, down, :] - u)
    out = out + fw_ref[c, body, :] * (west - u)
    return out + fe_ref[c, body, :] * (east - u)


def sweeps(tiles, rows, bufs, fn_ref, fw_ref, fe_ref, finish):
    for step in range(SWEEPS):
        src, dst = bufs[step % 2], bufs[1 - step % 2]
        last = step == SWEEPS - 1

        def body(c, carry, src=src, dst=dst, last=last):
            value = sweep_tile(c, tiles, rows, src, fn_ref, fw_ref, fe_ref)
            if last:
                finish(c, value[PAD - HALO : rows - (PAD - HALO), :])
            else:
                dst[c, pl.ds(HALO, rows), :] = value
            return carry

        lax.fori_loop(0, tiles - 1 if last else tiles, body, 0)


def smooth_first_kernel(
    dir_ref, kap_ref, mask_ref, nbr_ref, top_ref, bot_ref,
    out_ref, fn_ref, fw_ref, fe_ref, u0, u1, kbuf,
):
    tiles, height, lanes = u0.shape
    own = dir_ref.shape[0]
    rows = own + 2 * HALO
    edge = (HALO, lanes)
    zero = jnp.zeros(edge, jnp.float32)

    def halos(c):
        cols = pl.ds(pl.multiple_of(c * lanes, lanes), lanes)
        low = row_iota(edge) < HALO // 2
        top = top_ref[:, cols]
        bot = bot_ref[:, cols]
        u0[c, pl.ds(0, HALO), :] = zero
        u1[c, pl.ds(0, HALO), :] = zero
        kbuf[c, pl.ds(0, HALO), :] = zero
        u0[c, pl.ds(HALO, HALO), :] = jnp.where(low, 0.0, pltpu.roll(top, HALO // 2, 0))
        kbuf[c, pl.ds(HALO, HALO), :] = jnp.where(low, 0.0, top)
        u0[c, pl.ds(PAD + own, HALO), :] = jnp.where(low, bot, 0.0)
        kbuf[c, pl.ds(PAD + own, HALO), :] = jnp.where(low, pltpu.roll(bot, HALO // 2, 0), 0.0)
        end = pl.ds(PAD + own + HALO, HALO)
        u0[c, end, :] = zero
        u1[c, end, :] = zero
        kbuf[c, end, :] = zero
        fn_ref[c, end, :] = zero

    def fill(c, carry):
        cols = pl.ds(pl.multiple_of(c * lanes, lanes), lanes)
        maskf = mask_ref[:, cols].astype(jnp.float32)
        u0[c, pl.ds(PAD, own), :] = dir_ref[:, cols] * maskf
        kbuf[c, pl.ds(PAD, own), :] = kap_ref[:, cols] * maskf
        halos(c)
        return carry

    lax.fori_loop(0, tiles - 1, fill, 0)
    u0[tiles - 1, pl.ds(PAD, own), :] = nbr_ref[0]
    kbuf[tiles - 1, pl.ds(PAD, own), :] = nbr_ref[1]
    halos(tiles - 1)

    def faces(c, carry):
        left = lax.rem(c + tiles - 1, tiles)
        right = lax.rem(c + 1, tiles)
        body = pl.ds(HALO, rows)
        k = kbuf[c, body, :]
        fn_ref[c, body, :] = face(k, kbuf[c, pl.ds(HALO - 1, rows), :])
        fw_ref[c, body, :] = face(k, from_left(k, kbuf[left, body, :]))
        fe_ref[c, body, :] = face(k, from_right(k, kbuf[right, body, :]))
        return carry

    lax.fori_loop(0, tiles, faces, 0)

    def finish(c, value):
        out_ref[c] = value.astype(jnp.bfloat16)

    sweeps(tiles, rows, (u0, u1), fn_ref, fw_ref, fe_ref, finish)


def smooth_last_kernel(
    ret_ref, nbr_ref, fn_ref, fw_ref, fe_ref, dir_ref, mask_ref, out_ref, u0, u1
):
    tiles, height, lanes = u0.shape
    own = dir_ref.shape[0]
    rows = own + 2 * HALO
    zero = jnp.zeros((HALO, lanes), jnp.float32)

    def ends(c):
        for buf in (u0, u1):
            buf[c, pl.ds(0, HALO), :] = zero
            buf[c, pl.ds(PAD + own + HALO, HALO), :] = zero

    def fill(c, carry):
        u0[c, pl.ds(HALO, rows), :] = ret_ref[c].astype(jnp.float32)
        ends(c)
        return carry

    lax.fori_loop(0, tiles - 1, fill, 0)
    u0[tiles - 1, pl.ds(HALO, rows), :] = nbr_ref[...].astype(jnp.float32)
    ends(tiles - 1)

    def finish(c, value):
        cols = pl.ds(pl.multiple_of(c * lanes, lanes), lanes)
        maskf = mask_ref[:, cols].astype(jnp.float32)
        out_ref[:, cols] = maskf * (dir_ref[:, cols] * maskf + value)

    sweeps(tiles, rows, (u0, u1), fn_ref, fw_ref, fe_ref, finish)


def segments_kernel(
    info_ref, index_ref, x_ref, table_ref, turned_ref, prec_ref, few_ref, all_ref,
    out_ref, prec, weighted, zbuf, spread, scale_row, adj, prec_sem, scale_sem,
    *, block, blocks, seg_tiles, tile_r,
):
    parts, chunk, lanes = out_ref.shape
    order = prec.shape[0]
    pieces = order // block
    count = info_ref[0]
    full = info_ref[1]

    def prec_copy(i):
        part = pl.ds(i * block, block)
        return pltpu.make_async_copy(prec_ref.at[part, :], prec.at[part, :], prec_sem.at[i])

    for i in range(pieces):
        prec_copy(i).start()
    adj[...] = jnp.zeros_like(adj)

    def group(g, carry):
        ids = []
        for j in range(2):
            e = 2 * g + j
            live = e < count
            e = jnp.minimum(e, count - 1)
            ids.append((info_ref[2 + 3 * e], live))
            few_row = info_ref[3 + 3 * e]
            all_row = info_ref[4 + 3 * e]

            @pl.when(full == 0)
            def _(few_row=few_row, j=j):
                pltpu.make_async_copy(few_ref.at[few_row], scale_row.at[j], scale_sem.at[j]).start()

            @pl.when(full != 0)
            def _(all_row=all_row, j=j):
                pltpu.make_async_copy(all_ref.at[all_row], scale_row.at[j], scale_sem.at[j]).start()

        for j in range(2):
            pltpu.make_async_copy(few_ref.at[0], scale_row.at[j], scale_sem.at[j]).wait()
        second = jnp.where(ids[1][1], 1.0, 0.0)

        def widen(b, carry):
            cols = pl.ds(pl.multiple_of(b * lanes, lanes), lanes)
            a0 = jnp.broadcast_to(scale_row[0, :, cols], (8, lanes))
            a1 = jnp.broadcast_to(scale_row[1, :, cols] * second, (8, lanes))
            turned = jnp.where(row_iota((8, lanes)) == 0, a0, a1).T
            rows = pl.ds(pl.multiple_of(b * lanes, lanes), lanes)
            spread[rows, pl.ds(0, lanes)] = jnp.broadcast_to(turned[:, 0:1], (lanes, lanes))
            spread[rows, pl.ds(lanes, lanes)] = jnp.broadcast_to(turned[:, 1:2], (lanes, lanes))
            return carry

        lax.fori_loop(0, order // lanes, widen, 0)

        def interp(t, carry):
            rows = pl.ds(pl.multiple_of(t * tile_r, tile_r), tile_r)
            w0 = table_ref[index_ref[ids[0][0], t]]
            w1 = table_ref[index_ref[ids[1][0], t]]
            seg = jnp.dot(
                jnp.concatenate([w0, w1], axis=0), x_ref[rows, :],
                preferred_element_type=jnp.float32,
            ).astype(jnp.bfloat16).astype(jnp.float32)
            both = jnp.concatenate([seg[:tile_r], seg[tile_r:]], axis=1)
            weighted[rows, :] = (both * spread[rows, :]).astype(jnp.bfloat16)
            return carry

        lax.fori_loop(0, seg_tiles, interp, 0, unroll=8)

        for i in range(pieces):
            part = pl.ds(i * block, block)

            @pl.when(g == 0)
            def _(i=i):
                prec_copy(i).wait()

            prod = jnp.dot(prec[part, :], weighted[...], preferred_element_type=jnp.float32)
            zbuf[part, :] = (prod * spread[part, :]).astype(jnp.bfloat16)

        def back(t, carry):
            rows = pl.ds(pl.multiple_of(t * tile_r, tile_r), tile_r)
            w0 = turned_ref[index_ref[ids[0][0], t]]
            w1 = turned_ref[index_ref[ids[1][0], t]]
            sums = jnp.dot(w0, zbuf[rows, pl.ds(0, lanes)], preferred_element_type=jnp.float32)
            sums = sums + jnp.dot(
                w1, zbuf[rows, pl.ds(lanes, lanes)], preferred_element_type=jnp.float32
            )
            place = pl.ds(pl.multiple_of(t * tile_r + HALO, HALO), tile_r)
            adj[place, :] = adj[place, :] + sums
            return carry

        lax.fori_loop(0, seg_tiles, back, 0, unroll=8)
        return carry

    lax.fori_loop(0, (count + 1) // 2, group, 0)

    @pl.when(count == 0)
    def _():
        for i in range(pieces):
            prec_copy(i).wait()

    own = chunk - 2 * HALO
    for s in range(parts):
        out_ref[s] = adj[pl.ds(s * own, chunk), :].astype(jnp.bfloat16)


def vmem_spec():
    return pl.BlockSpec(memory_space=pltpu.VMEM)


def any_spec():
    return pl.BlockSpec(memory_space=pl.ANY)


def smem_spec():
    return pl.BlockSpec(memory_space=pltpu.SMEM)


def per_device(
    direction, kappa, land_mask, owned_segments, seg_anchor,
    interp_index, interp_table, precision, obs_scale,
):
    rows_dev, cols_dev = direction.shape
    blocks, tile_r, _ = interp_table.shape
    order = precision.shape[0]
    segs, seg_tiles = interp_index.shape
    seg_max = obs_scale.shape[0]
    lanes = TILE_C
    col_tiles = cols_dev // lanes
    slab_count = lax.axis_size("slab")
    col_count = lax.axis_size("col")
    dev_count = slab_count * col_count
    span = order // rows_dev
    assert span == col_tiles and col_count == 2 and slab_count % span == 0
    groups = [list(range(i, i + span)) for i in range(0, slab_count, span)]
    if len(groups) == 1:
        groups = None
    my_slab = lax.axis_index("slab")
    my_col = lax.axis_index("col")
    my_device = my_slab * col_count + my_col
    is_low = my_col == 0

    def edge_cols(array):
        return jnp.where(is_low, array[:, cols_dev - lanes :], array[:, :lanes])

    edge_mask = edge_cols(land_mask).astype(jnp.float32)
    edge = jnp.stack([edge_cols(direction) * edge_mask, edge_cols(kappa) * edge_mask])
    nbr = lax.ppermute(edge, "col", [(0, 1), (1, 0)])
    near = jnp.where(
        is_low, lane_iota((1, lanes)) < SWEEPS, lane_iota((1, lanes)) >= lanes - SWEEPS
    )
    nbr = jnp.where(near[None], nbr, 0.0)

    def edge_rows(start):
        part = slice(start, start + SWEEPS)
        maskf = land_mask[part].astype(jnp.float32)
        field = jnp.concatenate([direction[part] * maskf, nbr[0, part]], axis=1)
        coeff = jnp.concatenate([kappa[part] * maskf, nbr[1, part]], axis=1)
        return jnp.concatenate([field, coeff], axis=0)

    first_rows, last_rows = edge_rows(0), edge_rows(rows_dev - SWEEPS)
    even = my_slab % 2 == 0
    pairs_a = [(i, i ^ 1) for i in range(slab_count)]
    pairs_b = [(i, i + 1) for i in range(1, slab_count - 1, 2)]
    pairs_b = pairs_b + [(j, i) for i, j in pairs_b]
    got_a = lax.ppermute(jnp.where(even, last_rows, first_rows), "slab", pairs_a)
    got_b = lax.ppermute(jnp.where(even, first_rows, last_rows), "slab", pairs_b)
    top = jnp.where(even, got_b, got_a)
    bot = jnp.where(even, got_a, got_b)

    slots = dev_count * seg_max
    slot_ids = jnp.arange(slots, dtype=jnp.int32)
    used = owned_segments >= 0
    seg_hot = owned_segments[:, None] == jnp.arange(segs, dtype=jnp.int32)[None, :]
    anchor_row = jnp.sum(jnp.where(seg_hot, seg_anchor[None, :, 0], 0), axis=1)
    anchor_col = jnp.sum(jnp.where(seg_hot, seg_anchor[None, :, 1], 0), axis=1)
    owner_slab = anchor_row // seg_tiles * span + anchor_col % col_tiles
    owner = owner_slab * col_count + anchor_col // col_tiles
    owner = jnp.where(used, owner, -1)
    by_dev = owner.reshape(dev_count, seg_max)
    slot_in = jnp.arange(seg_max, dtype=jnp.int32)
    before = slot_in[None, :] < slot_in[:, None]
    same = (by_dev[:, :, None] == by_dev[:, None, :]) & before[None]
    place = jnp.sum(same.astype(jnp.int32), axis=2).reshape(slots)
    overflow = jnp.max(jnp.where(used, place, 0)) >= CAP
    mine = owner == my_device
    rank = jnp.cumsum(mine.astype(jnp.int32)) - 1
    count = jnp.sum(mine.astype(jnp.int32))
    longest = segs
    pick = mine[None, :] & (rank[None, :] == jnp.arange(longest, dtype=jnp.int32)[:, None])
    src_slab = slot_ids // (seg_max * col_count)
    columns = [
        owned_segments,
        src_slab * CAP + jnp.minimum(place, CAP - 1),
        src_slab * seg_max + slot_ids % seg_max,
    ]
    listed = jnp.stack(
        [jnp.sum(jnp.where(pick, col[None, :], 0), axis=1) for col in columns], axis=1
    )
    info = jnp.concatenate(
        [count[None], overflow.astype(jnp.int32)[None], listed.reshape(-1)]
    )

    my_owner = lax.dynamic_slice_in_dim(owner_slab, my_device * seg_max, seg_max)
    my_used = lax.dynamic_slice_in_dim(used, my_device * seg_max, seg_max)
    my_place = lax.dynamic_slice_in_dim(place, my_device * seg_max, seg_max)

    def outbox(cap, position):
        target = jnp.arange(slab_count * cap, dtype=jnp.int32)
        hit = (
            (my_owner * cap + position)[None, :] == target[:, None]
        ) & (my_used & (position < cap))[None, :]
        slot = jnp.sum(jnp.where(hit, slot_in[None, :], 0), axis=1)
        return obs_scale[slot].reshape(slab_count * cap, 1, order)

    def swap(array, groups=None):
        return lax.all_to_all(
            array, "slab", split_axis=0, concat_axis=0, tiled=True, axis_index_groups=groups
        )

    few = swap(outbox(CAP, my_place))
    everything = lax.cond(
        overflow,
        lambda: swap(outbox(seg_max, slot_in)),
        lambda: jnp.zeros((slab_count * seg_max, 1, order), jnp.float32),
    )

    tiles = col_tiles + 1
    height = rows_dev + 2 * PAD
    buf = pltpu.VMEM((tiles, height, lanes), jnp.float32)
    face_shape = jax.ShapeDtypeStruct((tiles, height, lanes), jnp.float32)
    smoothed, fn, fw, fe = pl.pallas_call(
        smooth_first_kernel,
        out_shape=(
            jax.ShapeDtypeStruct((col_tiles, rows_dev, lanes), jnp.bfloat16),
            face_shape, face_shape, face_shape,
        ),
        in_specs=[vmem_spec()] * 6,
        out_specs=(vmem_spec(),) * 4,
        scratch_shapes=[buf, buf, buf],
        cost_estimate=pl.CostEstimate(flops=40000000, bytes_accessed=8 << 20, transcendentals=0),
        name="smooth_first",
    )(direction, kappa, land_mask, nbr, top, bot)

    gathered = swap(smoothed, groups)

    chunk = rows_dev + 2 * HALO
    block = min(512, order)
    returning = pl.pallas_call(
        functools.partial(
            segments_kernel, block=block, blocks=blocks, seg_tiles=seg_tiles, tile_r=tile_r
        ),
        out_shape=jax.ShapeDtypeStruct((span, chunk, lanes), jnp.bfloat16),
        in_specs=[smem_spec(), smem_spec(), vmem_spec(), vmem_spec(), vmem_spec()]
        + [any_spec()] * 3,
        out_specs=vmem_spec(),
        scratch_shapes=[
            pltpu.VMEM((order, order), jnp.bfloat16),
            pltpu.VMEM((order, 2 * lanes), jnp.bfloat16),
            pltpu.VMEM((order, 2 * lanes), jnp.bfloat16),
            pltpu.VMEM((order, 2 * lanes), jnp.float32),
            pltpu.VMEM((2, 1, order), jnp.float32),
            pltpu.VMEM((order + 2 * HALO, lanes), jnp.float32),
            pltpu.SemaphoreType.DMA((order // block,)),
            pltpu.SemaphoreType.DMA((2,)),
        ],
        cost_estimate=pl.CostEstimate(
            flops=8 * 2 * order * order * lanes, bytes_accessed=12 << 20, transcendentals=0
        ),
        name="segments",
    )(
        info, interp_index, gathered.reshape(order, lanes), interp_table,
        interp_table.transpose(0, 2, 1), precision, few, everything,
    )

    returned = swap(returning, groups)

    if groups is not None:
        returned = lane_edges(returned, slab_count, span, my_slab, rows_dev)

    border = jnp.where(is_low, returned[col_tiles - 1], returned[0])
    border = lax.ppermute(border, "col", [(0, 1), (1, 0)])
    return pl.pallas_call(
        smooth_last_kernel,
        out_shape=jax.ShapeDtypeStruct((rows_dev, cols_dev), jnp.float32),
        in_specs=[vmem_spec()] * 7,
        out_specs=vmem_spec(),
        scratch_shapes=[buf, buf],
        cost_estimate=pl.CostEstimate(flops=40000000, bytes_accessed=8 << 20, transcendentals=0),
        name="smooth_last",
    )(returned, border, fn, fw, fe, direction, land_mask)


def lane_edges(returned, slab_count, span, my_slab, rows_dev):
    up = [(i, i + 1) for i in range(span - 1, slab_count - 1, span)]
    down = [(j, i) for i, j in up]
    own_last = returned[:, rows_dev : rows_dev + HALO]
    own_first = returned[:, HALO : 2 * HALO]
    above = lax.ppermute(own_last, "slab", up)
    below = lax.ppermute(own_first, "slab", down)
    first = (my_slab % span == 0)
    last = (my_slab % span == span - 1)
    head = jnp.where(first, above, returned[:, :HALO])
    tail = jnp.where(last, below, returned[:, rows_dev + HALO :])
    return jnp.concatenate([head, returned[:, HALO : rows_dev + HALO], tail], axis=1)


def solution(mesh):
    in_specs = (
        P("slab", "col"),
        P("slab", "col"),
        P("slab", "col"),
        P(),
        P(),
        P(),
        P(),
        P(),
        P(("slab", "col"), None),
    )
    return jax.shard_map(
        per_device, mesh=mesh, in_specs=in_specs, out_specs=P("slab", "col"), check_vma=False
    )
```

```python
import functools

import jax
import jax.numpy as jnp
from jax import lax
from jax.experimental import pallas as pl
from jax.experimental.pallas import tpu as pltpu
from jax.sharding import PartitionSpec as P

TILE_C = 128
SWEEPS = 4
HALO = 8
PAD = 16
CAP = 3


def lane_iota(shape):
    return lax.broadcasted_iota(jnp.int32, shape, len(shape) - 1)


def row_iota(shape):
    return lax.broadcasted_iota(jnp.int32, shape, len(shape) - 2)


def from_left(own, left):
    lanes = own.shape[-1]
    return pltpu.roll(jnp.where(lane_iota(own.shape) == lanes - 1, left, own), 1, 1)


def from_right(own, right):
    lanes = own.shape[-1]
    return pltpu.roll(jnp.where(lane_iota(own.shape) == 0, right, own), lanes - 1, 1)


def face(own, other):
    return jnp.where((own > 0) & (other > 0), 0.5 * (own + other), 0.0)


def sweeps(tiles, rows, bufs, own_ref, fn_ref, fw_ref, fe_ref, finish):
    for step in range(SWEEPS):
        src, dst = bufs[step % 2], bufs[1 - step % 2]
        last = step == SWEEPS - 1
        first_row = PAD if last else HALO
        length = (rows - 2 * (PAD - HALO) if last else rows) // 2

        for half in range(2):
            start = first_row + half * length
            body = pl.ds(start, length)

            def tile(c, right, u_left, u, src=src, dst=dst, last=last, start=start, body=body):
                u_right = src[right, body, :]
                up = src[c, pl.ds(start - 1, length), :]
                down = src[c, pl.ds(start + 1, length), :]
                out = own_ref[c, body, :] * u + fn_ref[c, body, :] * up
                out = out + fn_ref[c, pl.ds(start + 1, length), :] * down
                out = out + fw_ref[c, body, :] * from_left(u, u_left)
                out = out + fe_ref[c, body, :] * from_right(u, u_right)
                if last:
                    finish(c, start - PAD, out)
                else:
                    dst[c, body, :] = out
                return u, u_right

            def step_tile(c, carry):
                return tile(c, c + 1, *carry)

            carry = src[tiles - 1, body, :], src[0, body, :]
            carry = lax.fori_loop(0, tiles - 1, step_tile, carry, unroll=4)
            if not last:
                tile(tiles - 1, 0, *carry)


def smooth_first_kernel(
    dir_ref, kap_ref, mask_ref, nbr_ref, top_ref, bot_ref,
    out_ref, own_ref, fn_ref, fw_ref, fe_ref, u0, u1, kbuf,
):
    tiles, height, lanes = u0.shape
    own = dir_ref.shape[0]
    rows = own + 2 * HALO
    edge = (HALO, lanes)
    zero = jnp.zeros(edge, jnp.float32)

    def halos(c):
        cols = pl.ds(pl.multiple_of(c * lanes, lanes), lanes)
        low = row_iota(edge) < HALO // 2
        top = top_ref[:, cols]
        bot = bot_ref[:, cols]
        u0[c, pl.ds(0, HALO), :] = zero
        u1[c, pl.ds(0, HALO), :] = zero
        kbuf[c, pl.ds(0, HALO), :] = zero
        u0[c, pl.ds(HALO, HALO), :] = jnp.where(low, 0.0, pltpu.roll(top, HALO // 2, 0))
        kbuf[c, pl.ds(HALO, HALO), :] = jnp.where(low, 0.0, top)
        u0[c, pl.ds(PAD + own, HALO), :] = jnp.where(low, bot, 0.0)
        kbuf[c, pl.ds(PAD + own, HALO), :] = jnp.where(low, pltpu.roll(bot, HALO // 2, 0), 0.0)
        end = pl.ds(PAD + own + HALO, HALO)
        u0[c, end, :] = zero
        u1[c, end, :] = zero
        kbuf[c, end, :] = zero
        fn_ref[c, end, :] = zero

    def fill(c, carry):
        cols = pl.ds(pl.multiple_of(c * lanes, lanes), lanes)
        maskf = mask_ref[:, cols].astype(jnp.float32)
        u0[c, pl.ds(PAD, own), :] = dir_ref[:, cols] * maskf
        kbuf[c, pl.ds(PAD, own), :] = kap_ref[:, cols] * maskf
        halos(c)
        return carry

    lax.fori_loop(0, tiles - 1, fill, 0)
    u0[tiles - 1, pl.ds(PAD, own), :] = nbr_ref[0]
    kbuf[tiles - 1, pl.ds(PAD, own), :] = nbr_ref[1]
    halos(tiles - 1)

    def faces(c, right, k_left, k):
        body = pl.ds(HALO, rows)
        k_right = kbuf[right, body, :]
        north = face(k, kbuf[c, pl.ds(HALO - 1, rows), :])
        south = face(k, kbuf[c, pl.ds(HALO + 1, rows), :])
        west = face(k, from_left(k, k_left))
        east = face(k, from_right(k, k_right))
        fn_ref[c, body, :] = north
        fw_ref[c, body, :] = west
        fe_ref[c, body, :] = east
        own_ref[c, body, :] = 1.0 - ((north + south) + (west + east))
        return k, k_right

    body = pl.ds(HALO, rows)
    carry = kbuf[tiles - 1, body, :], kbuf[0, body, :]
    carry = lax.fori_loop(0, tiles - 1, lambda c, carry: faces(c, c + 1, *carry), carry)
    faces(tiles - 1, 0, *carry)

    def finish(c, row, value):
        out_ref[c, pl.ds(row, value.shape[0]), :] = value.astype(jnp.bfloat16)

    sweeps(tiles, rows, (u0, u1), own_ref, fn_ref, fw_ref, fe_ref, finish)


def smooth_last_kernel(
    ret_ref, nbr_ref, own_ref, fn_ref, fw_ref, fe_ref, dir_ref, mask_ref, out_ref, u0, u1
):
    tiles, height, lanes = u0.shape
    own = dir_ref.shape[0]
    rows = own + 2 * HALO
    zero = jnp.zeros((HALO, lanes), jnp.float32)

    def ends(c):
        for buf in (u0, u1):
            buf[c, pl.ds(0, HALO), :] = zero
            buf[c, pl.ds(PAD + own + HALO, HALO), :] = zero

    def fill(c, carry):
        u0[c, pl.ds(HALO, rows), :] = ret_ref[c].astype(jnp.float32)
        ends(c)
        return carry

    lax.fori_loop(0, tiles - 1, fill, 0)
    u0[tiles - 1, pl.ds(HALO, rows), :] = nbr_ref[...].astype(jnp.float32)
    ends(tiles - 1)

    def finish(c, row, value):
        cols = pl.ds(pl.multiple_of(c * lanes, lanes), lanes)
        part = pl.ds(row, value.shape[0])
        maskf = mask_ref[part, cols].astype(jnp.float32)
        out_ref[part, cols] = maskf * (dir_ref[part, cols] * maskf + value)

    sweeps(tiles, rows, (u0, u1), own_ref, fn_ref, fw_ref, fe_ref, finish)


def outbox_kernel(owned_ref, anchor_ref, scale_ref, out_ref, *, seg_tiles, col_tiles, span):
    seg_max = scale_ref.shape[0]
    me = lax.axis_index("slab") * lax.axis_size("col") + lax.axis_index("col")
    owners = []
    for i in range(seg_max):
        seg = owned_ref[me * seg_max + i]
        safe = jnp.maximum(seg, 0)
        lane = anchor_ref[2 * safe] // seg_tiles
        owner = lane * span + lax.rem(anchor_ref[2 * safe + 1], col_tiles)
        owner = jnp.where(seg >= 0, owner, -1)
        place = jnp.int32(0)
        for other in owners:
            place = place + jnp.where(other == owner, 1, 0)
        owners.append(owner)

        @pl.when((seg >= 0) & (place < CAP))
        def _(i=i, owner=owner, place=place):
            out_ref[owner * CAP + place] = scale_ref[i : i + 1, :]


def segments_kernel(
    info_ref, index_ref, x_ref, ahead_ref, behind_ref, prec_ref, few_ref, all_ref,
    out_ref, turned, weighted, zbuf, scale_row, adj, grid, scale_sem, *, width, batch,
):
    parts, chunk, lanes = out_ref.shape
    order = prec_ref.shape[0]
    blocks = order // lanes
    count = info_ref[0]
    full = info_ref[1]
    groups = (count + batch - 1) // batch

    def scale_copy(source, row, slot, j):
        return pltpu.make_async_copy(source.at[row], scale_row.at[slot, j], scale_sem.at[slot, j])

    def fetch(g, slot):
        for j in range(batch):
            e = g * batch + j

            @pl.when((e < count) & (full == 0))
            def _(e=e, j=j):
                scale_copy(few_ref, info_ref[3 + 3 * e], slot, j).start()

            @pl.when((e < count) & (full != 0))
            def _(e=e, j=j):
                scale_copy(all_ref, info_ref[4 + 3 * e], slot, j).start()

    fetch(0, 0)

    def turn(q, carry):
        part = pl.ds(pl.multiple_of(q * lanes, lanes), lanes)
        turned[:, part] = x_ref[part, :].astype(jnp.float32).T.astype(jnp.bfloat16)
        adj[:, part] = jnp.zeros((lanes, lanes), jnp.float32)
        return carry

    lax.fori_loop(0, blocks, turn, 0, unroll=4)

    def work(g, size):
        slot = lax.rem(g, 2)
        ids = [info_ref[2 + 3 * (g * batch + j)] for j in range(size)]
        for j in range(size):
            scale_copy(few_ref, 0, slot, j).wait()
        fetch(g + 1, 1 - slot)

        def pair_of(table, q):
            sides = []
            for j in range(size):
                low = table[0, index_ref[ids[j], 2 * q]]
                high = table[1, index_ref[ids[j], 2 * q + 1]]
                sides.append(jnp.concatenate([low, high], axis=0))
            return sides

        def interp(q, carry):
            part = pl.ds(pl.multiple_of(q * lanes, lanes), lanes)
            right = jnp.concatenate(pair_of(ahead_ref, q), axis=1)
            seg = jnp.dot(turned[:, part], right, preferred_element_type=jnp.float32)
            seg = seg.astype(jnp.bfloat16).astype(jnp.float32)
            for j in range(size):
                value = seg[:, j * lanes : (j + 1) * lanes] * scale_row[slot, j, :, part]
                weighted[j * lanes : (j + 1) * lanes, part] = value.astype(jnp.bfloat16)
            return carry

        lax.fori_loop(0, blocks, interp, 0, unroll=4)

        for i in range(order // width):
            cols = pl.ds(i * width, width)
            prod = jnp.dot(
                weighted[: size * lanes, :], prec_ref[:, cols],
                preferred_element_type=jnp.float32,
            )
            for j in range(size):
                rows = slice(j * lanes, (j + 1) * lanes)
                zbuf[rows, cols] = (prod[rows] * scale_row[slot, j, :, cols]).astype(jnp.bfloat16)

        def back(q, carry):
            part = pl.ds(pl.multiple_of(q * lanes, lanes), lanes)
            left = jnp.concatenate(
                [zbuf[j * lanes : (j + 1) * lanes, part] for j in range(size)], axis=1
            )
            right = jnp.concatenate(pair_of(behind_ref, q), axis=0)
            adj[:, part] = adj[:, part] + jnp.dot(left, right, preferred_element_type=jnp.float32)
            return carry

        lax.fori_loop(0, blocks, back, 0, unroll=4)

    def whole_group(g, carry):
        work(g, batch)
        return carry

    lax.fori_loop(0, count // batch, whole_group, 0)
    for size in range(1, batch):

        @pl.when(lax.rem(count, batch) == size)
        def _(size=size):
            work(count // batch, size)

    zero = jnp.zeros((HALO, lanes), jnp.float32)
    grid[pl.ds(0, HALO), :] = zero
    grid[pl.ds(order + HALO, HALO), :] = zero

    def unturn(q, carry):
        part = pl.ds(pl.multiple_of(q * lanes, lanes), lanes)
        grid[pl.ds(pl.multiple_of(q * lanes + HALO, HALO), lanes), :] = adj[:, part].T
        return carry

    lax.fori_loop(0, blocks, unturn, 0, unroll=4)
    own = chunk - 2 * HALO
    for s in range(parts):
        out_ref[s] = grid[pl.ds(s * own, chunk), :].astype(jnp.bfloat16)


def vmem_need(rows):
    return min(2 * rows * TILE_C * 4, 60 << 20)


def vmem_spec():
    return pl.BlockSpec(memory_space=pltpu.VMEM)


def any_spec():
    return pl.BlockSpec(memory_space=pl.ANY)


def smem_spec():
    return pl.BlockSpec(memory_space=pltpu.SMEM)


def per_device(
    direction, kappa, land_mask, owned_segments, seg_anchor,
    interp_index, interp_table, precision, obs_scale,
):
    rows_dev, cols_dev = direction.shape
    blocks, tile_r, _ = interp_table.shape
    order = precision.shape[0]
    segs, seg_tiles = interp_index.shape
    seg_max = obs_scale.shape[0]
    lanes = TILE_C
    col_tiles = cols_dev // lanes
    slab_count = lax.axis_size("slab")
    col_count = lax.axis_size("col")
    dev_count = slab_count * col_count
    span = order // rows_dev
    assert span == col_tiles and col_count == 2 and slab_count % span == 0
    groups = [list(range(i, i + span)) for i in range(0, slab_count, span)]
    if len(groups) == 1:
        groups = None
    my_slab = lax.axis_index("slab")
    my_col = lax.axis_index("col")
    my_device = my_slab * col_count + my_col
    is_low = my_col == 0

    def edge_cols(array):
        return jnp.where(is_low, array[:, cols_dev - lanes :], array[:, :lanes])

    edge_mask = edge_cols(land_mask).astype(jnp.float32)
    edge = jnp.stack([edge_cols(direction) * edge_mask, edge_cols(kappa) * edge_mask])
    nbr = lax.ppermute(edge, "col", [(0, 1), (1, 0)])
    near = jnp.where(
        is_low, lane_iota((1, lanes)) < SWEEPS, lane_iota((1, lanes)) >= lanes - SWEEPS
    )
    nbr = jnp.where(near[None], nbr, 0.0)

    def edge_rows(start):
        part = slice(start, start + SWEEPS)
        maskf = land_mask[part].astype(jnp.float32)
        field = jnp.concatenate([direction[part] * maskf, nbr[0, part]], axis=1)
        coeff = jnp.concatenate([kappa[part] * maskf, nbr[1, part]], axis=1)
        return jnp.concatenate([field, coeff], axis=0)

    first_rows, last_rows = edge_rows(0), edge_rows(rows_dev - SWEEPS)
    even = my_slab % 2 == 0
    pairs_a = [(i, i ^ 1) for i in range(slab_count)]
    pairs_b = [(i, i + 1) for i in range(1, slab_count - 1, 2)]
    pairs_b = pairs_b + [(j, i) for i, j in pairs_b]
    send_a = jnp.where(even, last_rows, first_rows)
    send_b = jnp.where(even, first_rows, last_rows)
    got_a = lax.ppermute(send_a, "slab", pairs_a)
    got_b = lax.ppermute(send_b, "slab", pairs_b)
    owned_segments, seg_anchor, send_a = lax.optimization_barrier(
        (owned_segments, seg_anchor, send_a)
    )
    top = jnp.where(even, got_b, got_a)
    bot = jnp.where(even, got_a, got_b)

    slots = dev_count * seg_max
    slot_ids = jnp.arange(slots, dtype=jnp.int32)
    used = owned_segments >= 0
    seg_hot = owned_segments[:, None] == jnp.arange(segs, dtype=jnp.int32)[None, :]
    anchor_row = jnp.sum(jnp.where(seg_hot, seg_anchor[None, :, 0], 0), axis=1)
    anchor_col = jnp.sum(jnp.where(seg_hot, seg_anchor[None, :, 1], 0), axis=1)
    owner_slab = anchor_row // seg_tiles * span + anchor_col % col_tiles
    owner = owner_slab * col_count + anchor_col // col_tiles
    owner = jnp.where(used, owner, -1)
    by_dev = owner.reshape(dev_count, seg_max)
    slot_in = jnp.arange(seg_max, dtype=jnp.int32)
    before = slot_in[None, :] < slot_in[:, None]
    same = (by_dev[:, :, None] == by_dev[:, None, :]) & before[None]
    place = jnp.sum(same.astype(jnp.int32), axis=2).reshape(slots)
    overflow = jnp.max(jnp.where(used, place, 0)) >= CAP
    mine = owner == my_device
    rank = jnp.cumsum(mine.astype(jnp.int32)) - 1
    count = jnp.sum(mine.astype(jnp.int32))
    longest = segs
    pick = mine[None, :] & (rank[None, :] == jnp.arange(longest, dtype=jnp.int32)[:, None])
    src_slab = slot_ids // (seg_max * col_count)
    columns = [
        owned_segments,
        src_slab * CAP + jnp.minimum(place, CAP - 1),
        src_slab * seg_max + slot_ids % seg_max,
    ]
    listed = jnp.stack(
        [jnp.sum(jnp.where(pick, col[None, :], 0), axis=1) for col in columns], axis=1
    )
    info = jnp.concatenate(
        [count[None], overflow.astype(jnp.int32)[None], listed.reshape(-1)]
    )

    my_owner = lax.dynamic_slice_in_dim(owner_slab, my_device * seg_max, seg_max)
    my_used = lax.dynamic_slice_in_dim(used, my_device * seg_max, seg_max)

    def outbox(cap, position):
        target = jnp.arange(slab_count * cap, dtype=jnp.int32)
        hit = (
            (my_owner * cap + position)[None, :] == target[:, None]
        ) & (my_used & (position < cap))[None, :]
        slot = jnp.sum(jnp.where(hit, slot_in[None, :], 0), axis=1)
        return obs_scale[slot].reshape(slab_count * cap, 1, order)

    def swap(array, groups=None):
        return lax.all_to_all(
            array, "slab", split_axis=0, concat_axis=0, tiled=True, axis_index_groups=groups
        )

    few = swap(
        pl.pallas_call(
            functools.partial(outbox_kernel, seg_tiles=seg_tiles, col_tiles=col_tiles, span=span),
            out_shape=jax.ShapeDtypeStruct((slab_count * CAP, 1, order), jnp.float32),
            in_specs=[smem_spec(), smem_spec(), vmem_spec()],
            out_specs=vmem_spec(),
            compiler_params=pltpu.CompilerParams(vmem_limit_bytes=2 << 20),
            name="outbox",
        )(owned_segments, seg_anchor.reshape(-1), obs_scale)
    )
    everything = lax.cond(
        overflow,
        lambda: swap(outbox(seg_max, slot_in)),
        lambda: jnp.zeros((slab_count * seg_max, 1, order), jnp.float32),
    )

    tiles = col_tiles + 1
    height = rows_dev + 2 * PAD
    buf = pltpu.VMEM((tiles, height, lanes), jnp.float32)
    face_shape = jax.ShapeDtypeStruct((tiles, height, lanes), jnp.float32)
    smoothed, own, fn, fw, fe = pl.pallas_call(
        smooth_first_kernel,
        out_shape=(
            jax.ShapeDtypeStruct((col_tiles, rows_dev, lanes), jnp.bfloat16),
            face_shape, face_shape, face_shape, face_shape,
        ),
        in_specs=[vmem_spec()] * 6,
        out_specs=(vmem_spec(),) * 5,
        scratch_shapes=[buf, buf, buf],
        compiler_params=pltpu.CompilerParams(vmem_limit_bytes=vmem_need(8 * tiles * height)),
        cost_estimate=pl.CostEstimate(flops=40000000, bytes_accessed=8 << 20, transcendentals=0),
        name="smooth_first",
    )(direction, kappa, land_mask, nbr, top, bot)

    gathered = swap(smoothed, groups)

    chunk = rows_dev + 2 * HALO
    width = min(512, order)
    batch = 4

    def sides(table):
        empty = jnp.zeros_like(table)
        return jnp.stack(
            [jnp.concatenate([table, empty], axis=2), jnp.concatenate([empty, table], axis=2)]
        )

    returning = pl.pallas_call(
        functools.partial(segments_kernel, width=width, batch=batch),
        out_shape=jax.ShapeDtypeStruct((span, chunk, lanes), jnp.bfloat16),
        in_specs=[smem_spec(), smem_spec(), vmem_spec(), vmem_spec(), vmem_spec(), vmem_spec()]
        + [any_spec()] * 2,
        out_specs=vmem_spec(),
        scratch_shapes=[
            pltpu.VMEM((lanes, order), jnp.bfloat16),
            pltpu.VMEM((batch * lanes, order), jnp.bfloat16),
            pltpu.VMEM((batch * lanes, order), jnp.bfloat16),
            pltpu.VMEM((2, batch, 1, order), jnp.float32),
            pltpu.VMEM((lanes, order), jnp.float32),
            pltpu.VMEM((order + 2 * HALO, lanes), jnp.float32),
            pltpu.SemaphoreType.DMA((2, batch)),
        ],
        compiler_params=pltpu.CompilerParams(vmem_limit_bytes=vmem_need(order * order // 256)),
        cost_estimate=pl.CostEstimate(
            flops=8 * 2 * order * order * lanes, bytes_accessed=12 << 20, transcendentals=0
        ),
        name="segments",
    )(
        info, interp_index, gathered.reshape(order, lanes),
        sides(interp_table.transpose(0, 2, 1)), sides(interp_table), precision, few, everything,
    )

    returned = swap(returning, groups)

    if groups is not None:
        returned = lane_edges(returned, slab_count, span, my_slab, rows_dev)

    border = jnp.where(is_low, returned[col_tiles - 1], returned[0])
    border = lax.ppermute(border, "col", [(0, 1), (1, 0)])
    return pl.pallas_call(
        smooth_last_kernel,
        out_shape=jax.ShapeDtypeStruct((rows_dev, cols_dev), jnp.float32),
        in_specs=[vmem_spec()] * 8,
        out_specs=vmem_spec(),
        scratch_shapes=[buf, buf],
        compiler_params=pltpu.CompilerParams(vmem_limit_bytes=vmem_need(8 * tiles * height)),
        cost_estimate=pl.CostEstimate(flops=40000000, bytes_accessed=8 << 20, transcendentals=0),
        name="smooth_last",
    )(returned, border, own, fn, fw, fe, direction, land_mask)


def lane_edges(returned, slab_count, span, my_slab, rows_dev):
    up = [(i, i + 1) for i in range(span - 1, slab_count - 1, span)]
    down = [(j, i) for i, j in up]
    own_last = returned[:, rows_dev : rows_dev + HALO]
    own_first = returned[:, HALO : 2 * HALO]
    above = lax.ppermute(own_last, "slab", up)
    below = lax.ppermute(own_first, "slab", down)
    first = (my_slab % span == 0)
    last = (my_slab % span == span - 1)
    head = jnp.where(first, above, returned[:, :HALO])
    tail = jnp.where(last, below, returned[:, rows_dev + HALO :])
    return jnp.concatenate([head, returned[:, HALO : rows_dev + HALO], tail], axis=1)


def solution(mesh):
    in_specs = (
        P("slab", "col"),
        P("slab", "col"),
        P("slab", "col"),
        P(),
        P(),
        P(),
        P(),
        P(),
        P(("slab", "col"), None),
    )
    return jax.shard_map(
        per_device, mesh=mesh, in_specs=in_specs, out_specs=P("slab", "col"), check_vma=False
    )
```

```python
import functools

import jax
import jax.numpy as jnp
from jax import lax
from jax.experimental import pallas as pl
from jax.experimental.pallas import tpu as pltpu
from jax.sharding import PartitionSpec as P


TILE_C = 128
SWEEPS = 4
HALO = 8
PAD = 16
CAP = 3


def lane_iota(shape):
    return lax.broadcasted_iota(jnp.int32, shape, len(shape) - 1)


def row_iota(shape):
    return lax.broadcasted_iota(jnp.int32, shape, len(shape) - 2)


def from_left(own, left):
    lanes = own.shape[-1]
    return pltpu.roll(jnp.where(lane_iota(own.shape) == lanes - 1, left, own), 1, 1)


def from_right(own, right):
    lanes = own.shape[-1]
    return pltpu.roll(jnp.where(lane_iota(own.shape) == 0, right, own), lanes - 1, 1)


def face(own, other):
    return jnp.where((own > 0) & (other > 0), 0.5 * (own + other), 0.0)


def sweeps(tiles, rows, bufs, own_ref, fn_ref, fw_ref, fe_ref, finish, half_done=None):
    for step in range(SWEEPS):
        src, dst = bufs[step % 2], bufs[1 - step % 2]
        last = step == SWEEPS - 1
        first_row = PAD if last else HALO
        length = (rows - 2 * (PAD - HALO) if last else rows) // 2

        for half in range(2):
            start = first_row + half * length
            body = pl.ds(start, length)

            def tile(c, right, u_left, u, src=src, dst=dst, last=last, start=start, body=body):
                u_right = src[right, body, :]
                up = src[c, pl.ds(start - 1, length), :]
                down = src[c, pl.ds(start + 1, length), :]
                out = own_ref[c, body, :] * u + fn_ref[c, body, :] * up
                out = out + fn_ref[c, pl.ds(start + 1, length), :] * down
                out = out + fw_ref[c, body, :] * from_left(u, u_left)
                out = out + fe_ref[c, body, :] * from_right(u, u_right)
                if last:
                    finish(c, start - PAD, out)
                else:
                    dst[c, body, :] = out
                return u, u_right

            def step_tile(c, carry):
                return tile(c, c + 1, *carry)

            carry = src[tiles - 1, body, :], src[0, body, :]
            carry = lax.fori_loop(0, tiles - 1, step_tile, carry, unroll=4)
            if not last:
                tile(tiles - 1, 0, *carry)
            elif half_done is not None:
                half_done(start - PAD, length)


def smooth_first_kernel(
    dir_ref, kap_ref, mask_ref, nbr_ref, got_a_ref, got_b_ref,
    out_ref, own_out, fn_out, fw_out, fe_out,
    done, own_ref, fn_ref, fw_ref, fe_ref, u0, u1, kbuf, sems,
):
    tiles, _, lanes = u0.shape
    own = dir_ref.shape[0]
    rows = own + 2 * HALO
    edge = (HALO, lanes)
    zero = jnp.zeros(edge, jnp.float32)
    even = lax.rem(lax.axis_index("slab"), 2) == 0
    low = row_iota(edge) < HALO // 2

    def ends(c):
        for part in (pl.ds(0, HALO), pl.ds(PAD + own + HALO, HALO)):
            u0[c, part, :] = zero
            u1[c, part, :] = zero
            kbuf[c, part, :] = zero
        fn_ref[c, pl.ds(PAD + own + HALO, HALO), :] = zero

    def fill(c, carry):
        cols = pl.ds(pl.multiple_of(c * lanes, lanes), lanes)
        maskf = mask_ref[:, cols].astype(jnp.float32)
        u0[c, pl.ds(PAD, own), :] = dir_ref[:, cols] * maskf
        kbuf[c, pl.ds(PAD, own), :] = kap_ref[:, cols] * maskf
        got_a, got_b = got_a_ref[:, cols], got_b_ref[:, cols]
        top = jnp.where(even, got_b, got_a)
        bot = jnp.where(even, got_a, got_b)
        u0[c, pl.ds(HALO, HALO), :] = jnp.where(low, 0.0, pltpu.roll(top, HALO // 2, 0))
        kbuf[c, pl.ds(HALO, HALO), :] = jnp.where(low, 0.0, top)
        u0[c, pl.ds(PAD + own, HALO), :] = jnp.where(low, bot, 0.0)
        kbuf[c, pl.ds(PAD + own, HALO), :] = jnp.where(low, pltpu.roll(bot, HALO // 2, 0), 0.0)
        ends(c)
        return carry

    lax.fori_loop(0, tiles - 1, fill, 0)
    body = pl.ds(HALO, rows)
    lane = lane_iota((rows, lanes))
    near = jnp.where(lax.axis_index("col") == 0, lanes - 1 - lane, lane) >= lanes - SWEEPS
    u0[tiles - 1, body, :] = nbr_ref[0]
    kbuf[tiles - 1, body, :] = jnp.where(near, nbr_ref[1], 0.0)
    ends(tiles - 1)

    def faces(c, right, k_left, k):
        body = pl.ds(HALO, rows)
        k_right = kbuf[right, body, :]
        north = face(k, kbuf[c, pl.ds(HALO - 1, rows), :])
        south = face(k, kbuf[c, pl.ds(HALO + 1, rows), :])
        west = face(k, from_left(k, k_left))
        east = face(k, from_right(k, k_right))
        fn_ref[c, body, :] = north
        fw_ref[c, body, :] = west
        fe_ref[c, body, :] = east
        own_ref[c, body, :] = 1.0 - ((north + south) + (west + east))
        return k, k_right

    body = pl.ds(HALO, rows)
    carry = kbuf[tiles - 1, body, :], kbuf[0, body, :]
    carry = lax.fori_loop(0, tiles - 1, lambda c, carry: faces(c, c + 1, *carry), carry)
    faces(tiles - 1, 0, *carry)
    copies = [
        pltpu.make_async_copy(ref, out, sems.at[i])
        for i, (ref, out) in enumerate(
            ((own_ref, own_out), (fn_ref, fn_out), (fw_ref, fw_out), (fe_ref, fe_out))
        )
    ]
    for copy in copies:
        copy.start()

    def finish(c, row, value):
        done[c, pl.ds(row, value.shape[0]), :] = value.astype(jnp.bfloat16)

    def half_done(row, length):
        part = pl.ds(row, length)
        copy = pltpu.make_async_copy(
            done.at[:, part, :], out_ref.at[:, part, :], sems.at[len(copies)]
        )
        copies.append(copy)
        copy.start()

    sweeps(tiles, rows, (u0, u1), own_ref, fn_ref, fw_ref, fe_ref, finish, half_done)
    for copy in copies:
        copy.wait()


def smooth_last_kernel(
    ret_ref, nbr_ref, own_ref, fn_ref, fw_ref, fe_ref, dir_ref, mask_ref, out_ref, u0, u1
):
    tiles, _, lanes = u0.shape
    own = dir_ref.shape[0]
    rows = own + 2 * HALO
    zero = jnp.zeros((HALO, lanes), jnp.float32)

    def ends(c):
        for buf in (u0, u1):
            buf[c, pl.ds(0, HALO), :] = zero
            buf[c, pl.ds(PAD + own + HALO, HALO), :] = zero

    def fill(c, carry):
        u0[c, pl.ds(HALO, rows), :] = ret_ref[c].astype(jnp.float32)
        ends(c)
        return carry

    lax.fori_loop(0, tiles - 1, fill, 0)
    u0[tiles - 1, pl.ds(HALO, rows), :] = nbr_ref[...].astype(jnp.float32)
    ends(tiles - 1)

    def finish(c, row, value):
        cols = pl.ds(pl.multiple_of(c * lanes, lanes), lanes)
        part = pl.ds(row, value.shape[0])
        maskf = mask_ref[part, cols].astype(jnp.float32)
        out_ref[part, cols] = maskf * (dir_ref[part, cols] * maskf + value)

    sweeps(tiles, rows, (u0, u1), own_ref, fn_ref, fw_ref, fe_ref, finish)


def outbox_kernel(owned_ref, anchor_ref, scale_ref, out_ref, *, seg_tiles, col_tiles, span):
    seg_max = scale_ref.shape[0]
    me = lax.axis_index("slab") * lax.axis_size("col") + lax.axis_index("col")
    owners = []
    for i in range(seg_max):
        seg = owned_ref[me * seg_max + i]
        safe = jnp.maximum(seg, 0)
        lane = anchor_ref[2 * safe] // seg_tiles
        owner = lane * span + lax.rem(anchor_ref[2 * safe + 1], col_tiles)
        owner = jnp.where(seg >= 0, owner, -1)
        place = jnp.int32(0)
        for other in owners:
            place = place + jnp.where(other == owner, 1, 0)
        owners.append(owner)

        @pl.when((seg >= 0) & (place < CAP))
        def _(i=i, owner=owner, place=place):
            out_ref[owner * CAP + place] = scale_ref[i : i + 1, :]


def segments_kernel(
    info_ref, index_ref, x_ref, ahead_ref, behind_ref, prec_in, few_ref, all_ref,
    out_ref, prec_ref, turned, weighted, zbuf, scale_row, adj, grid, prec_sem, scale_sem,
    *, width, batch,
):
    parts, chunk, lanes = out_ref.shape
    order = prec_ref.shape[0]
    blocks = order // lanes
    count = info_ref[0]
    full = info_ref[1]

    def scale_copy(source, row, slot, j):
        return pltpu.make_async_copy(source.at[row], scale_row.at[slot, j], scale_sem.at[slot, j])

    def fetch(g, slot):
        for j in range(batch):
            e = g * batch + j

            @pl.when((e < count) & (full == 0))
            def _(e=e, j=j):
                scale_copy(few_ref, info_ref[3 + 3 * e], slot, j).start()

            @pl.when((e < count) & (full != 0))
            def _(e=e, j=j):
                scale_copy(all_ref, info_ref[4 + 3 * e], slot, j).start()

    def prec_copy(i):
        cols = pl.ds(i * width, width)
        return pltpu.make_async_copy(prec_in.at[:, cols], prec_ref.at[:, cols], prec_sem.at[i])

    fetch(0, 0)
    for i in range(order // width):
        prec_copy(i).start()

    def turn(q, carry):
        part = pl.ds(pl.multiple_of(q * lanes, lanes), lanes)
        turned[:, part] = x_ref[part, :].astype(jnp.float32).T.astype(jnp.bfloat16)
        adj[:, part] = jnp.zeros((lanes, lanes), jnp.float32)
        return carry

    lax.fori_loop(0, blocks, turn, 0, unroll=4)

    def work(g, size):
        slot = lax.rem(g, 2)
        ids = [info_ref[2 + 3 * (g * batch + j)] for j in range(size)]
        for j in range(size):
            scale_copy(few_ref, 0, slot, j).wait()
        fetch(g + 1, 1 - slot)

        def pair_of(table, q):
            sides = []
            for j in range(size):
                low = table[0, index_ref[ids[j], 2 * q]]
                high = table[1, index_ref[ids[j], 2 * q + 1]]
                sides.append(jnp.concatenate([low, high], axis=0))
            return sides

        def interp(q, carry):
            part = pl.ds(pl.multiple_of(q * lanes, lanes), lanes)
            right = jnp.concatenate(pair_of(ahead_ref, q), axis=1)
            seg = jnp.dot(turned[:, part], right, preferred_element_type=jnp.float32)
            seg = seg.astype(jnp.bfloat16).astype(jnp.float32)
            for j in range(size):
                value = seg[:, j * lanes : (j + 1) * lanes] * scale_row[slot, j, :, part]
                weighted[j * lanes : (j + 1) * lanes, part] = value.astype(jnp.bfloat16)
            return carry

        lax.fori_loop(0, blocks, interp, 0, unroll=4)

        for i in range(order // width):
            cols = pl.ds(i * width, width)

            @pl.when(g == 0)
            def _(i=i):
                prec_copy(i).wait()

            prod = jnp.dot(
                weighted[: size * lanes, :], prec_ref[:, cols],
                preferred_element_type=jnp.float32,
            )
            for j in range(size):
                rows = slice(j * lanes, (j + 1) * lanes)
                zbuf[rows, cols] = (prod[rows] * scale_row[slot, j, :, cols]).astype(jnp.bfloat16)

        def back(q, carry):
            part = pl.ds(pl.multiple_of(q * lanes, lanes), lanes)
            left = jnp.concatenate(
                [zbuf[j * lanes : (j + 1) * lanes, part] for j in range(size)], axis=1
            )
            right = jnp.concatenate(pair_of(behind_ref, q), axis=0)
            adj[:, part] = adj[:, part] + jnp.dot(left, right, preferred_element_type=jnp.float32)
            return carry

        lax.fori_loop(0, blocks, back, 0, unroll=4)

    def whole_group(g, carry):
        work(g, batch)
        return carry

    lax.fori_loop(0, count // batch, whole_group, 0)
    for size in range(1, batch):

        @pl.when(lax.rem(count, batch) == size)
        def _(size=size):
            work(count // batch, size)

    @pl.when(count == 0)
    def _():
        for i in range(order // width):
            prec_copy(i).wait()

    zero = jnp.zeros((HALO, lanes), jnp.float32)
    grid[pl.ds(0, HALO), :] = zero
    grid[pl.ds(order + HALO, HALO), :] = zero

    def unturn(q, carry):
        part = pl.ds(pl.multiple_of(q * lanes, lanes), lanes)
        grid[pl.ds(pl.multiple_of(q * lanes + HALO, HALO), lanes), :] = adj[:, part].T
        return carry

    lax.fori_loop(0, blocks, unturn, 0, unroll=4)
    own = chunk - 2 * HALO
    for s in range(parts):
        out_ref[s] = grid[pl.ds(s * own, chunk), :].astype(jnp.bfloat16)


def vmem_need(rows):
    return min(2 * rows * TILE_C * 4, 60 << 20)


def vmem_spec():
    return pl.BlockSpec(memory_space=pltpu.VMEM)


def hbm_spec():
    return pl.BlockSpec(memory_space=pltpu.HBM)


def smem_spec():
    return pl.BlockSpec(memory_space=pltpu.SMEM)


def owner_tables(
    owned_segments, seg_anchor, seg_tiles, seg_max, dev_count, col_count, span, col_tiles, my_device
):
    segs = seg_anchor.shape[0]
    slots = dev_count * seg_max
    slot_ids = jnp.arange(slots, dtype=jnp.int32)
    used = owned_segments >= 0
    seg_hot = owned_segments[:, None] == jnp.arange(segs, dtype=jnp.int32)[None, :]
    anchor_row = jnp.sum(jnp.where(seg_hot, seg_anchor[None, :, 0], 0), axis=1)
    anchor_col = jnp.sum(jnp.where(seg_hot, seg_anchor[None, :, 1], 0), axis=1)
    owner_slab = anchor_row // seg_tiles * span + anchor_col % col_tiles
    owner = owner_slab * col_count + anchor_col // col_tiles
    owner = jnp.where(used, owner, -1)
    by_dev = owner.reshape(dev_count, seg_max)
    slot_in = jnp.arange(seg_max, dtype=jnp.int32)
    before = slot_in[None, :] < slot_in[:, None]
    same = (by_dev[:, :, None] == by_dev[:, None, :]) & before[None]
    place = jnp.sum(same.astype(jnp.int32), axis=2).reshape(slots)
    overflow = jnp.max(jnp.where(used, place, 0)) >= CAP
    mine = owner == my_device
    rank = jnp.cumsum(mine.astype(jnp.int32)) - 1
    count = jnp.sum(mine.astype(jnp.int32))
    longest = segs
    pick = mine[None, :] & (rank[None, :] == jnp.arange(longest, dtype=jnp.int32)[:, None])
    src_slab = slot_ids // (seg_max * col_count)
    columns = [
        owned_segments,
        src_slab * CAP + jnp.minimum(place, CAP - 1),
        src_slab * seg_max + slot_ids % seg_max,
    ]
    listed = jnp.stack(
        [jnp.sum(jnp.where(pick, col[None, :], 0), axis=1) for col in columns], axis=1
    )
    info = jnp.concatenate(
        [count[None], overflow.astype(jnp.int32)[None], listed.reshape(-1)]
    )
    return info, overflow, owner_slab, used, slot_in


def sides(table):
    empty = jnp.zeros_like(table)
    return jnp.stack(
        [jnp.concatenate([table, empty], axis=2), jnp.concatenate([empty, table], axis=2)]
    )


def per_device(
    direction, kappa, land_mask, owned_segments, seg_anchor,
    interp_index, interp_table, precision, obs_scale,
):
    rows_dev, cols_dev = direction.shape
    order = precision.shape[0]
    _, seg_tiles = interp_index.shape
    seg_max = obs_scale.shape[0]
    lanes = TILE_C
    col_tiles = cols_dev // lanes
    slab_count = lax.axis_size("slab")
    col_count = lax.axis_size("col")
    dev_count = slab_count * col_count
    span = order // rows_dev
    assert span == col_tiles and col_count == 2 and slab_count % span == 0
    groups = [list(range(i, i + span)) for i in range(0, slab_count, span)]
    if len(groups) == 1:
        groups = None
    my_slab = lax.axis_index("slab")
    my_col = lax.axis_index("col")
    my_device = my_slab * col_count + my_col
    is_low = my_col == 0

    def edge_rows(start):
        part = slice(start, start + SWEEPS)
        maskf = land_mask[part].astype(jnp.float32)
        return jnp.concatenate([direction[part] * maskf, kappa[part] * maskf], axis=0)

    first_rows, last_rows = edge_rows(0), edge_rows(rows_dev - SWEEPS)
    even = my_slab % 2 == 0
    pairs_a = [(i, i ^ 1) for i in range(slab_count)]
    pairs_b = [(i, i + 1) for i in range(1, slab_count - 1, 2)]
    pairs_b = pairs_b + [(j, i) for i, j in pairs_b]
    send_a = jnp.where(even, last_rows, first_rows)
    send_b = jnp.where(even, first_rows, last_rows)
    got_b = lax.ppermute(send_b, "slab", pairs_b)
    got_a = lax.ppermute(send_a, "slab", pairs_a)

    def swap(array, groups=None):
        return lax.all_to_all(
            array, "slab", split_axis=0, concat_axis=0, tiled=True, axis_index_groups=groups
        )

    scales_out = pl.pallas_call(
        functools.partial(outbox_kernel, seg_tiles=seg_tiles, col_tiles=col_tiles, span=span),
        out_shape=jax.ShapeDtypeStruct((slab_count * CAP, 1, order), jnp.float32),
        in_specs=[smem_spec(), smem_spec(), vmem_spec()],
        out_specs=vmem_spec(),
        compiler_params=pltpu.CompilerParams(vmem_limit_bytes=2 << 20),
        name="outbox",
    )(owned_segments, seg_anchor.reshape(-1), obs_scale)
    few = swap(scales_out)

    def edge_cols(array):
        return jnp.where(is_low, array[:, cols_dev - lanes :], array[:, :lanes])

    edge_mask = edge_cols(land_mask).astype(jnp.float32)
    above = edge_cols(jnp.where(even, got_b, got_a))
    below = edge_cols(jnp.where(even, got_a, got_b))
    blank = jnp.zeros((HALO - SWEEPS, lanes), jnp.float32)

    def with_halo(array, part):
        return jnp.concatenate([blank, above[part], array, below[part], blank], axis=0)

    edge = jnp.stack([
        with_halo(edge_cols(direction) * edge_mask, slice(0, SWEEPS)),
        with_halo(edge_cols(kappa) * edge_mask, slice(SWEEPS, 2 * SWEEPS)),
    ])
    nbr = lax.ppermute(edge, "col", [(0, 1), (1, 0)])

    tiles = col_tiles + 1
    height = rows_dev + 2 * PAD
    buf = pltpu.VMEM((tiles, height, lanes), jnp.float32)
    face_shape = jax.ShapeDtypeStruct((tiles, height, lanes), jnp.float32)
    smoothed, own, fn, fw, fe = pl.pallas_call(
        smooth_first_kernel,
        out_shape=(
            jax.ShapeDtypeStruct((col_tiles, rows_dev, lanes), jnp.bfloat16),
            face_shape, face_shape, face_shape, face_shape,
        ),
        in_specs=[vmem_spec()] * 6,
        out_specs=(hbm_spec(),) * 5,
        scratch_shapes=[pltpu.VMEM((col_tiles, rows_dev, lanes), jnp.bfloat16)]
        + [buf] * 7
        + [pltpu.SemaphoreType.DMA((6,))],
        cost_estimate=pl.CostEstimate(flops=40000000, bytes_accessed=8 << 20, transcendentals=0),
        name="smooth_first",
    )(direction, kappa, land_mask, nbr, got_a, got_b)

    smoothed, owned_segments, seg_anchor, interp_index, interp_table, obs_scale = (
        lax.optimization_barrier(
            (smoothed, owned_segments, seg_anchor, interp_index, interp_table, obs_scale)
        )
    )
    gathered = swap(smoothed, groups)

    info, overflow, owner_slab, used, slot_in = owner_tables(
        owned_segments, seg_anchor, seg_tiles, seg_max, dev_count, col_count, span,
        col_tiles, my_device,
    )
    ahead, behind = sides(interp_table.transpose(0, 2, 1)), sides(interp_table)

    my_owner = lax.dynamic_slice_in_dim(owner_slab, my_device * seg_max, seg_max)
    my_used = lax.dynamic_slice_in_dim(used, my_device * seg_max, seg_max)

    def outbox(cap, position):
        target = jnp.arange(slab_count * cap, dtype=jnp.int32)
        hit = (
            (my_owner * cap + position)[None, :] == target[:, None]
        ) & (my_used & (position < cap))[None, :]
        slot = jnp.sum(jnp.where(hit, slot_in[None, :], 0), axis=1)
        return obs_scale[slot].reshape(slab_count * cap, 1, order)

    many = (slab_count * seg_max, 1, order)
    overflow = overflow & (gathered[0, 0, 0] < jnp.inf)
    everything = lax.cond(
        overflow,
        lambda: swap(outbox(seg_max, slot_in)),
        lambda: pl.pallas_call(
            lambda out_ref: None,
            out_shape=jax.ShapeDtypeStruct(many, jnp.float32),
            out_specs=hbm_spec(),
            name="unread",
        )(),
    )

    chunk = rows_dev + 2 * HALO
    width = min(512, order)
    batch = 4

    returning = pl.pallas_call(
        functools.partial(segments_kernel, width=width, batch=batch),
        out_shape=jax.ShapeDtypeStruct((span, chunk, lanes), jnp.bfloat16),
        in_specs=[smem_spec(), smem_spec(), vmem_spec(), vmem_spec(), vmem_spec()]
        + [hbm_spec()] * 3,
        out_specs=vmem_spec(),
        scratch_shapes=[
            pltpu.VMEM((order, order), jnp.bfloat16),
            pltpu.VMEM((lanes, order), jnp.bfloat16),
            pltpu.VMEM((batch * lanes, order), jnp.bfloat16),
            pltpu.VMEM((batch * lanes, order), jnp.bfloat16),
            pltpu.VMEM((2, batch, 1, order), jnp.float32),
            pltpu.VMEM((lanes, order), jnp.float32),
            pltpu.VMEM((order + 2 * HALO, lanes), jnp.float32),
            pltpu.SemaphoreType.DMA((order // width,)),
            pltpu.SemaphoreType.DMA((2, batch)),
        ],
        cost_estimate=pl.CostEstimate(
            flops=8 * 2 * order * order * lanes, bytes_accessed=12 << 20, transcendentals=0
        ),
        name="segments",
    )(
        info, interp_index, gathered.reshape(order, lanes),
        ahead, behind, precision, few, everything,
    )

    returned = swap(returning, groups)

    if groups is not None:
        returned = lane_edges(returned, slab_count, span, my_slab, rows_dev)

    border = jnp.where(is_low, returned[col_tiles - 1], returned[0])
    border = lax.ppermute(border, "col", [(0, 1), (1, 0)])
    return pl.pallas_call(
        smooth_last_kernel,
        out_shape=jax.ShapeDtypeStruct((rows_dev, cols_dev), jnp.float32),
        in_specs=[vmem_spec()] * 8,
        out_specs=vmem_spec(),
        scratch_shapes=[buf, buf],
        compiler_params=pltpu.CompilerParams(vmem_limit_bytes=vmem_need(8 * tiles * height)),
        cost_estimate=pl.CostEstimate(flops=40000000, bytes_accessed=8 << 20, transcendentals=0),
        name="smooth_last",
    )(returned, border, own, fn, fw, fe, direction, land_mask)


def lane_edges(returned, slab_count, span, my_slab, rows_dev):
    up = [(i, i + 1) for i in range(span - 1, slab_count - 1, span)]
    down = [(j, i) for i, j in up]
    own_last = returned[:, rows_dev : rows_dev + HALO]
    own_first = returned[:, HALO : 2 * HALO]
    above = lax.ppermute(own_last, "slab", up)
    below = lax.ppermute(own_first, "slab", down)
    first = (my_slab % span == 0)
    last = (my_slab % span == span - 1)
    head = jnp.where(first, above, returned[:, :HALO])
    tail = jnp.where(last, below, returned[:, rows_dev + HALO :])
    return jnp.concatenate([head, returned[:, HALO : rows_dev + HALO], tail], axis=1)


def solution(mesh):
    in_specs = (
        P("slab", "col"),
        P("slab", "col"),
        P("slab", "col"),
        P(),
        P(),
        P(),
        P(),
        P(),
        P(("slab", "col"), None),
    )

    return jax.shard_map(
        per_device, mesh=mesh, in_specs=in_specs, out_specs=P("slab", "col"), check_vma=False
    )
```

```python
import functools

import jax
import jax.numpy as jnp
from jax import lax
from jax.experimental import pallas as pl
from jax.experimental.pallas import tpu as pltpu
from jax.sharding import PartitionSpec as P


TILE_C = 128
SWEEPS = 4
HALO = 8
PAD = 16
CHUNKS = 4
CAP = 3


def lane_iota(shape):
    return lax.broadcasted_iota(jnp.int32, shape, len(shape) - 1)


def row_iota(shape):
    return lax.broadcasted_iota(jnp.int32, shape, len(shape) - 2)


def from_left(own, left):
    lanes = own.shape[-1]
    return pltpu.roll(jnp.where(lane_iota(own.shape) == lanes - 1, left, own), 1, 1)


def from_right(own, right):
    lanes = own.shape[-1]
    return pltpu.roll(jnp.where(lane_iota(own.shape) == 0, right, own), lanes - 1, 1)


def face(own, other):
    return jnp.where((own > 0) & (other > 0), 0.5 * (own + other), 0.0)


def sweeps(tiles, rows, bufs, own_ref, fn_ref, fw_ref, fe_ref, finish, ready=None, part_done=None):
    for step in range(SWEEPS):
        src, dst = bufs[step % 2], bufs[1 - step % 2]
        last = step == SWEEPS - 1
        first_row = PAD if last else HALO
        parts = 2 if last else 3
        length = (rows - 2 * (PAD - HALO) if last else rows) // parts

        for index in range(parts):
            start = first_row + index * length
            body = pl.ds(start, length)

            def tile(c, right, u_left, u, src=src, dst=dst, last=last, start=start, body=body):
                u_right = src[right, body, :]
                up = src[c, pl.ds(start - 1, length), :]
                down = src[c, pl.ds(start + 1, length), :]
                out = own_ref[c, body, :] * u + fn_ref[c, body, :] * up
                out = out + fn_ref[c, pl.ds(start + 1, length), :] * down
                out = out + fw_ref[c, body, :] * from_left(u, u_left)
                out = out + fe_ref[c, body, :] * from_right(u, u_right)
                if last:
                    finish(c, start - PAD, out)
                else:
                    dst[c, body, :] = out
                return u, u_right

            def step_tile(c, carry):
                return tile(c, c + 1, *carry)

            carry = src[tiles - 1, body, :], src[0, body, :]
            if ready is not None and step == 0 and index == 0:
                for k in range(CHUNKS):
                    ready(k)
                    low, high = chunk_of(tiles - 1, k)
                    carry = lax.fori_loop(low, high, step_tile, carry, unroll=True)
            else:
                carry = lax.fori_loop(0, tiles - 1, step_tile, carry, unroll=8)
            if not last:
                tile(tiles - 1, 0, *carry)
            elif part_done is not None:
                part_done(start - PAD, length)


def chunk_of(tiles, k):
    return k * tiles // CHUNKS, (k + 1) * tiles // CHUNKS


def column_chunks(refs, scratch, sems, tiles, lanes):
    copies = []
    for k in range(CHUNKS):
        low, high = chunk_of(tiles, k)
        cols = pl.ds(low * lanes, (high - low) * lanes)
        copies.append([
            pltpu.make_async_copy(ref.at[:, cols], buf.at[:, cols], sems.at[i, k])
            for i, (ref, buf) in enumerate(zip(refs, scratch))
        ])
    return copies


def smooth_first_kernel(
    dir_in, kap_in, mask_in, nbr_ref, got_a_ref, got_b_ref,
    out_ref, own_out, fn_out, fw_out, fe_out,
    dir_ref, kap_ref, mask_ref, done, own_ref, fn_ref, fw_ref, fe_ref, u0, u1, kbuf,
    load_sems, sems,
):
    tiles, _, lanes = u0.shape
    loads = column_chunks(
        (dir_in, kap_in, mask_in), (dir_ref, kap_ref, mask_ref), load_sems, tiles - 1, lanes
    )
    for load in sum(loads, []):
        load.start()
    own = dir_ref.shape[0]
    rows = own + 2 * HALO
    edge = (HALO, lanes)
    zero = jnp.zeros(edge, jnp.float32)
    even = lax.rem(lax.axis_index("slab"), 2) == 0
    low = row_iota(edge) < HALO // 2

    def ends(c):
        for part in (pl.ds(0, HALO), pl.ds(PAD + own + HALO, HALO)):
            u0[c, part, :] = zero
            u1[c, part, :] = zero
            kbuf[c, part, :] = zero
        fn_ref[c, pl.ds(PAD + own + HALO, HALO), :] = zero

    def fill(c, carry):
        cols = pl.ds(pl.multiple_of(c * lanes, lanes), lanes)
        maskf = mask_ref[:, cols].astype(jnp.float32)
        u0[c, pl.ds(PAD, own), :] = dir_ref[:, cols] * maskf
        kbuf[c, pl.ds(PAD, own), :] = kap_ref[:, cols] * maskf
        got_a, got_b = got_a_ref[:, cols], got_b_ref[:, cols]
        top = jnp.where(even, got_b, got_a)
        bot = jnp.where(even, got_a, got_b)
        u0[c, pl.ds(HALO, HALO), :] = jnp.where(low, 0.0, pltpu.roll(top, HALO // 2, 0))
        kbuf[c, pl.ds(HALO, HALO), :] = jnp.where(low, 0.0, top)
        u0[c, pl.ds(PAD + own, HALO), :] = jnp.where(low, bot, 0.0)
        kbuf[c, pl.ds(PAD + own, HALO), :] = jnp.where(low, pltpu.roll(bot, HALO // 2, 0), 0.0)
        ends(c)
        return carry

    for k in range(CHUNKS):
        for load in loads[k]:
            load.wait()
        lax.fori_loop(*chunk_of(tiles - 1, k), fill, 0)
    body = pl.ds(HALO, rows)
    lane = lane_iota((rows, lanes))
    near = jnp.where(lax.axis_index("col") == 0, lanes - 1 - lane, lane) >= lanes - SWEEPS
    u0[tiles - 1, body, :] = nbr_ref[0]
    kbuf[tiles - 1, body, :] = jnp.where(near, nbr_ref[1], 0.0)
    ends(tiles - 1)

    def faces(c, right, k_left, k):
        body = pl.ds(HALO, rows)
        k_right = kbuf[right, body, :]
        north = face(k, kbuf[c, pl.ds(HALO - 1, rows), :])
        south = face(k, kbuf[c, pl.ds(HALO + 1, rows), :])
        west = face(k, from_left(k, k_left))
        east = face(k, from_right(k, k_right))
        fn_ref[c, body, :] = north
        fw_ref[c, body, :] = west
        fe_ref[c, body, :] = east
        own_ref[c, body, :] = 1.0 - ((north + south) + (west + east))
        return k, k_right

    body = pl.ds(HALO, rows)
    carry = kbuf[tiles - 1, body, :], kbuf[0, body, :]
    carry = lax.fori_loop(0, tiles - 1, lambda c, carry: faces(c, c + 1, *carry), carry)
    faces(tiles - 1, 0, *carry)
    copies = [
        pltpu.make_async_copy(ref, out, sems.at[i])
        for i, (ref, out) in enumerate(
            ((own_ref, own_out), (fn_ref, fn_out), (fw_ref, fw_out), (fe_ref, fe_out))
        )
    ]
    for copy in copies:
        copy.start()

    def finish(c, row, value):
        done[c, pl.ds(row, value.shape[0]), :] = value.astype(jnp.bfloat16)

    def part_done(row, length):
        part = pl.ds(row, length)
        copy = pltpu.make_async_copy(
            done.at[:, part, :], out_ref.at[:, part, :], sems.at[len(copies)]
        )
        copies.append(copy)
        copy.start()

    sweeps(tiles, rows, (u0, u1), own_ref, fn_ref, fw_ref, fe_ref, finish, part_done=part_done)
    for copy in copies:
        copy.wait()


def smooth_last_kernel(
    ret_ref, nbr_ref, own_in, fn_in, fw_in, fe_in, dir_in, mask_in, out_ref,
    own_ref, fn_ref, fw_ref, fe_ref, dir_ref, mask_ref, u0, u1, load_sems, sems,
):
    tiles, _, lanes = u0.shape
    pairs = ((own_in, own_ref), (fn_in, fn_ref), (fw_in, fw_ref), (fe_in, fe_ref))
    faces = []
    for k in range(CHUNKS):
        low, high = chunk_of(tiles - 1, k)
        part = pl.ds(low, high - low + (1 if k == CHUNKS - 1 else 0))
        faces.append([
            pltpu.make_async_copy(ref.at[part], buf.at[part], sems.at[i, k])
            for i, (ref, buf) in enumerate(pairs)
        ])
    loads = column_chunks((dir_in, mask_in), (dir_ref, mask_ref), load_sems, tiles - 1, lanes)
    for load in sum(faces + loads, []):
        load.start()
    own = dir_ref.shape[0]
    rows = own + 2 * HALO
    zero = jnp.zeros((HALO, lanes), jnp.float32)

    def ends(c):
        for buf in (u0, u1):
            buf[c, pl.ds(0, HALO), :] = zero
            buf[c, pl.ds(PAD + own + HALO, HALO), :] = zero

    def fill(c, carry):
        u0[c, pl.ds(HALO, rows), :] = ret_ref[c].astype(jnp.float32)
        ends(c)
        return carry

    lax.fori_loop(0, tiles - 1, fill, 0)
    u0[tiles - 1, pl.ds(HALO, rows), :] = nbr_ref[...].astype(jnp.float32)
    ends(tiles - 1)

    def finish(c, row, value):
        cols = pl.ds(pl.multiple_of(c * lanes, lanes), lanes)
        part = pl.ds(row, value.shape[0])
        maskf = mask_ref[part, cols].astype(jnp.float32)
        out_ref[part, cols] = maskf * (dir_ref[part, cols] * maskf + value)

    def ready(k):
        for load in faces[k]:
            load.wait()
        if k == CHUNKS - 1:
            for load in sum(loads, []):
                load.wait()

    sweeps(tiles, rows, (u0, u1), own_ref, fn_ref, fw_ref, fe_ref, finish, ready=ready)


def outbox_kernel(owned_ref, anchor_ref, scale_ref, out_ref, *, seg_tiles, col_tiles, span):
    seg_max = scale_ref.shape[0]
    me = lax.axis_index("slab") * lax.axis_size("col") + lax.axis_index("col")
    owners = []
    for i in range(seg_max):
        seg = owned_ref[me * seg_max + i]
        safe = jnp.maximum(seg, 0)
        lane = anchor_ref[0, safe] // seg_tiles
        owner = lane * span + lax.rem(anchor_ref[1, safe], col_tiles)
        owner = jnp.where(seg >= 0, owner, -1)
        place = jnp.int32(0)
        for other in owners:
            place = place + jnp.where(other == owner, 1, 0)
        owners.append(owner)

        @pl.when((seg >= 0) & (place < CAP))
        def _(i=i, owner=owner, place=place):
            out_ref[owner * CAP + place] = scale_ref[i : i + 1, :]


def segments_kernel(
    info_ref, index_ref, x_ref, ahead_ref, behind_ref, prec_in, few_ref, all_ref,
    out_ref, prec_ref, turned, weighted, zbuf, scale_row, adj, grid, prec_sem, scale_sem,
    *, width, batch,
):
    parts, chunk, lanes = out_ref.shape
    order = prec_ref.shape[0]
    blocks = order // lanes
    count = info_ref[0]
    full = info_ref[1]

    def scale_copy(source, row, slot, j):
        return pltpu.make_async_copy(source.at[row], scale_row.at[slot, j], scale_sem.at[slot, j])

    def fetch(g, slot):
        for j in range(batch):
            e = g * batch + j

            @pl.when((e < count) & (full == 0))
            def _(e=e, j=j):
                scale_copy(few_ref, info_ref[3 + 3 * e], slot, j).start()

            @pl.when((e < count) & (full != 0))
            def _(e=e, j=j):
                scale_copy(all_ref, info_ref[4 + 3 * e], slot, j).start()

    def prec_copy(i):
        cols = pl.ds(i * width, width)
        return pltpu.make_async_copy(prec_in.at[:, cols], prec_ref.at[:, cols], prec_sem.at[i])

    for i in range(order // width):
        prec_copy(i).start()
    fetch(0, 0)

    def turn(q, carry):
        part = pl.ds(pl.multiple_of(q * lanes, lanes), lanes)
        turned[:, part] = x_ref[part, :].astype(jnp.float32).T.astype(jnp.bfloat16)
        adj[:, part] = jnp.zeros((lanes, lanes), jnp.float32)
        return carry

    lax.fori_loop(0, blocks, turn, 0, unroll=4)

    def work(g, size):
        slot = lax.rem(g, 2)
        ids = [info_ref[2 + 3 * (g * batch + j)] for j in range(size)]
        for j in range(size):
            scale_copy(few_ref, 0, slot, j).wait()
        fetch(g + 1, 1 - slot)

        def pair_of(table, q):
            sides = []
            for j in range(size):
                low = table[0, index_ref[2 * q, ids[j]]]
                high = table[1, index_ref[2 * q + 1, ids[j]]]
                sides.append(jnp.concatenate([low, high], axis=0))
            return sides

        def interp(q, carry):
            part = pl.ds(pl.multiple_of(q * lanes, lanes), lanes)
            right = jnp.concatenate(pair_of(ahead_ref, q), axis=1)
            seg = jnp.dot(turned[:, part], right, preferred_element_type=jnp.float32)
            seg = seg.astype(jnp.bfloat16).astype(jnp.float32)
            for j in range(size):
                value = seg[:, j * lanes : (j + 1) * lanes] * scale_row[slot, j, :, part]
                weighted[j * lanes : (j + 1) * lanes, part] = value.astype(jnp.bfloat16)
            return carry

        lax.fori_loop(0, blocks, interp, 0, unroll=4)

        for i in range(order // width):
            cols = pl.ds(i * width, width)

            @pl.when(g == 0)
            def _(i=i):
                prec_copy(i).wait()

            prod = jnp.dot(
                weighted[: size * lanes, :], prec_ref[:, cols],
                preferred_element_type=jnp.float32,
            )
            for j in range(size):
                rows = slice(j * lanes, (j + 1) * lanes)
                zbuf[rows, cols] = (prod[rows] * scale_row[slot, j, :, cols]).astype(jnp.bfloat16)

        def back(q, carry):
            part = pl.ds(pl.multiple_of(q * lanes, lanes), lanes)
            left = jnp.concatenate(
                [zbuf[j * lanes : (j + 1) * lanes, part] for j in range(size)], axis=1
            )
            right = jnp.concatenate(pair_of(behind_ref, q), axis=0)
            adj[:, part] = adj[:, part] + jnp.dot(left, right, preferred_element_type=jnp.float32)
            return carry

        lax.fori_loop(0, blocks, back, 0, unroll=4)

    def whole_group(g, carry):
        work(g, batch)
        return carry

    lax.fori_loop(0, count // batch, whole_group, 0)
    for size in range(1, batch):

        @pl.when(lax.rem(count, batch) == size)
        def _(size=size):
            work(count // batch, size)

    @pl.when(count == 0)
    def _():
        for i in range(order // width):
            prec_copy(i).wait()

    zero = jnp.zeros((HALO, lanes), jnp.float32)
    grid[pl.ds(0, HALO), :] = zero
    grid[pl.ds(order + HALO, HALO), :] = zero

    def unturn(q, carry):
        part = pl.ds(pl.multiple_of(q * lanes, lanes), lanes)
        grid[pl.ds(pl.multiple_of(q * lanes + HALO, HALO), lanes), :] = adj[:, part].T
        return carry

    lax.fori_loop(0, blocks, unturn, 0, unroll=4)
    own = chunk - 2 * HALO
    for s in range(parts):
        out_ref[s] = grid[pl.ds(s * own, chunk), :].astype(jnp.bfloat16)


def vmem_spec():
    return pl.BlockSpec(memory_space=pltpu.VMEM)


def hbm_spec():
    return pl.BlockSpec(memory_space=pltpu.HBM)


def smem_spec():
    return pl.BlockSpec(memory_space=pltpu.SMEM)


def owner_tables(
    owned_segments, seg_anchor, seg_tiles, seg_max, dev_count, col_count, span, col_tiles, my_device
):
    segs = seg_anchor.shape[0]
    slots = dev_count * seg_max
    slot_ids = jnp.arange(slots, dtype=jnp.int32)
    used = owned_segments >= 0
    seg_hot = owned_segments[:, None] == jnp.arange(segs, dtype=jnp.int32)[None, :]
    anchor_row = jnp.sum(jnp.where(seg_hot, seg_anchor[None, :, 0], 0), axis=1)
    anchor_col = jnp.sum(jnp.where(seg_hot, seg_anchor[None, :, 1], 0), axis=1)
    owner_slab = anchor_row // seg_tiles * span + anchor_col % col_tiles
    owner = owner_slab * col_count + anchor_col // col_tiles
    owner = jnp.where(used, owner, -1)
    by_dev = owner.reshape(dev_count, seg_max)
    slot_in = jnp.arange(seg_max, dtype=jnp.int32)
    before = slot_in[None, :] < slot_in[:, None]
    same = (by_dev[:, :, None] == by_dev[:, None, :]) & before[None]
    place = jnp.sum(same.astype(jnp.int32), axis=2).reshape(slots)
    overflow = jnp.max(jnp.where(used, place, 0)) >= CAP
    mine = owner == my_device
    rank = jnp.cumsum(mine.astype(jnp.int32)) - 1
    count = jnp.sum(mine.astype(jnp.int32))
    longest = segs
    pick = mine[None, :] & (rank[None, :] == jnp.arange(longest, dtype=jnp.int32)[:, None])
    src_slab = slot_ids // (seg_max * col_count)
    columns = [
        owned_segments,
        src_slab * CAP + jnp.minimum(place, CAP - 1),
        src_slab * seg_max + slot_ids % seg_max,
    ]
    listed = jnp.stack(
        [jnp.sum(jnp.where(pick, col[None, :], 0), axis=1) for col in columns], axis=1
    )
    info = jnp.concatenate(
        [count[None], overflow.astype(jnp.int32)[None], listed.reshape(-1)]
    )
    return info, overflow, owner_slab, used, slot_in


def sides(table):
    empty = jnp.zeros_like(table)
    return jnp.stack(
        [jnp.concatenate([table, empty], axis=2), jnp.concatenate([empty, table], axis=2)]
    )


def per_device(
    direction, kappa, land_mask, owned_segments, seg_anchor,
    interp_index, interp_table, precision, obs_scale,
):
    rows_dev, cols_dev = direction.shape
    order = precision.shape[0]
    _, seg_tiles = interp_index.shape
    seg_max = obs_scale.shape[0]
    lanes = TILE_C
    col_tiles = cols_dev // lanes
    slab_count = lax.axis_size("slab")
    col_count = lax.axis_size("col")
    dev_count = slab_count * col_count
    span = order // rows_dev
    assert span == col_tiles and col_count == 2 and slab_count % span == 0
    groups = [list(range(i, i + span)) for i in range(0, slab_count, span)]
    if len(groups) == 1:
        groups = None
    my_slab = lax.axis_index("slab")
    my_col = lax.axis_index("col")
    my_device = my_slab * col_count + my_col
    is_low = my_col == 0

    def edge_rows(start):
        part = slice(start, start + SWEEPS)
        maskf = land_mask[part].astype(jnp.float32)
        return jnp.concatenate([direction[part] * maskf, kappa[part] * maskf], axis=0)

    first_rows, last_rows = edge_rows(0), edge_rows(rows_dev - SWEEPS)
    even = my_slab % 2 == 0
    pairs_a = [(i, i ^ 1) for i in range(slab_count)]
    pairs_b = [(i, i + 1) for i in range(1, slab_count - 1, 2)]
    pairs_b = pairs_b + [(j, i) for i, j in pairs_b]
    send_a = jnp.where(even, last_rows, first_rows)
    send_b = jnp.where(even, first_rows, last_rows)
    got_b = lax.ppermute(send_b, "slab", pairs_b)
    got_a = lax.ppermute(send_a, "slab", pairs_a)

    def swap(array, groups=None):
        return lax.all_to_all(
            array, "slab", split_axis=0, concat_axis=0, tiled=True, axis_index_groups=groups
        )

    scales_out = pl.pallas_call(
        functools.partial(outbox_kernel, seg_tiles=seg_tiles, col_tiles=col_tiles, span=span),
        out_shape=jax.ShapeDtypeStruct((slab_count * CAP, 1, order), jnp.float32),
        in_specs=[smem_spec(), smem_spec(), vmem_spec()],
        out_specs=vmem_spec(),
        compiler_params=pltpu.CompilerParams(vmem_limit_bytes=2 << 20),
        name="outbox",
    )(owned_segments, seg_anchor.T, obs_scale)
    few = swap(scales_out)

    def edge_cols(array):
        return jnp.where(is_low, array[:, cols_dev - lanes :], array[:, :lanes])

    edge_mask = edge_cols(land_mask).astype(jnp.float32)
    above = edge_cols(jnp.where(even, got_b, got_a))
    below = edge_cols(jnp.where(even, got_a, got_b))
    blank = jnp.zeros((HALO - SWEEPS, lanes), jnp.float32)

    def with_halo(array, part):
        return jnp.concatenate([blank, above[part], array, below[part], blank], axis=0)

    edge = jnp.stack([
        with_halo(edge_cols(direction) * edge_mask, slice(0, SWEEPS)),
        with_halo(edge_cols(kappa) * edge_mask, slice(SWEEPS, 2 * SWEEPS)),
    ])
    nbr = lax.ppermute(edge, "col", [(0, 1), (1, 0)])

    tiles = col_tiles + 1
    height = rows_dev + 2 * PAD
    buf = pltpu.VMEM((tiles, height, lanes), jnp.float32)
    own_float = pltpu.VMEM((rows_dev, cols_dev), jnp.float32)
    own_int = pltpu.VMEM((rows_dev, cols_dev), jnp.int32)
    face_shape = jax.ShapeDtypeStruct((tiles, height, lanes), jnp.float32)
    smoothed, own, fn, fw, fe = pl.pallas_call(
        smooth_first_kernel,
        out_shape=(
            jax.ShapeDtypeStruct((col_tiles, rows_dev, lanes), jnp.bfloat16),
            face_shape, face_shape, face_shape, face_shape,
        ),
        in_specs=[hbm_spec()] * 3 + [vmem_spec()] * 3,
        out_specs=(hbm_spec(),) * 5,
        scratch_shapes=[own_float, own_float, own_int]
        + [pltpu.VMEM((col_tiles, rows_dev, lanes), jnp.bfloat16)]
        + [buf] * 7
        + [pltpu.SemaphoreType.DMA((3, CHUNKS)), pltpu.SemaphoreType.DMA((6,))],
        cost_estimate=pl.CostEstimate(flops=40000000, bytes_accessed=8 << 20, transcendentals=0),
        name="smooth_first",
    )(direction, kappa, land_mask, nbr, got_a, got_b)

    smoothed, owned_segments, seg_anchor, interp_index, interp_table, obs_scale = (
        lax.optimization_barrier(
            (smoothed, owned_segments, seg_anchor, interp_index, interp_table, obs_scale)
        )
    )
    gathered = swap(smoothed, groups)

    info, overflow, owner_slab, used, slot_in = owner_tables(
        owned_segments, seg_anchor, seg_tiles, seg_max, dev_count, col_count, span,
        col_tiles, my_device,
    )
    ahead, behind = sides(interp_table.transpose(0, 2, 1)), sides(interp_table)

    my_owner = lax.dynamic_slice_in_dim(owner_slab, my_device * seg_max, seg_max)
    my_used = lax.dynamic_slice_in_dim(used, my_device * seg_max, seg_max)

    def outbox(cap, position):
        target = jnp.arange(slab_count * cap, dtype=jnp.int32)
        hit = (
            (my_owner * cap + position)[None, :] == target[:, None]
        ) & (my_used & (position < cap))[None, :]
        slot = jnp.sum(jnp.where(hit, slot_in[None, :], 0), axis=1)
        return obs_scale[slot].reshape(slab_count * cap, 1, order)

    many = (slab_count * seg_max, 1, order)
    overflow = overflow & (gathered[0, 0, 0] < jnp.inf)
    everything = lax.cond(
        overflow,
        lambda: swap(outbox(seg_max, slot_in)),
        lambda: pl.pallas_call(
            lambda out_ref: None,
            out_shape=jax.ShapeDtypeStruct(many, jnp.float32),
            out_specs=hbm_spec(),
            name="unread",
        )(),
    )

    chunk = rows_dev + 2 * HALO
    width = min(512, order)
    batch = 4

    returning = pl.pallas_call(
        functools.partial(segments_kernel, width=width, batch=batch),
        out_shape=jax.ShapeDtypeStruct((span, chunk, lanes), jnp.bfloat16),
        in_specs=[smem_spec(), smem_spec(), vmem_spec(), vmem_spec(), vmem_spec()]
        + [hbm_spec()] * 3,
        out_specs=vmem_spec(),
        scratch_shapes=[
            pltpu.VMEM((order, order), jnp.bfloat16),
            pltpu.VMEM((lanes, order), jnp.bfloat16),
            pltpu.VMEM((batch * lanes, order), jnp.bfloat16),
            pltpu.VMEM((batch * lanes, order), jnp.bfloat16),
            pltpu.VMEM((2, batch, 1, order), jnp.float32),
            pltpu.VMEM((lanes, order), jnp.float32),
            pltpu.VMEM((order + 2 * HALO, lanes), jnp.float32),
            pltpu.SemaphoreType.DMA((order // width,)),
            pltpu.SemaphoreType.DMA((2, batch)),
        ],
        compiler_params=pltpu.CompilerParams(vmem_limit_bytes=57 << 20),
        cost_estimate=pl.CostEstimate(
            flops=8 * 2 * order * order * lanes, bytes_accessed=12 << 20, transcendentals=0
        ),
        name="segments",
    )(
        info, interp_index.T, gathered.reshape(order, lanes),
        ahead, behind, precision, few, everything,
    )

    returned = swap(returning, groups)

    if groups is not None:
        returned = lane_edges(returned, slab_count, span, my_slab, rows_dev)

    border = jnp.where(is_low, returned[col_tiles - 1], returned[0])
    border = lax.ppermute(border, "col", [(0, 1), (1, 0)])
    return pl.pallas_call(
        smooth_last_kernel,
        out_shape=jax.ShapeDtypeStruct((rows_dev, cols_dev), jnp.float32),
        in_specs=[vmem_spec()] * 2 + [hbm_spec()] * 6,
        out_specs=vmem_spec(),
        scratch_shapes=[buf] * 4
        + [own_float, own_int, buf, buf]
        + [pltpu.SemaphoreType.DMA((2, CHUNKS)), pltpu.SemaphoreType.DMA((4, CHUNKS))],
        cost_estimate=pl.CostEstimate(flops=40000000, bytes_accessed=8 << 20, transcendentals=0),
        name="smooth_last",
    )(returned, border, own, fn, fw, fe, direction, land_mask)


def lane_edges(returned, slab_count, span, my_slab, rows_dev):
    up = [(i, i + 1) for i in range(span - 1, slab_count - 1, span)]
    down = [(j, i) for i, j in up]
    own_last = returned[:, rows_dev : rows_dev + HALO]
    own_first = returned[:, HALO : 2 * HALO]
    above = lax.ppermute(own_last, "slab", up)
    below = lax.ppermute(own_first, "slab", down)
    first = (my_slab % span == 0)
    last = (my_slab % span == span - 1)
    head = jnp.where(first, above, returned[:, :HALO])
    tail = jnp.where(last, below, returned[:, rows_dev + HALO :])
    return jnp.concatenate([head, returned[:, HALO : rows_dev + HALO], tail], axis=1)


def solution(mesh):
    in_specs = (
        P("slab", "col"),
        P("slab", "col"),
        P("slab", "col"),
        P(),
        P(),
        P(),
        P(),
        P(),
        P(("slab", "col"), None),
    )

    return jax.shard_map(
        per_device, mesh=mesh, in_specs=in_specs, out_specs=P("slab", "col"), check_vma=False
    )
```

```python
import functools

import jax
import jax.numpy as jnp
from jax import lax
from jax.experimental import pallas as pl
from jax.experimental.pallas import tpu as pltpu
from jax.sharding import PartitionSpec as P


TILE_C = 128
SWEEPS = 4
HALO = 8
PAD = 16
CHUNKS = 4
CAP = 4


def lane_iota(shape):
    return lax.broadcasted_iota(jnp.int32, shape, len(shape) - 1)


def row_iota(shape):
    return lax.broadcasted_iota(jnp.int32, shape, len(shape) - 2)


def from_left(own, left):
    lanes = own.shape[-1]
    return pltpu.roll(jnp.where(lane_iota(own.shape) == lanes - 1, left, own), 1, 1)


def from_right(own, right):
    lanes = own.shape[-1]
    return pltpu.roll(jnp.where(lane_iota(own.shape) == 0, right, own), lanes - 1, 1)


def face(own, other):
    return jnp.where(jnp.minimum(own, other) > 0, own + other, 0.0)


def derive(tiles, rows, own_ref, fn_ref, fw_ref, fe_ref):
    def tile(c, right):
        body = pl.ds(HALO, rows)
        west = fw_ref[c, body, :]
        east = from_right(west, fw_ref[right, body, :])
        fe_ref[c, body, :] = east
        vertical = fn_ref[c, body, :] + fn_ref[c, pl.ds(HALO + 1, rows), :]
        own_ref[c, body, :] = 1.0 - (vertical + (west + east))

    def step(c, carry):
        tile(c, c + 1)
        return carry

    lax.fori_loop(0, tiles - 1, step, 0, unroll=2)
    tile(tiles - 1, 0)


def sweeps(tiles, rows, bufs, own_ref, fn_ref, fw_ref, fe_ref, finish, before_last=None, part_done=None):
    for step in range(SWEEPS):
        src, dst = bufs[step % 2], bufs[1 - step % 2]
        last = step == SWEEPS - 1
        first_row = PAD if last else HALO
        parts = 2 if last else 3
        if last and before_last is not None:
            before_last()
        length = (rows - 2 * (PAD - HALO) if last else rows) // parts

        for index in range(parts):
            start = first_row + index * length
            body = pl.ds(start, length)

            def tile(c, right, u_left, u, src=src, dst=dst, last=last, start=start, body=body):
                u_right = src[right, body, :]
                up = src[c, pl.ds(start - 1, length), :]
                down = src[c, pl.ds(start + 1, length), :]
                out = own_ref[c, body, :] * u + fn_ref[c, body, :] * up
                out = out + fn_ref[c, pl.ds(start + 1, length), :] * down
                out = out + fw_ref[c, body, :] * from_left(u, u_left)
                out = out + fe_ref[c, body, :] * from_right(u, u_right)
                if last:
                    finish(c, start - PAD, out)
                else:
                    dst[c, body, :] = out
                return u, u_right

            def step_tile(c, carry):
                return tile(c, c + 1, *carry)

            carry = src[tiles - 1, body, :], src[0, body, :]
            carry = lax.fori_loop(0, tiles - 1, step_tile, carry, unroll=8)
            if not last:
                tile(tiles - 1, 0, *carry)
            elif part_done is not None:
                part_done(start - PAD, length)


def chunk_of(tiles, k):
    return k * tiles // CHUNKS, (k + 1) * tiles // CHUNKS


def column_chunks(refs, scratch, sems, tiles, lanes):
    copies = []
    for k in range(CHUNKS):
        low, high = chunk_of(tiles, k)
        cols = pl.ds(low * lanes, (high - low) * lanes)
        copies.append([
            pltpu.make_async_copy(ref.at[:, cols], buf.at[:, cols], sems.at[i, k])
            for i, (ref, buf) in enumerate(zip(refs, scratch))
        ])
    return copies


def smooth_first_kernel(
    dir_in, kap_in, mask_in, nbr_ref, got_a_ref, got_b_ref,
    out_ref, fn_out, fw_out,
    dir_ref, kap_ref, mask_ref, done, own_ref, fn_ref, fw_ref, fe_ref, u0, u1, kbuf,
    load_sems, sems,
):
    tiles, _, lanes = u0.shape
    loads = column_chunks(
        (dir_in, kap_in, mask_in), (dir_ref, kap_ref, mask_ref), load_sems, tiles - 1, lanes
    )
    for load in sum(loads, []):
        load.start()
    own = dir_ref.shape[0]
    rows = own + 2 * HALO
    edge = (HALO, lanes)
    zero = jnp.zeros(edge, jnp.float32)
    even = lax.rem(lax.axis_index("slab"), 2) == 0
    low = row_iota(edge) < HALO // 2

    def edges(c, cols):
        got_a, got_b = got_a_ref[:, cols], got_b_ref[:, cols]
        top = jnp.where(even, got_b, got_a)
        bot = jnp.where(even, got_a, got_b)
        u0[c, pl.ds(HALO, HALO), :] = jnp.where(low, 0.0, pltpu.roll(top, HALO // 2, 0))
        kbuf[c, pl.ds(HALO, HALO), :] = jnp.where(low, 0.0, 0.5 * top)
        u0[c, pl.ds(PAD + own, HALO), :] = jnp.where(low, bot, 0.0)
        kbuf[c, pl.ds(PAD + own, HALO), :] = jnp.where(
            low, 0.5 * pltpu.roll(bot, HALO // 2, 0), 0.0
        )
        for part in (pl.ds(0, HALO), pl.ds(PAD + own + HALO, HALO)):
            u0[c, part, :] = zero
            u1[c, part, :] = zero
            kbuf[c, part, :] = zero
        fn_ref[c, pl.ds(PAD + own + HALO, HALO), :] = zero

    def fill(c, carry):
        cols = pl.ds(pl.multiple_of(c * lanes, lanes), lanes)
        maskf = mask_ref[:, cols].astype(jnp.float32)
        u0[c, pl.ds(PAD, own), :] = dir_ref[:, cols] * maskf
        kbuf[c, pl.ds(PAD, own), :] = kap_ref[:, cols] * (0.5 * maskf)
        edges(c, cols)
        return carry

    u0[tiles - 1, pl.ds(PAD, own), :] = nbr_ref[0]
    kbuf[tiles - 1, pl.ds(PAD, own), :] = 0.5 * nbr_ref[1]
    edges(tiles - 1, pl.ds((tiles - 1) * lanes, lanes))

    def faces(c, k_left):
        body = pl.ds(HALO, rows)
        k = kbuf[c, body, :]
        fn_ref[c, body, :] = face(k, kbuf[c, pl.ds(HALO - 1, rows), :])
        fw_ref[c, body, :] = face(k, from_left(k, k_left))
        return k

    k_left = kbuf[tiles - 1, pl.ds(HALO, rows), :]
    for k in range(CHUNKS):
        for load in loads[k]:
            load.wait()
        low_tile, high_tile = chunk_of(tiles - 1, k)
        lax.fori_loop(low_tile, high_tile, fill, 0)
        k_left = lax.fori_loop(low_tile, high_tile, faces, k_left)
    faces(tiles - 1, k_left)
    copies = [
        pltpu.make_async_copy(ref, out, sems.at[i])
        for i, (ref, out) in enumerate(((fn_ref, fn_out), (fw_ref, fw_out)))
    ]
    for copy in copies:
        copy.start()
    derive(tiles, rows, own_ref, fn_ref, fw_ref, fe_ref)

    def finish(c, row, value):
        done[c, pl.ds(row, value.shape[0]), :] = value.astype(jnp.bfloat16)

    def part_done(row, length):
        part = pl.ds(row, length)
        copy = pltpu.make_async_copy(
            done.at[:, part, :], out_ref.at[:, part, :], sems.at[len(copies)]
        )
        copies.append(copy)
        copy.start()

    sweeps(tiles, rows, (u0, u1), own_ref, fn_ref, fw_ref, fe_ref, finish, part_done=part_done)
    for copy in copies:
        copy.wait()


def smooth_last_kernel(
    ret_ref, nbr_ref, fn_in, fw_in, dir_in, mask_in, out_ref,
    own_ref, fn_ref, fw_ref, fe_ref, dir_ref, mask_ref, u0, u1, load_sems, sems,
):
    tiles, _, lanes = u0.shape
    faces = [
        pltpu.make_async_copy(ref, buf, sems.at[i])
        for i, (ref, buf) in enumerate(((fn_in, fn_ref), (fw_in, fw_ref)))
    ]
    loads = sum(
        column_chunks((dir_in, mask_in), (dir_ref, mask_ref), load_sems, tiles - 1, lanes), []
    )
    for load in faces + loads:
        load.start()
    own, chunk = dir_ref.shape[0], ret_ref.shape[1]
    rows = own + 2 * HALO
    zero = jnp.zeros((PAD, lanes), jnp.float32)

    def put(c, value):
        for part in (pl.ds(0, PAD), pl.ds(PAD + own, PAD)):
            u0[c, part, :] = zero
            u1[c, part, :] = zero
        u0[c, pl.ds(PAD - (chunk - own) // 2, chunk), :] = value.astype(jnp.float32)

    def fill(c, carry):
        put(c, ret_ref[c])
        return carry

    lax.fori_loop(0, tiles - 1, fill, 0)
    put(tiles - 1, nbr_ref[...])
    for load in faces:
        load.wait()
    derive(tiles, rows, own_ref, fn_ref, fw_ref, fe_ref)

    def finish(c, row, value):
        cols = pl.ds(pl.multiple_of(c * lanes, lanes), lanes)
        part = pl.ds(row, value.shape[0])
        maskf = mask_ref[part, cols].astype(jnp.float32)
        out_ref[part, cols] = maskf * (dir_ref[part, cols] * maskf + value)

    def before_last():
        for load in loads:
            load.wait()

    sweeps(tiles, rows, (u0, u1), own_ref, fn_ref, fw_ref, fe_ref, finish, before_last)


def outbox_kernel(
    owned_in, anchor_in, scale_ref, out_ref, owned_ref, anchor_ref, sems,
    *, seg_tiles, col_tiles, span,
):
    copies = [
        pltpu.make_async_copy(owned_in, owned_ref, sems.at[0]),
        pltpu.make_async_copy(anchor_in, anchor_ref, sems.at[1]),
    ]
    for copy in copies:
        copy.start()
    for copy in copies:
        copy.wait()
    seg_max = scale_ref.shape[0]
    me = lax.axis_index("slab") * lax.axis_size("col") + lax.axis_index("col")
    owners = []
    for i in range(seg_max):
        seg = owned_ref[me * seg_max + i]
        safe = jnp.maximum(seg, 0)
        lane = anchor_ref[0, safe] // seg_tiles
        owner = lane * span + lax.rem(anchor_ref[1, safe], col_tiles)
        owner = jnp.where(seg >= 0, owner, -1)
        place = jnp.int32(0)
        for other in owners:
            place = place + jnp.where(other == owner, 1, 0)
        owners.append(owner)

        @pl.when((seg >= 0) & (place < CAP))
        def _(i=i, owner=owner, place=place):
            out_ref[owner * CAP + place] = scale_ref[i : i + 1, :]


def segments_kernel(
    info_ref, index_ref, x_ref, ahead_ref, behind_ref, prec_in, few_ref, all_ref,
    out_ref, prec_ref, turned, weighted, zbuf, scale_row, adj, grid, prec_sem, scale_sem,
    *, width, batch,
):
    parts, chunk, lanes = out_ref.shape
    order = prec_ref.shape[0]
    blocks = order // lanes
    count = info_ref[0]
    full = info_ref[1]

    def scale_copy(source, row, slot, j):
        return pltpu.make_async_copy(source.at[row], scale_row.at[slot, j], scale_sem.at[slot, j])

    def fetch(g, slot):
        for j in range(batch):
            e = g * batch + j

            @pl.when((e < count) & (full == 0))
            def _(e=e, j=j):
                scale_copy(few_ref, info_ref[3 + 3 * e], slot, j).start()

            @pl.when((e < count) & (full != 0))
            def _(e=e, j=j):
                scale_copy(all_ref, info_ref[4 + 3 * e], slot, j).start()

    def prec_copy(i):
        cols = pl.ds(i * width, width)
        return pltpu.make_async_copy(prec_in.at[:, cols], prec_ref.at[:, cols], prec_sem.at[i])

    for i in range(order // width):
        prec_copy(i).start()
    fetch(0, 0)

    def turn(q, carry):
        part = pl.ds(pl.multiple_of(q * lanes, lanes), lanes)
        turned[:, part] = x_ref[part, :].astype(jnp.float32).T.astype(jnp.bfloat16)
        adj[:, part] = jnp.zeros((lanes, lanes), jnp.float32)
        return carry

    lax.fori_loop(0, blocks, turn, 0, unroll=4)

    def work(g, size):
        slot = lax.rem(g, 2)
        ids = [info_ref[2 + 3 * (g * batch + j)] for j in range(size)]
        for j in range(size):
            scale_copy(few_ref, 0, slot, j).wait()
        fetch(g + 1, 1 - slot)

        def pair_of(table, q):
            sides = []
            for j in range(size):
                low = table[0, index_ref[2 * q, ids[j]]]
                high = table[1, index_ref[2 * q + 1, ids[j]]]
                sides.append(jnp.concatenate([low, high], axis=0))
            return sides

        def interp(q, carry):
            part = pl.ds(pl.multiple_of(q * lanes, lanes), lanes)
            right = jnp.concatenate(pair_of(ahead_ref, q), axis=1)
            seg = jnp.dot(turned[:, part], right, preferred_element_type=jnp.float32)
            seg = seg.astype(jnp.bfloat16).astype(jnp.float32)
            for j in range(size):
                value = seg[:, j * lanes : (j + 1) * lanes] * scale_row[slot, j, :, part]
                weighted[j * lanes : (j + 1) * lanes, part] = value.astype(jnp.bfloat16)
            return carry

        lax.fori_loop(0, blocks, interp, 0, unroll=4)

        for i in range(order // width):
            cols = pl.ds(i * width, width)

            @pl.when(g == 0)
            def _(i=i):
                prec_copy(i).wait()

            prod = jnp.dot(
                weighted[: size * lanes, :], prec_ref[:, cols],
                preferred_element_type=jnp.float32,
            )
            for j in range(size):
                rows = slice(j * lanes, (j + 1) * lanes)
                zbuf[rows, cols] = (prod[rows] * scale_row[slot, j, :, cols]).astype(jnp.bfloat16)

        def back(q, carry):
            part = pl.ds(pl.multiple_of(q * lanes, lanes), lanes)
            left = jnp.concatenate(
                [zbuf[j * lanes : (j + 1) * lanes, part] for j in range(size)], axis=1
            )
            right = jnp.concatenate(pair_of(behind_ref, q), axis=0)
            adj[:, part] = adj[:, part] + jnp.dot(left, right, preferred_element_type=jnp.float32)
            return carry

        lax.fori_loop(0, blocks, back, 0, unroll=4)

    def whole_group(g, carry):
        work(g, batch)
        return carry

    lax.fori_loop(0, count // batch, whole_group, 0)
    for size in range(1, batch):

        @pl.when(lax.rem(count, batch) == size)
        def _(size=size):
            work(count // batch, size)

    @pl.when(count == 0)
    def _():
        for i in range(order // width):
            prec_copy(i).wait()

    zero = jnp.zeros((HALO, lanes), jnp.float32)
    grid[pl.ds(0, HALO), :] = zero
    grid[pl.ds(order + HALO, HALO), :] = zero

    def unturn(q, carry):
        part = pl.ds(pl.multiple_of(q * lanes, lanes), lanes)
        grid[pl.ds(pl.multiple_of(q * lanes + HALO, HALO), lanes), :] = adj[:, part].T
        return carry

    lax.fori_loop(0, blocks, unturn, 0, unroll=4)
    own = order // parts
    first = HALO - (chunk - own) // 2
    for s in range(parts):
        out_ref[s] = grid[pl.ds(s * own + first, chunk), :].astype(jnp.bfloat16)


def vmem_spec():
    return pl.BlockSpec(memory_space=pltpu.VMEM)


def hbm_spec():
    return pl.BlockSpec(memory_space=pltpu.HBM)


def smem_spec():
    return pl.BlockSpec(memory_space=pltpu.SMEM)


def owner_tables(
    owned_segments, seg_anchor, seg_tiles, seg_max, dev_count, col_count, span, col_tiles, my_device
):
    segs = seg_anchor.shape[0]
    slots = dev_count * seg_max
    slot_ids = jnp.arange(slots, dtype=jnp.int32)
    used = owned_segments >= 0
    seg_hot = owned_segments[:, None] == jnp.arange(segs, dtype=jnp.int32)[None, :]
    anchor_row = jnp.sum(jnp.where(seg_hot, seg_anchor[None, :, 0], 0), axis=1)
    anchor_col = jnp.sum(jnp.where(seg_hot, seg_anchor[None, :, 1], 0), axis=1)
    owner_slab = anchor_row // seg_tiles * span + anchor_col % col_tiles
    owner = owner_slab * col_count + anchor_col // col_tiles
    owner = jnp.where(used, owner, -1)
    by_dev = owner.reshape(dev_count, seg_max)
    slot_in = jnp.arange(seg_max, dtype=jnp.int32)
    before = slot_in[None, :] < slot_in[:, None]
    same = (by_dev[:, :, None] == by_dev[:, None, :]) & before[None]
    place = jnp.sum(same.astype(jnp.int32), axis=2).reshape(slots)
    overflow = jnp.max(jnp.where(used, place, 0)) >= CAP
    mine = owner == my_device
    rank = jnp.cumsum(mine.astype(jnp.int32)) - 1
    count = jnp.sum(mine.astype(jnp.int32))
    longest = segs
    pick = mine[None, :] & (rank[None, :] == jnp.arange(longest, dtype=jnp.int32)[:, None])
    src_slab = slot_ids // (seg_max * col_count)
    columns = [
        owned_segments,
        src_slab * CAP + jnp.minimum(place, CAP - 1),
        src_slab * seg_max + slot_ids % seg_max,
    ]
    listed = jnp.stack(
        [jnp.sum(jnp.where(pick, col[None, :], 0), axis=1) for col in columns], axis=1
    )
    info = jnp.concatenate(
        [count[None], overflow.astype(jnp.int32)[None], listed.reshape(-1)]
    )
    return info, overflow, owner_slab, used, slot_in


def sides(table):
    empty = jnp.zeros_like(table)
    return jnp.stack(
        [jnp.concatenate([table, empty], axis=2), jnp.concatenate([empty, table], axis=2)]
    )


def per_device(
    direction, kappa, land_mask, owned_segments, seg_anchor,
    interp_index, interp_table, precision, obs_scale,
):
    rows_dev, cols_dev = direction.shape
    order = precision.shape[0]
    _, seg_tiles = interp_index.shape
    seg_max = obs_scale.shape[0]
    lanes = TILE_C
    col_tiles = cols_dev // lanes
    slab_count = lax.axis_size("slab")
    col_count = lax.axis_size("col")
    dev_count = slab_count * col_count
    span = order // rows_dev
    assert span == col_tiles and col_count == 2 and slab_count % span == 0
    groups = [list(range(i, i + span)) for i in range(0, slab_count, span)]
    if len(groups) == 1:
        groups = None
    my_slab = lax.axis_index("slab")
    my_col = lax.axis_index("col")
    my_device = my_slab * col_count + my_col
    is_low = my_col == 0

    def edge_cols(array):
        return jnp.where(is_low, array[:, cols_dev - lanes :], array[:, :lanes])

    edge_mask = edge_cols(land_mask).astype(jnp.float32)
    edge = jnp.stack([edge_cols(direction) * edge_mask, edge_cols(kappa) * edge_mask])
    nbr = lax.ppermute(edge, "col", [(0, 1), (1, 0)])
    near = jnp.where(
        is_low, lane_iota((1, lanes)) < SWEEPS, lane_iota((1, lanes)) >= lanes - SWEEPS
    )
    nbr = jnp.where(near[None], nbr, 0.0)

    def edge_rows(start):
        part = slice(start, start + SWEEPS)
        maskf = land_mask[part].astype(jnp.float32)
        field = jnp.concatenate([direction[part] * maskf, nbr[0, part]], axis=1)
        coeff = jnp.concatenate([kappa[part] * maskf, nbr[1, part]], axis=1)
        return jnp.concatenate([field, coeff], axis=0)

    first_rows, last_rows = edge_rows(0), edge_rows(rows_dev - SWEEPS)
    even = my_slab % 2 == 0
    pairs_a = [(i, i ^ 1) for i in range(slab_count)]
    pairs_b = [(i, i + 1) for i in range(1, slab_count - 1, 2)]
    pairs_b = pairs_b + [(j, i) for i, j in pairs_b]
    got_b = lax.ppermute(jnp.where(even, first_rows, last_rows), "slab", pairs_b)
    got_a = lax.ppermute(jnp.where(even, last_rows, first_rows), "slab", pairs_a)

    def swap(array, groups=None):
        return lax.all_to_all(
            array, "slab", split_axis=0, concat_axis=0, tiled=True, axis_index_groups=groups
        )

    scales_out = pl.pallas_call(
        functools.partial(outbox_kernel, seg_tiles=seg_tiles, col_tiles=col_tiles, span=span),
        out_shape=jax.ShapeDtypeStruct((slab_count * CAP, 1, order), jnp.float32),
        in_specs=[hbm_spec(), hbm_spec(), vmem_spec()],
        out_specs=vmem_spec(),
        scratch_shapes=[
            pltpu.SMEM(owned_segments.shape, jnp.int32),
            pltpu.SMEM(seg_anchor.shape[::-1], jnp.int32),
            pltpu.SemaphoreType.DMA((2,)),
        ],
        name="outbox",
    )(owned_segments, seg_anchor.T, obs_scale)
    few = swap(scales_out)

    tiles = col_tiles + 1
    height = rows_dev + 2 * PAD
    buf = pltpu.VMEM((tiles, height, lanes), jnp.float32)
    own_float = pltpu.VMEM((rows_dev, cols_dev), jnp.float32)
    own_int = pltpu.VMEM((rows_dev, cols_dev), jnp.int32)
    face_shape = jax.ShapeDtypeStruct((tiles, height, lanes), jnp.float32)
    smoothed, fn, fw = pl.pallas_call(
        smooth_first_kernel,
        out_shape=(
            jax.ShapeDtypeStruct((col_tiles, rows_dev, lanes), jnp.bfloat16),
            face_shape, face_shape,
        ),
        in_specs=[hbm_spec()] * 3 + [vmem_spec()] * 3,
        out_specs=(hbm_spec(),) * 3,
        scratch_shapes=[own_float, own_float, own_int]
        + [pltpu.VMEM((col_tiles, rows_dev, lanes), jnp.bfloat16)]
        + [buf] * 7
        + [pltpu.SemaphoreType.DMA((3, CHUNKS)), pltpu.SemaphoreType.DMA((4,))],
        cost_estimate=pl.CostEstimate(flops=40000000, bytes_accessed=8 << 20, transcendentals=0),
        name="smooth_first",
    )(direction, kappa, land_mask, nbr, got_a, got_b)

    smoothed, owned_segments, seg_anchor, interp_index, interp_table, obs_scale = (
        lax.optimization_barrier(
            (smoothed, owned_segments, seg_anchor, interp_index, interp_table, obs_scale)
        )
    )
    gathered = swap(smoothed, groups)

    info, overflow, owner_slab, used, slot_in = owner_tables(
        owned_segments, seg_anchor, seg_tiles, seg_max, dev_count, col_count, span,
        col_tiles, my_device,
    )
    ahead, behind = sides(interp_table.transpose(0, 2, 1)), sides(interp_table)

    my_owner = lax.dynamic_slice_in_dim(owner_slab, my_device * seg_max, seg_max)
    my_used = lax.dynamic_slice_in_dim(used, my_device * seg_max, seg_max)

    def outbox(cap, position):
        target = jnp.arange(slab_count * cap, dtype=jnp.int32)
        hit = (
            (my_owner * cap + position)[None, :] == target[:, None]
        ) & (my_used & (position < cap))[None, :]
        slot = jnp.sum(jnp.where(hit, slot_in[None, :], 0), axis=1)
        return obs_scale[slot].reshape(slab_count * cap, 1, order)

    many = (slab_count * seg_max, 1, order)
    everything = lax.cond(
        overflow,
        lambda: swap(outbox(seg_max, slot_in)),
        lambda: pl.pallas_call(
            lambda out_ref: None,
            out_shape=jax.ShapeDtypeStruct(many, jnp.float32),
            out_specs=hbm_spec(),
            name="unread",
        )(),
    )

    chunk = rows_dev + 2 * SWEEPS
    width = min(512, order)
    batch = 4

    returning = pl.pallas_call(
        functools.partial(segments_kernel, width=width, batch=batch),
        out_shape=jax.ShapeDtypeStruct((span, chunk, lanes), jnp.bfloat16),
        in_specs=[smem_spec(), smem_spec(), vmem_spec(), vmem_spec(), vmem_spec()]
        + [hbm_spec()] * 3,
        out_specs=vmem_spec(),
        scratch_shapes=[
            pltpu.VMEM((order, order), jnp.bfloat16),
            pltpu.VMEM((lanes, order), jnp.bfloat16),
            pltpu.VMEM((batch * lanes, order), jnp.bfloat16),
            pltpu.VMEM((batch * lanes, order), jnp.bfloat16),
            pltpu.VMEM((2, batch, 1, order), jnp.float32),
            pltpu.VMEM((lanes, order), jnp.float32),
            pltpu.VMEM((order + 2 * HALO, lanes), jnp.float32),
            pltpu.SemaphoreType.DMA((order // width,)),
            pltpu.SemaphoreType.DMA((2, batch)),
        ],
        compiler_params=pltpu.CompilerParams(vmem_limit_bytes=57 << 20),
        cost_estimate=pl.CostEstimate(
            flops=8 * 2 * order * order * lanes, bytes_accessed=12 << 20, transcendentals=0
        ),
        name="segments",
    )(
        info, interp_index.T, gathered.reshape(order, lanes),
        ahead, behind, precision, few, everything,
    )

    returned = swap(returning, groups)

    if groups is not None:
        returned = lane_edges(returned, slab_count, span, my_slab, rows_dev)

    border = jnp.where(is_low, returned[col_tiles - 1], returned[0])
    border = lax.ppermute(border, "col", [(0, 1), (1, 0)])
    return pl.pallas_call(
        smooth_last_kernel,
        out_shape=jax.ShapeDtypeStruct((rows_dev, cols_dev), jnp.float32),
        in_specs=[vmem_spec()] * 2 + [hbm_spec()] * 4,
        out_specs=vmem_spec(),
        scratch_shapes=[buf] * 4
        + [own_float, own_int, buf, buf]
        + [pltpu.SemaphoreType.DMA((2, CHUNKS)), pltpu.SemaphoreType.DMA((2,))],
        cost_estimate=pl.CostEstimate(flops=40000000, bytes_accessed=8 << 20, transcendentals=0),
        name="smooth_last",
    )(returned, border, fn, fw, direction, land_mask)


def lane_edges(returned, slab_count, span, my_slab, rows_dev):
    halo = SWEEPS
    up = [(i, i + 1) for i in range(span - 1, slab_count - 1, span)]
    down = [(j, i) for i, j in up]
    own = returned[:, halo : halo + rows_dev]
    above = lax.ppermute(own[:, rows_dev - halo :], "slab", up)
    below = lax.ppermute(own[:, :halo], "slab", down)
    first = my_slab % span == 0
    last = my_slab % span == span - 1
    head = jnp.where(first, above, returned[:, :halo])
    tail = jnp.where(last, below, returned[:, halo + rows_dev :])
    return jnp.concatenate([head, own, tail], axis=1)


def solution(mesh):
    in_specs = (
        P("slab", "col"),
        P("slab", "col"),
        P("slab", "col"),
        P(),
        P(),
        P(),
        P(),
        P(),
        P(("slab", "col"), None),
    )

    return jax.shard_map(
        per_device, mesh=mesh, in_specs=in_specs, out_specs=P("slab", "col"), check_vma=False
    )
```

```python
import functools

import jax
import jax.numpy as jnp
from jax import lax
from jax.experimental import pallas as pl
from jax.experimental.pallas import tpu as pltpu
from jax.sharding import PartitionSpec as P


TILE_C = 128
SWEEPS = 4
HALO = 8
PAD = 16
CHUNKS = 4
CAP = 4


def lane_iota(shape):
    return lax.broadcasted_iota(jnp.int32, shape, len(shape) - 1)


def row_iota(shape):
    return lax.broadcasted_iota(jnp.int32, shape, len(shape) - 2)


def from_left(own, left):
    lanes = own.shape[-1]
    return pltpu.roll(jnp.where(lane_iota(own.shape) == lanes - 1, left, own), 1, 1)


def from_right(own, right):
    lanes = own.shape[-1]
    return pltpu.roll(jnp.where(lane_iota(own.shape) == 0, right, own), lanes - 1, 1)


def face(own, other):
    return jnp.where(jnp.minimum(own, other) > 0, own + other, 0.0)


def derive(tiles, rows, own_ref, fn_ref, fw_ref, fe_ref):
    def tile(c, right):
        body = pl.ds(HALO, rows)
        west = fw_ref[c, body, :]
        east = from_right(west, fw_ref[right, body, :])
        fe_ref[c, body, :] = east
        vertical = fn_ref[c, body, :] + fn_ref[c, pl.ds(HALO + 1, rows), :]
        own_ref[c, body, :] = 1.0 - (vertical + (west + east))

    def step(c, carry):
        tile(c, c + 1)
        return carry

    lax.fori_loop(0, tiles - 1, step, 0, unroll=2)
    tile(tiles - 1, 0)


def sweeps(tiles, rows, bufs, own_ref, fn_ref, fw_ref, fe_ref, finish, before_last=None, part_done=None):
    for step in range(SWEEPS):
        src, dst = bufs[step % 2], bufs[1 - step % 2]
        last = step == SWEEPS - 1
        first_row = PAD if last else HALO
        parts = 2 if last else 3
        if last and before_last is not None:
            before_last()
        length = (rows - 2 * (PAD - HALO) if last else rows) // parts

        for index in range(parts):
            start = first_row + index * length
            body = pl.ds(start, length)

            def tile(c, right, u_left, u, src=src, dst=dst, last=last, start=start, body=body):
                u_right = src[right, body, :]
                up = src[c, pl.ds(start - 1, length), :]
                down = src[c, pl.ds(start + 1, length), :]
                out = own_ref[c, body, :] * u + fn_ref[c, body, :] * up
                out = out + fn_ref[c, pl.ds(start + 1, length), :] * down
                out = out + fw_ref[c, body, :] * from_left(u, u_left)
                out = out + fe_ref[c, body, :] * from_right(u, u_right)
                if last:
                    finish(c, start - PAD, out)
                else:
                    dst[c, body, :] = out
                return u, u_right

            def step_tile(c, carry):
                return tile(c, c + 1, *carry)

            carry = src[tiles - 1, body, :], src[0, body, :]
            carry = lax.fori_loop(0, tiles - 1, step_tile, carry, unroll=8)
            if not last:
                tile(tiles - 1, 0, *carry)
            elif part_done is not None:
                part_done(start - PAD, length)


def chunk_of(tiles, k):
    return k * tiles // CHUNKS, (k + 1) * tiles // CHUNKS


def column_chunks(refs, scratch, sems, tiles, lanes):
    copies = []
    for k in range(CHUNKS):
        low, high = chunk_of(tiles, k)
        cols = pl.ds(low * lanes, (high - low) * lanes)
        copies.append([
            pltpu.make_async_copy(ref.at[:, cols], buf.at[:, cols], sems.at[i, k])
            for i, (ref, buf) in enumerate(zip(refs, scratch))
        ])
    return copies


def smooth_first_kernel(
    dir_in, kap_in, mask_in, nbr_ref, got_a_ref, got_b_ref,
    out_ref, fn_out, fw_out,
    dir_ref, kap_ref, mask_ref, done, own_ref, fn_ref, fw_ref, fe_ref, u0, u1, kbuf,
    load_sems, sems,
):
    tiles, _, lanes = u0.shape
    loads = column_chunks(
        (dir_in, kap_in, mask_in), (dir_ref, kap_ref, mask_ref), load_sems, tiles - 1, lanes
    )
    for load in sum(loads, []):
        load.start()
    own = dir_ref.shape[0]
    rows = own + 2 * HALO
    edge = (HALO, lanes)
    zero = jnp.zeros(edge, jnp.float32)
    even = lax.rem(lax.axis_index("slab"), 2) == 0
    low = row_iota(edge) < HALO // 2

    def edges(c, cols):
        got_a, got_b = got_a_ref[:, cols], got_b_ref[:, cols]
        top = jnp.where(even, got_b, got_a)
        bot = jnp.where(even, got_a, got_b)
        u0[c, pl.ds(HALO, HALO), :] = jnp.where(low, 0.0, pltpu.roll(top, HALO // 2, 0))
        kbuf[c, pl.ds(HALO, HALO), :] = jnp.where(low, 0.0, 0.5 * top)
        u0[c, pl.ds(PAD + own, HALO), :] = jnp.where(low, bot, 0.0)
        kbuf[c, pl.ds(PAD + own, HALO), :] = jnp.where(
            low, 0.5 * pltpu.roll(bot, HALO // 2, 0), 0.0
        )
        for part in (pl.ds(0, HALO), pl.ds(PAD + own + HALO, HALO)):
            u0[c, part, :] = zero
            u1[c, part, :] = zero
            kbuf[c, part, :] = zero
        fn_ref[c, pl.ds(PAD + own + HALO, HALO), :] = zero

    def fill(c, carry):
        cols = pl.ds(pl.multiple_of(c * lanes, lanes), lanes)
        maskf = mask_ref[:, cols].astype(jnp.float32)
        u0[c, pl.ds(PAD, own), :] = dir_ref[:, cols] * maskf
        kbuf[c, pl.ds(PAD, own), :] = kap_ref[:, cols] * (0.5 * maskf)
        edges(c, cols)
        return carry

    u0[tiles - 1, pl.ds(PAD, own), :] = nbr_ref[0]
    kbuf[tiles - 1, pl.ds(PAD, own), :] = 0.5 * nbr_ref[1]
    edges(tiles - 1, pl.ds((tiles - 1) * lanes, lanes))

    def faces(c, k_left):
        body = pl.ds(HALO, rows)
        k = kbuf[c, body, :]
        fn_ref[c, body, :] = face(k, kbuf[c, pl.ds(HALO - 1, rows), :])
        fw_ref[c, body, :] = face(k, from_left(k, k_left))
        return k

    k_left = kbuf[tiles - 1, pl.ds(HALO, rows), :]
    for k in range(CHUNKS):
        for load in loads[k]:
            load.wait()
        low_tile, high_tile = chunk_of(tiles - 1, k)
        lax.fori_loop(low_tile, high_tile, fill, 0)
        k_left = lax.fori_loop(low_tile, high_tile, faces, k_left)
    faces(tiles - 1, k_left)
    copies = [
        pltpu.make_async_copy(ref, out, sems.at[i])
        for i, (ref, out) in enumerate(((fn_ref, fn_out), (fw_ref, fw_out)))
    ]
    for copy in copies:
        copy.start()
    derive(tiles, rows, own_ref, fn_ref, fw_ref, fe_ref)

    def finish(c, row, value):
        done[c, pl.ds(row, value.shape[0]), :] = value.astype(jnp.bfloat16)

    def part_done(row, length):
        part = pl.ds(row, length)
        copy = pltpu.make_async_copy(
            done.at[:, part, :], out_ref.at[:, part, :], sems.at[len(copies)]
        )
        copies.append(copy)
        copy.start()

    sweeps(tiles, rows, (u0, u1), own_ref, fn_ref, fw_ref, fe_ref, finish, part_done=part_done)
    for copy in copies:
        copy.wait()


def smooth_last_kernel(
    ret_ref, nbr_ref, fn_in, fw_in, dir_in, mask_in, out_ref,
    own_ref, fn_ref, fw_ref, fe_ref, dir_ref, mask_ref, u0, u1, load_sems, sems,
):
    tiles, _, lanes = u0.shape
    faces = [
        pltpu.make_async_copy(ref, buf, sems.at[i])
        for i, (ref, buf) in enumerate(((fn_in, fn_ref), (fw_in, fw_ref)))
    ]
    loads = sum(
        column_chunks((dir_in, mask_in), (dir_ref, mask_ref), load_sems, tiles - 1, lanes), []
    )
    for load in faces + loads:
        load.start()
    own, chunk = dir_ref.shape[0], ret_ref.shape[1]
    rows = own + 2 * HALO
    zero = jnp.zeros((PAD, lanes), jnp.float32)

    def put(c, value):
        for part in (pl.ds(0, PAD), pl.ds(PAD + own, PAD)):
            u0[c, part, :] = zero
            u1[c, part, :] = zero
        u0[c, pl.ds(PAD - (chunk - own) // 2, chunk), :] = value.astype(jnp.float32)

    def fill(c, carry):
        put(c, ret_ref[c])
        return carry

    lax.fori_loop(0, tiles - 1, fill, 0)
    put(tiles - 1, nbr_ref[...])
    for load in faces:
        load.wait()
    derive(tiles, rows, own_ref, fn_ref, fw_ref, fe_ref)

    def finish(c, row, value):
        cols = pl.ds(pl.multiple_of(c * lanes, lanes), lanes)
        part = pl.ds(row, value.shape[0])
        maskf = mask_ref[part, cols].astype(jnp.float32)
        out_ref[part, cols] = maskf * (dir_ref[part, cols] * maskf + value)

    def before_last():
        for load in loads:
            load.wait()

    sweeps(tiles, rows, (u0, u1), own_ref, fn_ref, fw_ref, fe_ref, finish, before_last)


def outbox_kernel(
    owned_in, anchor_in, scale_ref, out_ref, owned_ref, anchor_ref, sems,
    *, seg_tiles, col_tiles, span,
):
    copies = [
        pltpu.make_async_copy(owned_in, owned_ref, sems.at[0]),
        pltpu.make_async_copy(anchor_in, anchor_ref, sems.at[1]),
    ]
    for copy in copies:
        copy.start()
    for copy in copies:
        copy.wait()
    seg_max = scale_ref.shape[0]
    me = lax.axis_index("slab") * lax.axis_size("col") + lax.axis_index("col")
    owners = []
    for i in range(seg_max):
        seg = owned_ref[me * seg_max + i]
        safe = jnp.maximum(seg, 0)
        lane = anchor_ref[0, safe] // seg_tiles
        owner = lane * span + lax.rem(anchor_ref[1, safe], col_tiles)
        owner = jnp.where(seg >= 0, owner, -1)
        place = jnp.int32(0)
        for other in owners:
            place = place + jnp.where(other == owner, 1, 0)
        owners.append(owner)

        @pl.when((seg >= 0) & (place < CAP))
        def _(i=i, owner=owner, place=place):
            out_ref[owner * CAP + place] = scale_ref[i : i + 1, :]


def segments_kernel(
    info_ref, index_ref, x_ref, ahead_ref, behind_ref, prec_in, few_ref, all_ref,
    out_ref, prec_ref, turned, weighted, zbuf, scale_row, adj, grid, prec_sem, scale_sem,
    *, width, sizes,
):
    parts, chunk, lanes = out_ref.shape
    order = prec_ref.shape[0]
    blocks = order // lanes
    pieces = order // width
    batch = sizes[-1]
    count = info_ref[0]
    full = info_ref[1]

    def prec_copy(i):
        cols = pl.ds(pl.multiple_of(i * width, width), width)
        return pltpu.make_async_copy(prec_in.at[:, cols], prec_ref.at[:, cols], prec_sem.at[i])

    def scale_copy(source, row, j):
        return pltpu.make_async_copy(source.at[row], scale_row.at[j], scale_sem.at[j])

    def fetch(g):
        for j in range(batch):
            e = g * batch + j

            @pl.when((e < count) & (full == 0))
            def _(e=e, j=j):
                scale_copy(few_ref, info_ref[3 + 3 * e], j).start()

            @pl.when((e < count) & (full != 0))
            def _(e=e, j=j):
                scale_copy(all_ref, info_ref[4 + 3 * e], j).start()

            @pl.when(e >= count)
            def _(j=j):
                scale_row[j] = jnp.zeros((1, order), jnp.float32)

    prec_copy(0).start()
    fetch(0)
    prec_copy(1).start()

    def turn(q, carry):
        part = pl.ds(pl.multiple_of(q * lanes, lanes), lanes)
        turned[:, part] = x_ref[part, :].astype(jnp.float32).T.astype(jnp.bfloat16)
        adj[:, part] = jnp.zeros((lanes, lanes), jnp.float32)
        return carry

    lax.fori_loop(0, blocks, turn, 0, unroll=4)

    def work(g, size, live):
        ids = []
        for j in range(size):
            e = g * batch + j
            ids.append(info_ref[2 + 3 * jnp.minimum(e, count - 1)])

            @pl.when(j < live)
            def _(j=j):
                scale_copy(few_ref, 0, j).wait()

        def pair_of(table, q):
            sides = []
            for j in range(size):
                low = table[0, index_ref[2 * q, ids[j]]]
                high = table[1, index_ref[2 * q + 1, ids[j]]]
                sides.append(jnp.concatenate([low, high], axis=0))
            return sides

        def interp(q, carry):
            part = pl.ds(pl.multiple_of(q * lanes, lanes), lanes)
            right = jnp.concatenate(pair_of(ahead_ref, q), axis=1)
            seg = jnp.dot(turned[:, part], right, preferred_element_type=jnp.float32)
            seg = seg.astype(jnp.bfloat16).astype(jnp.float32)
            for j in range(size):
                value = seg[:, j * lanes : (j + 1) * lanes] * scale_row[j, :, part]
                weighted[j * lanes : (j + 1) * lanes, part] = value.astype(jnp.bfloat16)
            return carry

        lax.fori_loop(0, blocks, interp, 0, unroll=4 if size <= 4 else 2)

        def product(i, carry):
            cols = pl.ds(pl.multiple_of(i * width, width), width)

            @pl.when(g == 0)
            def _():
                prec_copy(i).wait()

            @pl.when((g == 0) & (i + 2 < pieces))
            def _():
                prec_copy(i + 2).start()

            prod = jnp.dot(
                weighted[: size * lanes, :], prec_ref[:, cols],
                preferred_element_type=jnp.float32,
            )
            for j in range(size):
                rows = slice(j * lanes, (j + 1) * lanes)
                zbuf[rows, cols] = (prod[rows] * scale_row[j, :, cols]).astype(jnp.bfloat16)
            return carry

        lax.fori_loop(0, pieces, product, 0)

        def back(q, carry):
            part = pl.ds(pl.multiple_of(q * lanes, lanes), lanes)
            left = jnp.concatenate(
                [zbuf[j * lanes : (j + 1) * lanes, part] for j in range(size)], axis=1
            )
            right = jnp.concatenate(pair_of(behind_ref, q), axis=0)
            adj[:, part] = adj[:, part] + jnp.dot(left, right, preferred_element_type=jnp.float32)
            return carry

        lax.fori_loop(0, blocks, back, 0, unroll=4 if size <= 4 else 2)

    def whole_group(g, carry):
        work(g, batch, batch)
        fetch(g + 1)
        return carry

    lax.fori_loop(0, count // batch, whole_group, 0)
    rest = lax.rem(count, batch)
    smaller = 0
    for size in sizes:

        @pl.when((rest > smaller) & (rest <= size))
        def _(size=size):
            work(count // batch, size, rest)

        smaller = size

    @pl.when(count == 0)
    def _():
        for i in range(2):
            prec_copy(i).wait()

    zero = jnp.zeros((HALO, lanes), jnp.float32)
    grid[pl.ds(0, HALO), :] = zero
    grid[pl.ds(order + HALO, HALO), :] = zero

    def unturn(q, carry):
        part = pl.ds(pl.multiple_of(q * lanes, lanes), lanes)
        grid[pl.ds(pl.multiple_of(q * lanes + HALO, HALO), lanes), :] = adj[:, part].T
        return carry

    lax.fori_loop(0, blocks, unturn, 0, unroll=4)
    own = order // parts
    first = HALO - (chunk - own) // 2
    for s in range(parts):
        out_ref[s] = grid[pl.ds(s * own + first, chunk), :].astype(jnp.bfloat16)


def vmem_spec():
    return pl.BlockSpec(memory_space=pltpu.VMEM)


def hbm_spec():
    return pl.BlockSpec(memory_space=pltpu.HBM)


def smem_spec():
    return pl.BlockSpec(memory_space=pltpu.SMEM)


def owner_tables(
    owned_segments, seg_anchor, seg_tiles, seg_max, dev_count, col_count, span, col_tiles, my_device
):
    segs = seg_anchor.shape[0]
    slots = dev_count * seg_max
    slot_ids = jnp.arange(slots, dtype=jnp.int32)
    used = owned_segments >= 0
    seg_hot = owned_segments[:, None] == jnp.arange(segs, dtype=jnp.int32)[None, :]
    anchor_row = jnp.sum(jnp.where(seg_hot, seg_anchor[None, :, 0], 0), axis=1)
    anchor_col = jnp.sum(jnp.where(seg_hot, seg_anchor[None, :, 1], 0), axis=1)
    owner_slab = anchor_row // seg_tiles * span + anchor_col % col_tiles
    owner = owner_slab * col_count + anchor_col // col_tiles
    owner = jnp.where(used, owner, -1)
    by_dev = owner.reshape(dev_count, seg_max)
    slot_in = jnp.arange(seg_max, dtype=jnp.int32)
    before = slot_in[None, :] < slot_in[:, None]
    same = (by_dev[:, :, None] == by_dev[:, None, :]) & before[None]
    place = jnp.sum(same.astype(jnp.int32), axis=2).reshape(slots)
    overflow = jnp.max(jnp.where(used, place, 0)) >= CAP
    mine = owner == my_device
    rank = jnp.cumsum(mine.astype(jnp.int32)) - 1
    count = jnp.sum(mine.astype(jnp.int32))
    longest = segs
    pick = mine[None, :] & (rank[None, :] == jnp.arange(longest, dtype=jnp.int32)[:, None])
    src_slab = slot_ids // (seg_max * col_count)
    columns = [
        owned_segments,
        src_slab * CAP + jnp.minimum(place, CAP - 1),
        src_slab * seg_max + slot_ids % seg_max,
    ]
    listed = jnp.stack(
        [jnp.sum(jnp.where(pick, col[None, :], 0), axis=1) for col in columns], axis=1
    )
    info = jnp.concatenate(
        [count[None], overflow.astype(jnp.int32)[None], listed.reshape(-1)]
    )
    return info, overflow, owner_slab, used, slot_in


def sides(table):
    empty = jnp.zeros_like(table)
    return jnp.stack(
        [jnp.concatenate([table, empty], axis=2), jnp.concatenate([empty, table], axis=2)]
    )


def per_device(
    direction, kappa, land_mask, owned_segments, seg_anchor,
    interp_index, interp_table, precision, obs_scale,
):
    rows_dev, cols_dev = direction.shape
    order = precision.shape[0]
    _, seg_tiles = interp_index.shape
    seg_max = obs_scale.shape[0]
    lanes = TILE_C
    col_tiles = cols_dev // lanes
    slab_count = lax.axis_size("slab")
    col_count = lax.axis_size("col")
    dev_count = slab_count * col_count
    span = order // rows_dev
    assert span == col_tiles and col_count == 2 and slab_count % span == 0
    groups = [list(range(i, i + span)) for i in range(0, slab_count, span)]
    if len(groups) == 1:
        groups = None
    my_slab = lax.axis_index("slab")
    my_col = lax.axis_index("col")
    my_device = my_slab * col_count + my_col
    is_low = my_col == 0

    def edge_cols(array):
        return jnp.where(is_low, array[:, cols_dev - lanes :], array[:, :lanes])

    edge_mask = edge_cols(land_mask).astype(jnp.float32)
    edge = jnp.stack([edge_cols(direction) * edge_mask, edge_cols(kappa) * edge_mask])
    nbr = lax.ppermute(edge, "col", [(0, 1), (1, 0)])
    near = jnp.where(
        is_low, lane_iota((1, lanes)) < SWEEPS, lane_iota((1, lanes)) >= lanes - SWEEPS
    )
    nbr = jnp.where(near[None], nbr, 0.0)

    def edge_rows(start):
        part = slice(start, start + SWEEPS)
        maskf = land_mask[part].astype(jnp.float32)
        field = jnp.concatenate([direction[part] * maskf, nbr[0, part]], axis=1)
        coeff = jnp.concatenate([kappa[part] * maskf, nbr[1, part]], axis=1)
        return jnp.concatenate([field, coeff], axis=0)

    first_rows, last_rows = edge_rows(0), edge_rows(rows_dev - SWEEPS)
    even = my_slab % 2 == 0
    pairs_a = [(i, i ^ 1) for i in range(slab_count)]
    pairs_b = [(i, i + 1) for i in range(1, slab_count - 1, 2)]
    pairs_b = pairs_b + [(j, i) for i, j in pairs_b]
    got_b = lax.ppermute(jnp.where(even, first_rows, last_rows), "slab", pairs_b)
    got_a = lax.ppermute(jnp.where(even, last_rows, first_rows), "slab", pairs_a)

    def swap(array, groups=None):
        return lax.all_to_all(
            array, "slab", split_axis=0, concat_axis=0, tiled=True, axis_index_groups=groups
        )

    scales_out = pl.pallas_call(
        functools.partial(outbox_kernel, seg_tiles=seg_tiles, col_tiles=col_tiles, span=span),
        out_shape=jax.ShapeDtypeStruct((slab_count * CAP, 1, order), jnp.float32),
        in_specs=[hbm_spec(), hbm_spec(), vmem_spec()],
        out_specs=vmem_spec(),
        scratch_shapes=[
            pltpu.SMEM(owned_segments.shape, jnp.int32),
            pltpu.SMEM(seg_anchor.shape[::-1], jnp.int32),
            pltpu.SemaphoreType.DMA((2,)),
        ],
        name="outbox",
    )(owned_segments, seg_anchor.T, obs_scale)
    few = swap(scales_out)

    tiles = col_tiles + 1
    height = rows_dev + 2 * PAD
    buf = pltpu.VMEM((tiles, height, lanes), jnp.float32)
    own_float = pltpu.VMEM((rows_dev, cols_dev), jnp.float32)
    own_int = pltpu.VMEM((rows_dev, cols_dev), jnp.int32)
    face_shape = jax.ShapeDtypeStruct((tiles, height, lanes), jnp.float32)
    smoothed, fn, fw = pl.pallas_call(
        smooth_first_kernel,
        out_shape=(
            jax.ShapeDtypeStruct((col_tiles, rows_dev, lanes), jnp.bfloat16),
            face_shape, face_shape,
        ),
        in_specs=[hbm_spec()] * 3 + [vmem_spec()] * 3,
        out_specs=(hbm_spec(),) * 3,
        scratch_shapes=[own_float, own_float, own_int]
        + [pltpu.VMEM((col_tiles, rows_dev, lanes), jnp.bfloat16)]
        + [buf] * 7
        + [pltpu.SemaphoreType.DMA((3, CHUNKS)), pltpu.SemaphoreType.DMA((4,))],
        cost_estimate=pl.CostEstimate(flops=40000000, bytes_accessed=8 << 20, transcendentals=0),
        name="smooth_first",
    )(direction, kappa, land_mask, nbr, got_a, got_b)

    smoothed, owned_segments, seg_anchor, interp_index, interp_table, obs_scale = (
        lax.optimization_barrier(
            (smoothed, owned_segments, seg_anchor, interp_index, interp_table, obs_scale)
        )
    )
    gathered = swap(smoothed, groups)

    info, overflow, owner_slab, used, slot_in = owner_tables(
        owned_segments, seg_anchor, seg_tiles, seg_max, dev_count, col_count, span,
        col_tiles, my_device,
    )
    ahead, behind = sides(interp_table.transpose(0, 2, 1)), sides(interp_table)

    my_owner = lax.dynamic_slice_in_dim(owner_slab, my_device * seg_max, seg_max)
    my_used = lax.dynamic_slice_in_dim(used, my_device * seg_max, seg_max)

    def outbox(cap, position):
        target = jnp.arange(slab_count * cap, dtype=jnp.int32)
        hit = (
            (my_owner * cap + position)[None, :] == target[:, None]
        ) & (my_used & (position < cap))[None, :]
        slot = jnp.sum(jnp.where(hit, slot_in[None, :], 0), axis=1)
        return obs_scale[slot].reshape(slab_count * cap, 1, order)

    many = (slab_count * seg_max, 1, order)
    everything = lax.cond(
        overflow,
        lambda: swap(outbox(seg_max, slot_in)),
        lambda: pl.pallas_call(
            lambda out_ref: None,
            out_shape=jax.ShapeDtypeStruct(many, jnp.float32),
            out_specs=hbm_spec(),
            name="unread",
        )(),
    )

    chunk = rows_dev + 2 * SWEEPS
    width = order // 4
    sizes = (1, 2, 3, 4, 6, 8, 10)
    batch = sizes[-1]

    returning = pl.pallas_call(
        functools.partial(segments_kernel, width=width, sizes=sizes),
        out_shape=jax.ShapeDtypeStruct((span, chunk, lanes), jnp.bfloat16),
        in_specs=[smem_spec(), smem_spec(), vmem_spec(), vmem_spec(), vmem_spec()]
        + [hbm_spec()] * 3,
        out_specs=vmem_spec(),
        scratch_shapes=[
            pltpu.VMEM((order, order), jnp.bfloat16),
            pltpu.VMEM((lanes, order), jnp.bfloat16),
            pltpu.VMEM((batch * lanes, order), jnp.bfloat16),
            pltpu.VMEM((batch * lanes, order), jnp.bfloat16),
            pltpu.VMEM((batch, 1, order), jnp.float32),
            pltpu.VMEM((lanes, order), jnp.float32),
            pltpu.VMEM((order + 2 * HALO, lanes), jnp.float32),
            pltpu.SemaphoreType.DMA((order // width,)),
            pltpu.SemaphoreType.DMA((batch,)),
        ],
        compiler_params=pltpu.CompilerParams(vmem_limit_bytes=57 << 20),
        cost_estimate=pl.CostEstimate(
            flops=8 * 2 * order * order * lanes, bytes_accessed=12 << 20, transcendentals=0
        ),
        name="segments",
    )(
        info, interp_index.T, gathered.reshape(order, lanes),
        ahead, behind, precision, few, everything,
    )

    returned = swap(returning, groups)

    if groups is not None:
        returned = lane_edges(returned, slab_count, span, my_slab, rows_dev)

    border = jnp.where(is_low, returned[col_tiles - 1], returned[0])
    border = lax.ppermute(border, "col", [(0, 1), (1, 0)])
    return pl.pallas_call(
        smooth_last_kernel,
        out_shape=jax.ShapeDtypeStruct((rows_dev, cols_dev), jnp.float32),
        in_specs=[vmem_spec()] * 2 + [hbm_spec()] * 4,
        out_specs=vmem_spec(),
        scratch_shapes=[buf] * 4
        + [own_float, own_int, buf, buf]
        + [pltpu.SemaphoreType.DMA((2, CHUNKS)), pltpu.SemaphoreType.DMA((2,))],
        cost_estimate=pl.CostEstimate(flops=40000000, bytes_accessed=8 << 20, transcendentals=0),
        name="smooth_last",
    )(returned, border, fn, fw, direction, land_mask)


def lane_edges(returned, slab_count, span, my_slab, rows_dev):
    halo = SWEEPS
    up = [(i, i + 1) for i in range(span - 1, slab_count - 1, span)]
    down = [(j, i) for i, j in up]
    own = returned[:, halo : halo + rows_dev]
    above = lax.ppermute(own[:, rows_dev - halo :], "slab", up)
    below = lax.ppermute(own[:, :halo], "slab", down)
    first = my_slab % span == 0
    last = my_slab % span == span - 1
    head = jnp.where(first, above, returned[:, :halo])
    tail = jnp.where(last, below, returned[:, halo + rows_dev :])
    return jnp.concatenate([head, own, tail], axis=1)


def solution(mesh):
    in_specs = (
        P("slab", "col"),
        P("slab", "col"),
        P("slab", "col"),
        P(),
        P(),
        P(),
        P(),
        P(),
        P(("slab", "col"), None),
    )

    return jax.shard_map(
        per_device, mesh=mesh, in_specs=in_specs, out_specs=P("slab", "col"), check_vma=False
    )
```

```python
import functools

import jax
import jax.numpy as jnp
from jax import lax
from jax.experimental import pallas as pl
from jax.experimental.pallas import tpu as pltpu
from jax.sharding import PartitionSpec as P


TILE_C = 128
SWEEPS = 4
HALO = 8
PAD = 16
CHUNKS = 4
CAP = 4


def lane_iota(shape):
    return lax.broadcasted_iota(jnp.int32, shape, len(shape) - 1)


def row_iota(shape):
    return lax.broadcasted_iota(jnp.int32, shape, len(shape) - 2)


def from_left(own, left):
    lanes = own.shape[-1]
    return pltpu.roll(jnp.where(lane_iota(own.shape) == lanes - 1, left, own), 1, 1)


def from_right(own, right):
    lanes = own.shape[-1]
    return pltpu.roll(jnp.where(lane_iota(own.shape) == 0, right, own), lanes - 1, 1)


def face(own, other):
    return jnp.where(jnp.minimum(own, other) > 0, own + other, 0.0)


def derive(tiles, rows, own_ref, fn_ref, fw_ref, fe_ref):
    def tile(c, right):
        body = pl.ds(HALO, rows)
        west = fw_ref[c, body, :]
        east = from_right(west, fw_ref[right, body, :])
        fe_ref[c, body, :] = east
        vertical = fn_ref[c, body, :] + fn_ref[c, pl.ds(HALO + 1, rows), :]
        own_ref[c, body, :] = 1.0 - (vertical + (west + east))

    def step(c, carry):
        tile(c, c + 1)
        return carry

    lax.fori_loop(0, tiles - 1, step, 0, unroll=2)
    tile(tiles - 1, 0)


def sweeps(tiles, rows, bufs, own_ref, fn_ref, fw_ref, fe_ref, finish, before_last=None, part_done=None):
    for step in range(SWEEPS):
        src, dst = bufs[step % 2], bufs[1 - step % 2]
        last = step == SWEEPS - 1
        first_row = PAD if last else HALO
        parts = 2 if last else 3
        if last and before_last is not None:
            before_last()
        length = (rows - 2 * (PAD - HALO) if last else rows) // parts

        for index in range(parts):
            start = first_row + index * length
            body = pl.ds(start, length)

            def tile(c, right, u_left, u, src=src, dst=dst, last=last, start=start, body=body):
                u_right = src[right, body, :]
                up = src[c, pl.ds(start - 1, length), :]
                down = src[c, pl.ds(start + 1, length), :]
                out = own_ref[c, body, :] * u + fn_ref[c, body, :] * up
                out = out + fn_ref[c, pl.ds(start + 1, length), :] * down
                out = out + fw_ref[c, body, :] * from_left(u, u_left)
                out = out + fe_ref[c, body, :] * from_right(u, u_right)
                if last:
                    finish(c, start - PAD, out)
                else:
                    dst[c, body, :] = out
                return u, u_right

            def step_tile(c, carry):
                return tile(c, c + 1, *carry)

            carry = src[tiles - 1, body, :], src[0, body, :]
            carry = lax.fori_loop(0, tiles - 1, step_tile, carry, unroll=8)
            if not last:
                tile(tiles - 1, 0, *carry)
            elif part_done is not None:
                part_done(start - PAD, length)


def chunk_of(tiles, k):
    return k * tiles // CHUNKS, (k + 1) * tiles // CHUNKS


def column_chunks(refs, scratch, sems, tiles, lanes):
    copies = []
    for k in range(CHUNKS):
        low, high = chunk_of(tiles, k)
        cols = pl.ds(low * lanes, (high - low) * lanes)
        copies.append([
            pltpu.make_async_copy(ref.at[:, cols], buf.at[:, cols], sems.at[i, k])
            for i, (ref, buf) in enumerate(zip(refs, scratch))
        ])
    return copies


def smooth_first_kernel(
    dir_in, kap_in, mask_in, nbr_ref, got_a_ref, got_b_ref,
    out_ref, fn_out, fw_out,
    dir_ref, kap_ref, mask_ref, done, own_ref, fn_ref, fw_ref, fe_ref, u0, u1, kbuf,
    load_sems, sems,
):
    tiles, _, lanes = u0.shape
    loads = column_chunks(
        (dir_in, kap_in, mask_in), (dir_ref, kap_ref, mask_ref), load_sems, tiles - 1, lanes
    )
    for load in sum(loads, []):
        load.start()
    own = dir_ref.shape[0]
    rows = own + 2 * HALO
    edge = (HALO, lanes)
    zero = jnp.zeros(edge, jnp.float32)
    even = lax.rem(lax.axis_index("slab"), 2) == 0
    low = row_iota(edge) < HALO // 2

    def edges(c, cols):
        got_a, got_b = got_a_ref[:, cols], got_b_ref[:, cols]
        top = jnp.where(even, got_b, got_a)
        bot = jnp.where(even, got_a, got_b)
        u0[c, pl.ds(HALO, HALO), :] = jnp.where(low, 0.0, pltpu.roll(top, HALO // 2, 0))
        kbuf[c, pl.ds(HALO, HALO), :] = jnp.where(low, 0.0, 0.5 * top)
        u0[c, pl.ds(PAD + own, HALO), :] = jnp.where(low, bot, 0.0)
        kbuf[c, pl.ds(PAD + own, HALO), :] = jnp.where(
            low, 0.5 * pltpu.roll(bot, HALO // 2, 0), 0.0
        )
        for part in (pl.ds(0, HALO), pl.ds(PAD + own + HALO, HALO)):
            u0[c, part, :] = zero
            u1[c, part, :] = zero
            kbuf[c, part, :] = zero
        fn_ref[c, pl.ds(PAD + own + HALO, HALO), :] = zero

    def fill(c, carry):
        cols = pl.ds(pl.multiple_of(c * lanes, lanes), lanes)
        maskf = mask_ref[:, cols].astype(jnp.float32)
        u0[c, pl.ds(PAD, own), :] = dir_ref[:, cols] * maskf
        kbuf[c, pl.ds(PAD, own), :] = kap_ref[:, cols] * (0.5 * maskf)
        edges(c, cols)
        return carry

    u0[tiles - 1, pl.ds(PAD, own), :] = nbr_ref[0]
    kbuf[tiles - 1, pl.ds(PAD, own), :] = 0.5 * nbr_ref[1]
    edges(tiles - 1, pl.ds((tiles - 1) * lanes, lanes))

    def faces(c, k_left):
        body = pl.ds(HALO, rows)
        k = kbuf[c, body, :]
        fn_ref[c, body, :] = face(k, kbuf[c, pl.ds(HALO - 1, rows), :])
        fw_ref[c, body, :] = face(k, from_left(k, k_left))
        return k

    k_left = kbuf[tiles - 1, pl.ds(HALO, rows), :]
    for k in range(CHUNKS):
        for load in loads[k]:
            load.wait()
        low_tile, high_tile = chunk_of(tiles - 1, k)
        lax.fori_loop(low_tile, high_tile, fill, 0)
        k_left = lax.fori_loop(low_tile, high_tile, faces, k_left)
    faces(tiles - 1, k_left)
    copies = [
        pltpu.make_async_copy(ref, out, sems.at[i])
        for i, (ref, out) in enumerate(((fn_ref, fn_out), (fw_ref, fw_out)))
    ]
    for copy in copies:
        copy.start()
    derive(tiles, rows, own_ref, fn_ref, fw_ref, fe_ref)

    def finish(c, row, value):
        done[c, pl.ds(row, value.shape[0]), :] = value.astype(jnp.bfloat16)

    def part_done(row, length):
        part = pl.ds(row, length)
        copy = pltpu.make_async_copy(
            done.at[:, part, :], out_ref.at[:, part, :], sems.at[len(copies)]
        )
        copies.append(copy)
        copy.start()

    sweeps(tiles, rows, (u0, u1), own_ref, fn_ref, fw_ref, fe_ref, finish, part_done=part_done)
    for copy in copies:
        copy.wait()


def smooth_last_kernel(
    ret_ref, nbr_ref, fn_in, fw_in, dir_in, mask_in, out_ref,
    own_ref, fn_ref, fw_ref, fe_ref, dir_ref, mask_ref, u0, u1, load_sems, sems,
):
    tiles, _, lanes = u0.shape
    faces = [
        pltpu.make_async_copy(ref, buf, sems.at[i])
        for i, (ref, buf) in enumerate(((fn_in, fn_ref), (fw_in, fw_ref)))
    ]
    loads = sum(
        column_chunks((dir_in, mask_in), (dir_ref, mask_ref), load_sems, tiles - 1, lanes), []
    )
    for load in faces + loads:
        load.start()
    own, chunk = dir_ref.shape[0], ret_ref.shape[1]
    rows = own + 2 * HALO
    zero = jnp.zeros((PAD, lanes), jnp.float32)

    def put(c, value):
        for part in (pl.ds(0, PAD), pl.ds(PAD + own, PAD)):
            u0[c, part, :] = zero
            u1[c, part, :] = zero
        u0[c, pl.ds(PAD - (chunk - own) // 2, chunk), :] = value.astype(jnp.float32)

    def fill(c, carry):
        put(c, ret_ref[c])
        return carry

    lax.fori_loop(0, tiles - 1, fill, 0)
    put(tiles - 1, nbr_ref[...])
    for load in faces:
        load.wait()
    derive(tiles, rows, own_ref, fn_ref, fw_ref, fe_ref)

    def finish(c, row, value):
        cols = pl.ds(pl.multiple_of(c * lanes, lanes), lanes)
        part = pl.ds(row, value.shape[0])
        maskf = mask_ref[part, cols].astype(jnp.float32)
        out_ref[part, cols] = maskf * (dir_ref[part, cols] * maskf + value)

    def before_last():
        for load in loads:
            load.wait()

    sweeps(tiles, rows, (u0, u1), own_ref, fn_ref, fw_ref, fe_ref, finish, before_last)


def outbox_kernel(
    owned_in, anchor_in, scale_ref, out_ref, owned_ref, anchor_ref, sems,
    *, seg_tiles, col_tiles, span,
):
    copies = [
        pltpu.make_async_copy(owned_in, owned_ref, sems.at[0]),
        pltpu.make_async_copy(anchor_in, anchor_ref, sems.at[1]),
    ]
    for copy in copies:
        copy.start()
    for copy in copies:
        copy.wait()
    seg_max = scale_ref.shape[0]
    me = lax.axis_index("slab") * lax.axis_size("col") + lax.axis_index("col")
    owners = []
    for i in range(seg_max):
        seg = owned_ref[me * seg_max + i]
        safe = jnp.maximum(seg, 0)
        lane = anchor_ref[0, safe] // seg_tiles
        owner = lane * span + lax.rem(anchor_ref[1, safe], col_tiles)
        owner = jnp.where(seg >= 0, owner, -1)
        place = jnp.int32(0)
        for other in owners:
            place = place + jnp.where(other == owner, 1, 0)
        owners.append(owner)

        @pl.when((seg >= 0) & (place < CAP))
        def _(i=i, owner=owner, place=place):
            out_ref[owner * CAP + place] = scale_ref[i : i + 1, :]


def segments_kernel(
    count_ref, full_ref, seg_ref, few_row_ref, all_row_ref, index_ref, x_ref, table_ref,
    prec_in, few_ref, all_ref, out_ref,
    prec_ref, ahead_ref, behind_ref, turned, weighted, zbuf, scale_row, adj, grid,
    prec_sem, scale_sem, *, width, sizes,
):
    parts, chunk, lanes = out_ref.shape
    order = prec_ref.shape[0]
    blocks = order // lanes
    pieces = order // width
    batch = sizes[-1]
    count = count_ref[0]
    full = full_ref[0]

    def prec_copy(i):
        cols = pl.ds(pl.multiple_of(i * width, width), width)
        return pltpu.make_async_copy(prec_in.at[:, cols], prec_ref.at[:, cols], prec_sem.at[i])

    def scale_copy(source, row, j):
        return pltpu.make_async_copy(source.at[row], scale_row.at[j], scale_sem.at[j])

    def fetch(g):
        for j in range(batch):
            e = g * batch + j

            @pl.when((e < count) & (full == 0))
            def _(e=e, j=j):
                scale_copy(few_ref, few_row_ref[e], j).start()

            @pl.when((e < count) & (full != 0))
            def _(e=e, j=j):
                scale_copy(all_ref, all_row_ref[e], j).start()

            @pl.when(e >= count)
            def _(j=j):
                scale_row[j] = jnp.zeros((1, order), jnp.float32)

    prec_copy(0).start()
    fetch(0)
    prec_copy(1).start()

    def side(b, carry):
        block = table_ref[b].astype(jnp.float32)
        blank = jnp.zeros_like(block)
        for ref, value in ((ahead_ref, block.T), (behind_ref, block)):
            ref[0, b] = jnp.concatenate([value, blank], axis=1).astype(jnp.bfloat16)
            ref[1, b] = jnp.concatenate([blank, value], axis=1).astype(jnp.bfloat16)
        return carry

    lax.fori_loop(0, table_ref.shape[0], side, 0, unroll=4)

    def turn(q, carry):
        part = pl.ds(pl.multiple_of(q * lanes, lanes), lanes)
        turned[:, part] = x_ref[part, :].astype(jnp.float32).T.astype(jnp.bfloat16)
        adj[:, part] = jnp.zeros((lanes, lanes), jnp.float32)
        return carry

    lax.fori_loop(0, blocks, turn, 0, unroll=4)

    def work(g, size, live):
        ids = []
        for j in range(size):
            e = g * batch + j
            ids.append(seg_ref[jnp.minimum(e, count - 1)])

            @pl.when(j < live)
            def _(j=j):
                scale_copy(few_ref, 0, j).wait()

        def pair_of(table, q):
            sides = []
            for j in range(size):
                low = table[0, index_ref[2 * q, ids[j]]]
                high = table[1, index_ref[2 * q + 1, ids[j]]]
                sides.append(jnp.concatenate([low, high], axis=0))
            return sides

        def interp(q, carry):
            part = pl.ds(pl.multiple_of(q * lanes, lanes), lanes)
            right = jnp.concatenate(pair_of(ahead_ref, q), axis=1)
            seg = jnp.dot(turned[:, part], right, preferred_element_type=jnp.float32)
            seg = seg.astype(jnp.bfloat16).astype(jnp.float32)
            for j in range(size):
                value = seg[:, j * lanes : (j + 1) * lanes] * scale_row[j, :, part]
                weighted[j * lanes : (j + 1) * lanes, part] = value.astype(jnp.bfloat16)
            return carry

        lax.fori_loop(0, blocks, interp, 0, unroll=4 if size <= 4 else 2)

        def product(i, carry):
            cols = pl.ds(pl.multiple_of(i * width, width), width)

            @pl.when(g == 0)
            def _():
                prec_copy(i).wait()

            @pl.when((g == 0) & (i + 2 < pieces))
            def _():
                prec_copy(i + 2).start()

            cuts = (0, size) if size <= 8 else (0, size // 2, size)
            for low, high in zip(cuts, cuts[1:]):
                prod = jnp.dot(
                    weighted[low * lanes : high * lanes, :], prec_ref[:, cols],
                    preferred_element_type=jnp.float32,
                )
                for j in range(low, high):
                    value = prod[(j - low) * lanes : (j - low + 1) * lanes]
                    rows = slice(j * lanes, (j + 1) * lanes)
                    zbuf[rows, cols] = (value * scale_row[j, :, cols]).astype(jnp.bfloat16)
            return carry

        lax.fori_loop(0, pieces, product, 0)

        def back(q, carry):
            part = pl.ds(pl.multiple_of(q * lanes, lanes), lanes)
            left = jnp.concatenate(
                [zbuf[j * lanes : (j + 1) * lanes, part] for j in range(size)], axis=1
            )
            right = jnp.concatenate(pair_of(behind_ref, q), axis=0)
            adj[:, part] = adj[:, part] + jnp.dot(left, right, preferred_element_type=jnp.float32)
            return carry

        lax.fori_loop(0, blocks, back, 0, unroll=4 if size <= 4 else 2)

    def whole_group(g, carry):
        work(g, batch, batch)
        fetch(g + 1)
        return carry

    lax.fori_loop(0, count // batch, whole_group, 0)
    rest = lax.rem(count, batch)
    smaller = 0
    for size in sizes:

        @pl.when((rest > smaller) & (rest <= size))
        def _(size=size):
            work(count // batch, size, rest)

        smaller = size

    @pl.when(count == 0)
    def _():
        for i in range(2):
            prec_copy(i).wait()

    zero = jnp.zeros((HALO, lanes), jnp.float32)
    grid[pl.ds(0, HALO), :] = zero
    grid[pl.ds(order + HALO, HALO), :] = zero

    def unturn(q, carry):
        part = pl.ds(pl.multiple_of(q * lanes, lanes), lanes)
        grid[pl.ds(pl.multiple_of(q * lanes + HALO, HALO), lanes), :] = adj[:, part].T
        return carry

    lax.fori_loop(0, blocks, unturn, 0, unroll=4)
    own = order // parts
    first = HALO - (chunk - own) // 2
    for s in range(parts):
        out_ref[s] = grid[pl.ds(s * own + first, chunk), :].astype(jnp.bfloat16)


def vmem_spec():
    return pl.BlockSpec(memory_space=pltpu.VMEM)


def hbm_spec():
    return pl.BlockSpec(memory_space=pltpu.HBM)


def smem_spec():
    return pl.BlockSpec(memory_space=pltpu.SMEM)


def owner_tables(
    owned_segments, seg_anchor, seg_tiles, seg_max, dev_count, col_count, span, col_tiles, my_device
):
    segs = seg_anchor.shape[0]
    slots = dev_count * seg_max
    slot_ids = jnp.arange(slots, dtype=jnp.int32)
    used = owned_segments >= 0
    seg_hot = owned_segments[:, None] == jnp.arange(segs, dtype=jnp.int32)[None, :]
    anchor_row = jnp.sum(jnp.where(seg_hot, seg_anchor[None, :, 0], 0), axis=1)
    anchor_col = jnp.sum(jnp.where(seg_hot, seg_anchor[None, :, 1], 0), axis=1)
    owner_slab = anchor_row // seg_tiles * span + anchor_col % col_tiles
    owner = owner_slab * col_count + anchor_col // col_tiles
    owner = jnp.where(used, owner, -1)
    by_dev = owner.reshape(dev_count, seg_max)
    slot_in = jnp.arange(seg_max, dtype=jnp.int32)
    before = slot_in[None, :] < slot_in[:, None]
    same = (by_dev[:, :, None] == by_dev[:, None, :]) & before[None]
    place = jnp.sum(same.astype(jnp.int32), axis=2).reshape(slots)
    overflow = jnp.max(jnp.where(used, place, 0)) >= CAP
    mine = owner == my_device
    rank = jnp.cumsum(mine.astype(jnp.int32)) - 1
    count = jnp.sum(mine.astype(jnp.int32))
    longest = segs
    pick = mine[None, :] & (rank[None, :] == jnp.arange(longest, dtype=jnp.int32)[:, None])
    src_slab = slot_ids // (seg_max * col_count)
    columns = [
        owned_segments,
        src_slab * CAP + jnp.minimum(place, CAP - 1),
        src_slab * seg_max + slot_ids % seg_max,
    ]
    listed = [jnp.sum(jnp.where(pick, col[None, :], 0), axis=1) for col in columns]
    return count, listed, overflow, owner_slab, used, slot_in


def per_device(
    direction, kappa, land_mask, owned_segments, seg_anchor,
    interp_index, interp_table, precision, obs_scale,
):
    rows_dev, cols_dev = direction.shape
    blocks, tile_r, _ = interp_table.shape
    order = precision.shape[0]
    _, seg_tiles = interp_index.shape
    seg_max = obs_scale.shape[0]
    lanes = TILE_C
    col_tiles = cols_dev // lanes
    slab_count = lax.axis_size("slab")
    col_count = lax.axis_size("col")
    dev_count = slab_count * col_count
    span = order // rows_dev
    assert span == col_tiles and col_count == 2 and slab_count % span == 0
    groups = [list(range(i, i + span)) for i in range(0, slab_count, span)]
    if len(groups) == 1:
        groups = None
    my_slab = lax.axis_index("slab")
    my_col = lax.axis_index("col")
    my_device = my_slab * col_count + my_col
    is_low = my_col == 0

    def edge_cols(array):
        return jnp.where(is_low, array[:, cols_dev - lanes :], array[:, :lanes])

    edge_mask = edge_cols(land_mask).astype(jnp.float32)
    edge = jnp.stack([edge_cols(direction) * edge_mask, edge_cols(kappa) * edge_mask])
    nbr = lax.ppermute(edge, "col", [(0, 1), (1, 0)])
    near = jnp.where(
        is_low, lane_iota((1, lanes)) < SWEEPS, lane_iota((1, lanes)) >= lanes - SWEEPS
    )
    nbr = jnp.where(near[None], nbr, 0.0)

    def edge_rows(start):
        part = slice(start, start + SWEEPS)
        maskf = land_mask[part].astype(jnp.float32)
        field = jnp.concatenate([direction[part] * maskf, nbr[0, part]], axis=1)
        coeff = jnp.concatenate([kappa[part] * maskf, nbr[1, part]], axis=1)
        return jnp.concatenate([field, coeff], axis=0)

    first_rows, last_rows = edge_rows(0), edge_rows(rows_dev - SWEEPS)
    even = my_slab % 2 == 0
    pairs_a = [(i, i ^ 1) for i in range(slab_count)]
    pairs_b = [(i, i + 1) for i in range(1, slab_count - 1, 2)]
    pairs_b = pairs_b + [(j, i) for i, j in pairs_b]
    got_b = lax.ppermute(jnp.where(even, first_rows, last_rows), "slab", pairs_b)
    got_a = lax.ppermute(jnp.where(even, last_rows, first_rows), "slab", pairs_a)

    def swap(array, groups=None):
        return lax.all_to_all(
            array, "slab", split_axis=0, concat_axis=0, tiled=True, axis_index_groups=groups
        )

    scales_out = pl.pallas_call(
        functools.partial(outbox_kernel, seg_tiles=seg_tiles, col_tiles=col_tiles, span=span),
        out_shape=jax.ShapeDtypeStruct((slab_count * CAP, 1, order), jnp.float32),
        in_specs=[hbm_spec(), hbm_spec(), vmem_spec()],
        out_specs=vmem_spec(),
        scratch_shapes=[
            pltpu.SMEM(owned_segments.shape, jnp.int32),
            pltpu.SMEM(seg_anchor.shape[::-1], jnp.int32),
            pltpu.SemaphoreType.DMA((2,)),
        ],
        name="outbox",
    )(owned_segments, seg_anchor.T, obs_scale)
    few = swap(scales_out)

    count, listed, overflow, owner_slab, used, slot_in = owner_tables(
        owned_segments, seg_anchor, seg_tiles, seg_max, dev_count, col_count, span,
        col_tiles, my_device,
    )

    tiles = col_tiles + 1
    height = rows_dev + 2 * PAD
    buf = pltpu.VMEM((tiles, height, lanes), jnp.float32)
    own_float = pltpu.VMEM((rows_dev, cols_dev), jnp.float32)
    own_int = pltpu.VMEM((rows_dev, cols_dev), jnp.int32)
    face_shape = jax.ShapeDtypeStruct((tiles, height, lanes), jnp.float32)
    smoothed, fn, fw = pl.pallas_call(
        smooth_first_kernel,
        out_shape=(
            jax.ShapeDtypeStruct((col_tiles, rows_dev, lanes), jnp.bfloat16),
            face_shape, face_shape,
        ),
        in_specs=[hbm_spec()] * 3 + [vmem_spec()] * 3,
        out_specs=(hbm_spec(),) * 3,
        scratch_shapes=[own_float, own_float, own_int]
        + [pltpu.VMEM((col_tiles, rows_dev, lanes), jnp.bfloat16)]
        + [buf] * 7
        + [pltpu.SemaphoreType.DMA((3, CHUNKS)), pltpu.SemaphoreType.DMA((4,))],
        cost_estimate=pl.CostEstimate(flops=40000000, bytes_accessed=8 << 20, transcendentals=0),
        name="smooth_first",
    )(direction, kappa, land_mask, nbr, got_a, got_b)

    gathered = swap(smoothed, groups)

    my_owner = lax.dynamic_slice_in_dim(owner_slab, my_device * seg_max, seg_max)
    my_used = lax.dynamic_slice_in_dim(used, my_device * seg_max, seg_max)

    def outbox(cap, position):
        target = jnp.arange(slab_count * cap, dtype=jnp.int32)
        hit = (
            (my_owner * cap + position)[None, :] == target[:, None]
        ) & (my_used & (position < cap))[None, :]
        slot = jnp.sum(jnp.where(hit, slot_in[None, :], 0), axis=1)
        return obs_scale[slot].reshape(slab_count * cap, 1, order)

    many = (slab_count * seg_max, 1, order)
    everything = lax.cond(
        overflow,
        lambda: swap(outbox(seg_max, slot_in)),
        lambda: pl.pallas_call(
            lambda out_ref: None,
            out_shape=jax.ShapeDtypeStruct(many, jnp.float32),
            out_specs=hbm_spec(),
            name="unread",
        )(),
    )

    chunk = rows_dev + 2 * SWEEPS
    width = order // 4
    sizes = tuple(range(1, 11))
    batch = sizes[-1]

    returning = pl.pallas_call(
        functools.partial(segments_kernel, width=width, sizes=sizes),
        out_shape=jax.ShapeDtypeStruct((span, chunk, lanes), jnp.bfloat16),
        in_specs=[smem_spec()] * 6 + [vmem_spec()] * 2 + [hbm_spec()] * 3,
        out_specs=vmem_spec(),
        scratch_shapes=[
            pltpu.VMEM((order, order), jnp.bfloat16),
            pltpu.VMEM((2, blocks, tile_r, 2 * tile_r), jnp.bfloat16),
            pltpu.VMEM((2, blocks, tile_r, 2 * tile_r), jnp.bfloat16),
            pltpu.VMEM((lanes, order), jnp.bfloat16),
            pltpu.VMEM((batch * lanes, order), jnp.bfloat16),
            pltpu.VMEM((batch * lanes, order), jnp.bfloat16),
            pltpu.VMEM((batch, 1, order), jnp.float32),
            pltpu.VMEM((lanes, order), jnp.float32),
            pltpu.VMEM((order + 2 * HALO, lanes), jnp.float32),
            pltpu.SemaphoreType.DMA((order // width,)),
            pltpu.SemaphoreType.DMA((batch,)),
        ],
        compiler_params=pltpu.CompilerParams(vmem_limit_bytes=57 << 20),
        cost_estimate=pl.CostEstimate(
            flops=8 * 2 * order * order * lanes, bytes_accessed=12 << 20, transcendentals=0
        ),
        name="segments",
    )(
        count.reshape(1), overflow.astype(jnp.int32).reshape(1), *listed, interp_index.T,
        gathered.reshape(order, lanes), interp_table, precision, few, everything,
    )

    returned = swap(returning, groups)

    if groups is not None:
        returned = lane_edges(returned, slab_count, span, my_slab, rows_dev)

    border = jnp.where(is_low, returned[col_tiles - 1], returned[0])
    border = lax.ppermute(border, "col", [(0, 1), (1, 0)])
    return pl.pallas_call(
        smooth_last_kernel,
        out_shape=jax.ShapeDtypeStruct((rows_dev, cols_dev), jnp.float32),
        in_specs=[vmem_spec()] * 2 + [hbm_spec()] * 4,
        out_specs=vmem_spec(),
        scratch_shapes=[buf] * 4
        + [own_float, own_int, buf, buf]
        + [pltpu.SemaphoreType.DMA((2, CHUNKS)), pltpu.SemaphoreType.DMA((2,))],
        cost_estimate=pl.CostEstimate(flops=40000000, bytes_accessed=8 << 20, transcendentals=0),
        name="smooth_last",
    )(returned, border, fn, fw, direction, land_mask)


def lane_edges(returned, slab_count, span, my_slab, rows_dev):
    halo = SWEEPS
    up = [(i, i + 1) for i in range(span - 1, slab_count - 1, span)]
    down = [(j, i) for i, j in up]
    own = returned[:, halo : halo + rows_dev]
    above = lax.ppermute(own[:, rows_dev - halo :], "slab", up)
    below = lax.ppermute(own[:, :halo], "slab", down)
    first = my_slab % span == 0
    last = my_slab % span == span - 1
    head = jnp.where(first, above, returned[:, :halo])
    tail = jnp.where(last, below, returned[:, halo + rows_dev :])
    return jnp.concatenate([head, own, tail], axis=1)


def solution(mesh):
    in_specs = (
        P("slab", "col"),
        P("slab", "col"),
        P("slab", "col"),
        P(),
        P(),
        P(),
        P(),
        P(),
        P(("slab", "col"), None),
    )

    return jax.shard_map(
        per_device, mesh=mesh, in_specs=in_specs, out_specs=P("slab", "col"), check_vma=False
    )
```

```python
import functools

import jax
import jax.numpy as jnp
from jax import lax
from jax.experimental import pallas as pl
from jax.experimental.pallas import tpu as pltpu
from jax.sharding import PartitionSpec as P


TILE_C = 128
SWEEPS = 4
HALO = 8
PAD = 16
CHUNKS = 4
CAP = 4


def lane_iota(shape):
    return lax.broadcasted_iota(jnp.int32, shape, len(shape) - 1)


def row_iota(shape):
    return lax.broadcasted_iota(jnp.int32, shape, len(shape) - 2)


def from_left(own, left):
    lanes = own.shape[-1]
    return pltpu.roll(jnp.where(lane_iota(own.shape) == lanes - 1, left, own), 1, 1)


def from_right(own, right):
    lanes = own.shape[-1]
    return pltpu.roll(jnp.where(lane_iota(own.shape) == 0, right, own), lanes - 1, 1)


def face(own, other):
    return jnp.where(jnp.minimum(own, other) > 0, own + other, 0.0)


def derive(tiles, rows, own_ref, fn_ref, fw_ref, fe_ref):
    def tile(c, right):
        body = pl.ds(HALO, rows)
        west = fw_ref[c, body, :]
        east = from_right(west, fw_ref[right, body, :])
        fe_ref[c, body, :] = east
        vertical = fn_ref[c, body, :] + fn_ref[c, pl.ds(HALO + 1, rows), :]
        own_ref[c, body, :] = 1.0 - (vertical + (west + east))

    def step(c, carry):
        tile(c, c + 1)
        return carry

    lax.fori_loop(0, tiles - 1, step, 0, unroll=2)
    tile(tiles - 1, 0)


def sweeps(tiles, rows, bufs, own_ref, fn_ref, fw_ref, fe_ref, finish, before_last=None, part_done=None):
    for step in range(SWEEPS):
        src, dst = bufs[step % 2], bufs[1 - step % 2]
        last = step == SWEEPS - 1
        first_row = PAD if last else HALO
        parts = 2 if last else 3
        if last and before_last is not None:
            before_last()
        length = (rows - 2 * (PAD - HALO) if last else rows) // parts

        for index in range(parts):
            start = first_row + index * length
            body = pl.ds(start, length)

            def tile(c, right, u_left, u, src=src, dst=dst, last=last, start=start, body=body):
                u_right = src[right, body, :]
                up = src[c, pl.ds(start - 1, length), :]
                down = src[c, pl.ds(start + 1, length), :]
                out = own_ref[c, body, :] * u + fn_ref[c, body, :] * up
                out = out + fn_ref[c, pl.ds(start + 1, length), :] * down
                out = out + fw_ref[c, body, :] * from_left(u, u_left)
                out = out + fe_ref[c, body, :] * from_right(u, u_right)
                if last:
                    finish(c, start - PAD, out)
                else:
                    dst[c, body, :] = out
                return u, u_right

            def step_tile(c, carry):
                return tile(c, c + 1, *carry)

            carry = src[tiles - 1, body, :], src[0, body, :]
            carry = lax.fori_loop(0, tiles - 1, step_tile, carry, unroll=8)
            if not last:
                tile(tiles - 1, 0, *carry)
            elif part_done is not None:
                part_done(start - PAD, length)


def chunk_of(tiles, k):
    return k * tiles // CHUNKS, (k + 1) * tiles // CHUNKS


def column_chunks(refs, scratch, sems, tiles, lanes):
    copies = []
    for k in range(CHUNKS):
        low, high = chunk_of(tiles, k)
        cols = pl.ds(low * lanes, (high - low) * lanes)
        copies.append([
            pltpu.make_async_copy(ref.at[:, cols], buf.at[:, cols], sems.at[i, k])
            for i, (ref, buf) in enumerate(zip(refs, scratch))
        ])
    return copies


def smooth_first_kernel(
    dir_in, kap_in, mask_in, nbr_ref, got_a_ref, got_b_ref,
    out_ref, fn_out, fw_out,
    dir_ref, kap_ref, mask_ref, done, own_ref, fn_ref, fw_ref, fe_ref, u0, u1, kbuf,
    load_sems, sems,
):
    tiles, _, lanes = u0.shape
    loads = column_chunks(
        (dir_in, kap_in, mask_in), (dir_ref, kap_ref, mask_ref), load_sems, tiles - 1, lanes
    )
    for load in sum(loads, []):
        load.start()
    own = dir_ref.shape[0]
    rows = own + 2 * HALO
    edge = (HALO, lanes)
    zero = jnp.zeros(edge, jnp.float32)
    even = lax.rem(lax.axis_index("slab"), 2) == 0
    low = row_iota(edge) < HALO // 2

    def edges(c, cols):
        got_a, got_b = got_a_ref[:, cols], got_b_ref[:, cols]
        top = jnp.where(even, got_b, got_a)
        bot = jnp.where(even, got_a, got_b)
        u0[c, pl.ds(HALO, HALO), :] = jnp.where(low, 0.0, pltpu.roll(top, HALO // 2, 0))
        kbuf[c, pl.ds(HALO, HALO), :] = jnp.where(low, 0.0, 0.5 * top)
        u0[c, pl.ds(PAD + own, HALO), :] = jnp.where(low, bot, 0.0)
        kbuf[c, pl.ds(PAD + own, HALO), :] = jnp.where(
            low, 0.5 * pltpu.roll(bot, HALO // 2, 0), 0.0
        )
        for part in (pl.ds(0, HALO), pl.ds(PAD + own + HALO, HALO)):
            u0[c, part, :] = zero
            u1[c, part, :] = zero
            kbuf[c, part, :] = zero
        fn_ref[c, pl.ds(PAD + own + HALO, HALO), :] = zero

    def fill(c, carry):
        cols = pl.ds(pl.multiple_of(c * lanes, lanes), lanes)
        maskf = mask_ref[:, cols].astype(jnp.float32)
        u0[c, pl.ds(PAD, own), :] = dir_ref[:, cols] * maskf
        kbuf[c, pl.ds(PAD, own), :] = kap_ref[:, cols] * (0.5 * maskf)
        edges(c, cols)
        return carry

    u0[tiles - 1, pl.ds(PAD, own), :] = nbr_ref[0]
    kbuf[tiles - 1, pl.ds(PAD, own), :] = 0.5 * nbr_ref[1]
    edges(tiles - 1, pl.ds((tiles - 1) * lanes, lanes))

    def faces(c, k_left):
        body = pl.ds(HALO, rows)
        k = kbuf[c, body, :]
        fn_ref[c, body, :] = face(k, kbuf[c, pl.ds(HALO - 1, rows), :])
        fw_ref[c, body, :] = face(k, from_left(k, k_left))
        return k

    k_left = kbuf[tiles - 1, pl.ds(HALO, rows), :]
    for k in range(CHUNKS):
        for load in loads[k]:
            load.wait()
        low_tile, high_tile = chunk_of(tiles - 1, k)
        lax.fori_loop(low_tile, high_tile, fill, 0)
        k_left = lax.fori_loop(low_tile, high_tile, faces, k_left)
    faces(tiles - 1, k_left)
    copies = [
        pltpu.make_async_copy(ref, out, sems.at[i])
        for i, (ref, out) in enumerate(((fn_ref, fn_out), (fw_ref, fw_out)))
    ]
    for copy in copies:
        copy.start()
    derive(tiles, rows, own_ref, fn_ref, fw_ref, fe_ref)

    def finish(c, row, value):
        done[c, pl.ds(row, value.shape[0]), :] = value.astype(jnp.bfloat16)

    def part_done(row, length):
        part = pl.ds(row, length)
        copy = pltpu.make_async_copy(
            done.at[:, part, :], out_ref.at[:, part, :], sems.at[len(copies)]
        )
        copies.append(copy)
        copy.start()

    sweeps(tiles, rows, (u0, u1), own_ref, fn_ref, fw_ref, fe_ref, finish, part_done=part_done)
    for copy in copies:
        copy.wait()


def smooth_last_kernel(
    ret_ref, nbr_ref, fn_ref, fw_ref, dir_in, mask_in, out_ref,
    own_ref, fe_ref, dir_ref, mask_ref, u0, u1, load_sems,
):
    tiles, _, lanes = u0.shape
    loads = sum(
        column_chunks((dir_in, mask_in), (dir_ref, mask_ref), load_sems, tiles - 1, lanes), []
    )
    for load in loads:
        load.start()
    own, chunk = dir_ref.shape[0], ret_ref.shape[1]
    rows = own + 2 * HALO
    zero = jnp.zeros((PAD, lanes), jnp.float32)

    def put(c, value):
        for part in (pl.ds(0, PAD), pl.ds(PAD + own, PAD)):
            u0[c, part, :] = zero
            u1[c, part, :] = zero
        u0[c, pl.ds(PAD - (chunk - own) // 2, chunk), :] = value.astype(jnp.float32)

    def fill(c, carry):
        put(c, ret_ref[c])
        return carry

    lax.fori_loop(0, tiles - 1, fill, 0)
    put(tiles - 1, nbr_ref[...])
    derive(tiles, rows, own_ref, fn_ref, fw_ref, fe_ref)

    def finish(c, row, value):
        cols = pl.ds(pl.multiple_of(c * lanes, lanes), lanes)
        part = pl.ds(row, value.shape[0])
        maskf = mask_ref[part, cols].astype(jnp.float32)
        out_ref[part, cols] = maskf * (dir_ref[part, cols] * maskf + value)

    def before_last():
        for load in loads:
            load.wait()

    sweeps(tiles, rows, (u0, u1), own_ref, fn_ref, fw_ref, fe_ref, finish, before_last)


def outbox_kernel(
    owned_in, anchor_in, scale_ref, out_ref, owned_ref, anchor_ref, sems,
    *, seg_tiles, col_tiles, span,
):
    copies = [
        pltpu.make_async_copy(owned_in, owned_ref, sems.at[0]),
        pltpu.make_async_copy(anchor_in, anchor_ref, sems.at[1]),
    ]
    for copy in copies:
        copy.start()
    for copy in copies:
        copy.wait()
    seg_max = scale_ref.shape[0]
    me = lax.axis_index("slab") * lax.axis_size("col") + lax.axis_index("col")
    owners = []
    for i in range(seg_max):
        seg = owned_ref[me * seg_max + i]
        safe = jnp.maximum(seg, 0)
        lane = anchor_ref[0, safe] // seg_tiles
        owner = lane * span + lax.rem(anchor_ref[1, safe], col_tiles)
        owner = jnp.where(seg >= 0, owner, -1)
        place = jnp.int32(0)
        for other in owners:
            place = place + jnp.where(other == owner, 1, 0)
        owners.append(owner)

        @pl.when((seg >= 0) & (place < CAP))
        def _(i=i, owner=owner, place=place):
            out_ref[owner * CAP + place] = scale_ref[i : i + 1, :]


def segments_kernel(
    count_ref, full_ref, seg_ref, few_row_ref, all_row_ref, index_ref, x_ref, table_ref,
    prec_in, few_ref, all_ref, out_ref,
    prec_ref, ahead_ref, behind_ref, turned, weighted, zbuf, scale_row, adj, grid,
    prec_sem, scale_sem, *, width, sizes,
):
    parts, chunk, lanes = out_ref.shape
    order = prec_ref.shape[0]
    blocks = order // lanes
    pieces = order // width
    batch = sizes[-1]
    count = count_ref[0]
    full = full_ref[0]

    def prec_copy(i):
        cols = pl.ds(pl.multiple_of(i * width, width), width)
        return pltpu.make_async_copy(prec_in.at[:, cols], prec_ref.at[:, cols], prec_sem.at[i])

    def scale_copy(source, row, j):
        return pltpu.make_async_copy(source.at[row], scale_row.at[j], scale_sem.at[j])

    def fetch(g):
        for j in range(batch):
            e = g * batch + j

            @pl.when((e < count) & (full == 0))
            def _(e=e, j=j):
                scale_copy(few_ref, few_row_ref[e], j).start()

            @pl.when((e < count) & (full != 0))
            def _(e=e, j=j):
                scale_copy(all_ref, all_row_ref[e], j).start()

            @pl.when(e >= count)
            def _(j=j):
                scale_row[j] = jnp.zeros((1, order), jnp.float32)

    prec_copy(0).start()
    fetch(0)
    prec_copy(1).start()

    def side(b, carry):
        block = table_ref[b].astype(jnp.float32)
        blank = jnp.zeros_like(block)
        for ref, value in ((ahead_ref, block.T), (behind_ref, block)):
            ref[0, b] = jnp.concatenate([value, blank], axis=1).astype(jnp.bfloat16)
            ref[1, b] = jnp.concatenate([blank, value], axis=1).astype(jnp.bfloat16)
        return carry

    lax.fori_loop(0, table_ref.shape[0], side, 0, unroll=4)

    def turn(q, carry):
        part = pl.ds(pl.multiple_of(q * lanes, lanes), lanes)
        turned[:, part] = x_ref[part, :].astype(jnp.float32).T.astype(jnp.bfloat16)
        adj[:, part] = jnp.zeros((lanes, lanes), jnp.float32)
        return carry

    lax.fori_loop(0, blocks, turn, 0, unroll=4)

    def work(g, size, live):
        ids = []
        for j in range(size):
            e = g * batch + j
            ids.append(seg_ref[jnp.minimum(e, count - 1)])

            @pl.when(j < live)
            def _(j=j):
                scale_copy(few_ref, 0, j).wait()

        def pair_of(table, q):
            sides = []
            for j in range(size):
                low = table[0, index_ref[2 * q, ids[j]]]
                high = table[1, index_ref[2 * q + 1, ids[j]]]
                sides.append(jnp.concatenate([low, high], axis=0))
            return sides

        def interp(q, carry):
            part = pl.ds(pl.multiple_of(q * lanes, lanes), lanes)
            right = jnp.concatenate(pair_of(ahead_ref, q), axis=1)
            seg = jnp.dot(turned[:, part], right, preferred_element_type=jnp.float32)
            seg = seg.astype(jnp.bfloat16).astype(jnp.float32)
            for j in range(size):
                value = seg[:, j * lanes : (j + 1) * lanes] * scale_row[j, :, part]
                weighted[j * lanes : (j + 1) * lanes, part] = value.astype(jnp.bfloat16)
            return carry

        lax.fori_loop(0, blocks, interp, 0, unroll=4 if size <= 4 else 2)

        def product(i, carry):
            cols = pl.ds(pl.multiple_of(i * width, width), width)

            @pl.when(g == 0)
            def _():
                prec_copy(i).wait()

            @pl.when((g == 0) & (i + 2 < pieces))
            def _():
                prec_copy(i + 2).start()

            cuts = (0, size) if size <= 8 else (0, size // 2, size)
            for low, high in zip(cuts, cuts[1:]):
                prod = jnp.dot(
                    weighted[low * lanes : high * lanes, :], prec_ref[:, cols],
                    preferred_element_type=jnp.float32,
                )
                for j in range(low, high):
                    value = prod[(j - low) * lanes : (j - low + 1) * lanes]
                    rows = slice(j * lanes, (j + 1) * lanes)
                    zbuf[rows, cols] = (value * scale_row[j, :, cols]).astype(jnp.bfloat16)
            return carry

        lax.fori_loop(0, pieces, product, 0)

        def back(q, carry):
            part = pl.ds(pl.multiple_of(q * lanes, lanes), lanes)
            left = jnp.concatenate(
                [zbuf[j * lanes : (j + 1) * lanes, part] for j in range(size)], axis=1
            )
            right = jnp.concatenate(pair_of(behind_ref, q), axis=0)
            adj[:, part] = adj[:, part] + jnp.dot(left, right, preferred_element_type=jnp.float32)
            return carry

        lax.fori_loop(0, blocks, back, 0, unroll=4 if size <= 4 else 2)

    def whole_group(g, carry):
        work(g, batch, batch)
        fetch(g + 1)
        return carry

    lax.fori_loop(0, count // batch, whole_group, 0)
    rest = lax.rem(count, batch)
    smaller = 0
    for size in sizes:

        @pl.when((rest > smaller) & (rest <= size))
        def _(size=size):
            work(count // batch, size, rest)

        smaller = size

    @pl.when(count == 0)
    def _():
        for i in range(2):
            prec_copy(i).wait()

    zero = jnp.zeros((HALO, lanes), jnp.float32)
    grid[pl.ds(0, HALO), :] = zero
    grid[pl.ds(order + HALO, HALO), :] = zero

    def unturn(q, carry):
        part = pl.ds(pl.multiple_of(q * lanes, lanes), lanes)
        grid[pl.ds(pl.multiple_of(q * lanes + HALO, HALO), lanes), :] = adj[:, part].T
        return carry

    lax.fori_loop(0, blocks, unturn, 0, unroll=4)
    own = order // parts
    first = HALO - (chunk - own) // 2
    for s in range(parts):
        out_ref[s] = grid[pl.ds(s * own + first, chunk), :].astype(jnp.bfloat16)


def vmem_spec():
    return pl.BlockSpec(memory_space=pltpu.VMEM)


def hbm_spec():
    return pl.BlockSpec(memory_space=pltpu.HBM)


def smem_spec():
    return pl.BlockSpec(memory_space=pltpu.SMEM)


def owner_tables(
    owned_segments, seg_anchor, seg_tiles, seg_max, dev_count, col_count, span, col_tiles, my_device
):
    segs = seg_anchor.shape[0]
    slots = dev_count * seg_max
    slot_ids = jnp.arange(slots, dtype=jnp.int32)
    used = owned_segments >= 0
    seg_hot = owned_segments[:, None] == jnp.arange(segs, dtype=jnp.int32)[None, :]
    anchor_row = jnp.sum(jnp.where(seg_hot, seg_anchor[None, :, 0], 0), axis=1)
    anchor_col = jnp.sum(jnp.where(seg_hot, seg_anchor[None, :, 1], 0), axis=1)
    owner_slab = anchor_row // seg_tiles * span + anchor_col % col_tiles
    owner = owner_slab * col_count + anchor_col // col_tiles
    owner = jnp.where(used, owner, -1)
    by_dev = owner.reshape(dev_count, seg_max)
    slot_in = jnp.arange(seg_max, dtype=jnp.int32)
    before = slot_in[None, :] < slot_in[:, None]
    same = (by_dev[:, :, None] == by_dev[:, None, :]) & before[None]
    place = jnp.sum(same.astype(jnp.int32), axis=2).reshape(slots)
    overflow = jnp.max(jnp.where(used, place, 0)) >= CAP
    mine = owner == my_device
    rank = jnp.cumsum(mine.astype(jnp.int32)) - 1
    count = jnp.sum(mine.astype(jnp.int32))
    longest = segs
    pick = mine[None, :] & (rank[None, :] == jnp.arange(longest, dtype=jnp.int32)[:, None])
    src_slab = slot_ids // (seg_max * col_count)
    columns = [
        owned_segments,
        src_slab * CAP + jnp.minimum(place, CAP - 1),
        src_slab * seg_max + slot_ids % seg_max,
    ]
    listed = [jnp.sum(jnp.where(pick, col[None, :], 0), axis=1) for col in columns]
    return count, listed, overflow, owner_slab, used, slot_in


def per_device(
    direction, kappa, land_mask, owned_segments, seg_anchor,
    interp_index, interp_table, precision, obs_scale,
):
    rows_dev, cols_dev = direction.shape
    blocks, tile_r, _ = interp_table.shape
    order = precision.shape[0]
    _, seg_tiles = interp_index.shape
    seg_max = obs_scale.shape[0]
    lanes = TILE_C
    col_tiles = cols_dev // lanes
    slab_count = lax.axis_size("slab")
    col_count = lax.axis_size("col")
    dev_count = slab_count * col_count
    span = order // rows_dev
    assert span == col_tiles and col_count == 2 and slab_count % span == 0
    groups = [list(range(i, i + span)) for i in range(0, slab_count, span)]
    if len(groups) == 1:
        groups = None
    my_slab = lax.axis_index("slab")
    my_col = lax.axis_index("col")
    my_device = my_slab * col_count + my_col
    is_low = my_col == 0

    def edge_cols(array):
        return jnp.where(is_low, array[:, cols_dev - lanes :], array[:, :lanes])

    edge_mask = edge_cols(land_mask).astype(jnp.float32)
    edge = jnp.stack([edge_cols(direction) * edge_mask, edge_cols(kappa) * edge_mask])
    nbr = lax.ppermute(edge, "col", [(0, 1), (1, 0)])
    near = jnp.where(
        is_low, lane_iota((1, lanes)) < SWEEPS, lane_iota((1, lanes)) >= lanes - SWEEPS
    )
    nbr = jnp.where(near[None], nbr, 0.0)

    def edge_rows(start):
        part = slice(start, start + SWEEPS)
        maskf = land_mask[part].astype(jnp.float32)
        field = jnp.concatenate([direction[part] * maskf, nbr[0, part]], axis=1)
        coeff = jnp.concatenate([kappa[part] * maskf, nbr[1, part]], axis=1)
        return jnp.concatenate([field, coeff], axis=0)

    first_rows, last_rows = edge_rows(0), edge_rows(rows_dev - SWEEPS)
    even = my_slab % 2 == 0
    pairs_a = [(i, i ^ 1) for i in range(slab_count)]
    pairs_b = [(i, i + 1) for i in range(1, slab_count - 1, 2)]
    pairs_b = pairs_b + [(j, i) for i, j in pairs_b]
    got_b = lax.ppermute(jnp.where(even, first_rows, last_rows), "slab", pairs_b)
    got_a = lax.ppermute(jnp.where(even, last_rows, first_rows), "slab", pairs_a)

    def swap(array, groups=None):
        return lax.all_to_all(
            array, "slab", split_axis=0, concat_axis=0, tiled=True, axis_index_groups=groups
        )

    scales_out = pl.pallas_call(
        functools.partial(outbox_kernel, seg_tiles=seg_tiles, col_tiles=col_tiles, span=span),
        out_shape=jax.ShapeDtypeStruct((slab_count * CAP, 1, order), jnp.float32),
        in_specs=[hbm_spec(), hbm_spec(), vmem_spec()],
        out_specs=vmem_spec(),
        scratch_shapes=[
            pltpu.SMEM(owned_segments.shape, jnp.int32),
            pltpu.SMEM(seg_anchor.shape[::-1], jnp.int32),
            pltpu.SemaphoreType.DMA((2,)),
        ],
        name="outbox",
    )(owned_segments, seg_anchor.T, obs_scale)
    few = swap(scales_out)

    tiles = col_tiles + 1
    height = rows_dev + 2 * PAD
    buf = pltpu.VMEM((tiles, height, lanes), jnp.float32)
    own_float = pltpu.VMEM((rows_dev, cols_dev), jnp.float32)
    own_int = pltpu.VMEM((rows_dev, cols_dev), jnp.int32)
    face_shape = jax.ShapeDtypeStruct((tiles, height, lanes), jnp.float32)
    smoothed, fn, fw = pl.pallas_call(
        smooth_first_kernel,
        out_shape=(
            jax.ShapeDtypeStruct((col_tiles, rows_dev, lanes), jnp.bfloat16),
            face_shape, face_shape,
        ),
        in_specs=[hbm_spec()] * 3 + [vmem_spec()] * 3,
        out_specs=(hbm_spec(),) * 3,
        scratch_shapes=[own_float, own_float, own_int]
        + [pltpu.VMEM((col_tiles, rows_dev, lanes), jnp.bfloat16)]
        + [buf] * 7
        + [pltpu.SemaphoreType.DMA((3, CHUNKS)), pltpu.SemaphoreType.DMA((4,))],
        compiler_params=pltpu.CompilerParams(vmem_limit_bytes=58 << 20),
        cost_estimate=pl.CostEstimate(flops=40000000, bytes_accessed=8 << 20, transcendentals=0),
        name="smooth_first",
    )(direction, kappa, land_mask, nbr, got_a, got_b)

    smoothed, owned_segments, seg_anchor, obs_scale = lax.optimization_barrier(
        (smoothed, owned_segments, seg_anchor, obs_scale)
    )
    gathered = swap(smoothed, groups)

    count, listed, overflow, owner_slab, used, slot_in = owner_tables(
        owned_segments, seg_anchor, seg_tiles, seg_max, dev_count, col_count, span,
        col_tiles, my_device,
    )

    my_owner = lax.dynamic_slice_in_dim(owner_slab, my_device * seg_max, seg_max)
    my_used = lax.dynamic_slice_in_dim(used, my_device * seg_max, seg_max)

    def outbox(cap, position):
        target = jnp.arange(slab_count * cap, dtype=jnp.int32)
        hit = (
            (my_owner * cap + position)[None, :] == target[:, None]
        ) & (my_used & (position < cap))[None, :]
        slot = jnp.sum(jnp.where(hit, slot_in[None, :], 0), axis=1)
        return obs_scale[slot].reshape(slab_count * cap, 1, order)

    many = (slab_count * seg_max, 1, order)
    everything = lax.cond(
        overflow,
        lambda: swap(outbox(seg_max, slot_in)),
        lambda: pl.pallas_call(
            lambda out_ref: None,
            out_shape=jax.ShapeDtypeStruct(many, jnp.float32),
            out_specs=hbm_spec(),
            name="unread",
        )(),
    )

    chunk = rows_dev + 2 * SWEEPS
    width = order // 4
    sizes = tuple(range(1, 11))
    batch = sizes[-1]

    returning = pl.pallas_call(
        functools.partial(segments_kernel, width=width, sizes=sizes),
        out_shape=jax.ShapeDtypeStruct((span, chunk, lanes), jnp.bfloat16),
        in_specs=[smem_spec()] * 6 + [vmem_spec()] * 2 + [hbm_spec()] * 3,
        out_specs=vmem_spec(),
        scratch_shapes=[
            pltpu.VMEM((order, order), jnp.bfloat16),
            pltpu.VMEM((2, blocks, tile_r, 2 * tile_r), jnp.bfloat16),
            pltpu.VMEM((2, blocks, tile_r, 2 * tile_r), jnp.bfloat16),
            pltpu.VMEM((lanes, order), jnp.bfloat16),
            pltpu.VMEM((batch * lanes, order), jnp.bfloat16),
            pltpu.VMEM((batch * lanes, order), jnp.bfloat16),
            pltpu.VMEM((batch, 1, order), jnp.float32),
            pltpu.VMEM((lanes, order), jnp.float32),
            pltpu.VMEM((order + 2 * HALO, lanes), jnp.float32),
            pltpu.SemaphoreType.DMA((order // width,)),
            pltpu.SemaphoreType.DMA((batch,)),
        ],
        compiler_params=pltpu.CompilerParams(vmem_limit_bytes=45 << 20),
        cost_estimate=pl.CostEstimate(
            flops=8 * 2 * order * order * lanes, bytes_accessed=12 << 20, transcendentals=0
        ),
        name="segments",
    )(
        count.reshape(1), overflow.astype(jnp.int32).reshape(1), *listed, interp_index.T,
        gathered.reshape(order, lanes), interp_table, precision, few, everything,
    )

    returned = swap(returning, groups)

    if groups is not None:
        returned = lane_edges(returned, slab_count, span, my_slab, rows_dev)

    border = jnp.where(is_low, returned[col_tiles - 1], returned[0])
    border = lax.ppermute(border, "col", [(0, 1), (1, 0)])
    return pl.pallas_call(
        smooth_last_kernel,
        out_shape=jax.ShapeDtypeStruct((rows_dev, cols_dev), jnp.float32),
        in_specs=[vmem_spec()] * 4 + [hbm_spec()] * 2,
        out_specs=vmem_spec(),
        scratch_shapes=[buf] * 2
        + [own_float, own_int, buf, buf]
        + [pltpu.SemaphoreType.DMA((2, CHUNKS))],
        compiler_params=pltpu.CompilerParams(vmem_limit_bytes=45 << 20),
        cost_estimate=pl.CostEstimate(flops=40000000, bytes_accessed=8 << 20, transcendentals=0),
        name="smooth_last",
    )(returned, border, fn, fw, direction, land_mask)


def lane_edges(returned, slab_count, span, my_slab, rows_dev):
    halo = SWEEPS
    up = [(i, i + 1) for i in range(span - 1, slab_count - 1, span)]
    down = [(j, i) for i, j in up]
    own = returned[:, halo : halo + rows_dev]
    above = lax.ppermute(own[:, rows_dev - halo :], "slab", up)
    below = lax.ppermute(own[:, :halo], "slab", down)
    first = my_slab % span == 0
    last = my_slab % span == span - 1
    head = jnp.where(first, above, returned[:, :halo])
    tail = jnp.where(last, below, returned[:, halo + rows_dev :])
    return jnp.concatenate([head, own, tail], axis=1)


def solution(mesh):
    in_specs = (
        P("slab", "col"),
        P("slab", "col"),
        P("slab", "col"),
        P(),
        P(),
        P(),
        P(),
        P(),
        P(("slab", "col"), None),
    )

    return jax.shard_map(
        per_device, mesh=mesh, in_specs=in_specs, out_specs=P("slab", "col"), check_vma=False
    )
```

```python
import functools

import jax
import jax.numpy as jnp
from jax import lax
from jax.experimental import pallas as pl
from jax.experimental.pallas import tpu as pltpu
from jax.sharding import PartitionSpec as P


TILE_C = 128
SWEEPS = 4
HALO = 8
PAD = 16
CHUNKS = 4
CAP = 3


def lane_iota(shape):
    return lax.broadcasted_iota(jnp.int32, shape, len(shape) - 1)


def row_iota(shape):
    return lax.broadcasted_iota(jnp.int32, shape, len(shape) - 2)


def from_left(own, left):
    lanes = own.shape[-1]
    return pltpu.roll(jnp.where(lane_iota(own.shape) == lanes - 1, left, own), 1, 1)


def from_right(own, right):
    lanes = own.shape[-1]
    return pltpu.roll(jnp.where(lane_iota(own.shape) == 0, right, own), lanes - 1, 1)


def face(own, other):
    return jnp.where(jnp.minimum(own, other) > 0, own + other, 0.0)


def derive(tiles, rows, own_ref, fn_ref, fw_ref, fe_ref):
    def tile(c, right):
        body = pl.ds(HALO, rows)
        west = fw_ref[c, body, :]
        east = from_right(west, fw_ref[right, body, :])
        fe_ref[c, body, :] = east
        vertical = fn_ref[c, body, :] + fn_ref[c, pl.ds(HALO + 1, rows), :]
        own_ref[c, body, :] = 1.0 - (vertical + (west + east))

    def step(c, carry):
        tile(c, c + 1)
        return carry

    lax.fori_loop(0, tiles - 1, step, 0, unroll=4)
    tile(tiles - 1, 0)


def sweeps(tiles, rows, bufs, own_ref, fn_ref, fw_ref, fe_ref, finish, before_last=None, part_done=None):
    for step in range(SWEEPS):
        src, dst = bufs[step % 2], bufs[1 - step % 2]
        last = step == SWEEPS - 1
        first_row = PAD if last else HALO
        parts = 4 if last else 6
        if last and before_last is not None:
            before_last()
        length = (rows - 2 * (PAD - HALO) if last else rows) // parts

        for index in range(parts):
            start = first_row + index * length
            body = pl.ds(start, length)

            def tile(c, right, u_left, u, src=src, dst=dst, last=last, start=start, body=body):
                u_right = src[right, body, :]
                up = src[c, pl.ds(start - 1, length), :]
                down = src[c, pl.ds(start + 1, length), :]
                out = own_ref[c, body, :] * u + fn_ref[c, body, :] * up
                out = out + fn_ref[c, pl.ds(start + 1, length), :] * down
                out = out + fw_ref[c, body, :] * from_left(u, u_left)
                out = out + fe_ref[c, body, :] * from_right(u, u_right)
                if last:
                    finish(c, start - PAD, out)
                else:
                    dst[c, body, :] = out
                return u, u_right

            def step_tile(c, carry):
                return tile(c, c + 1, *carry)

            carry = src[tiles - 1, body, :], src[0, body, :]
            carry = lax.fori_loop(0, tiles - 1, step_tile, carry, unroll=True)
            if not last:
                tile(tiles - 1, 0, *carry)
            elif part_done is not None:
                part_done(start - PAD, length)


def chunk_of(tiles, k):
    return k * tiles // CHUNKS, (k + 1) * tiles // CHUNKS


def column_chunks(refs, scratch, sems, tiles, lanes):
    copies = []
    for k in range(CHUNKS):
        low, high = chunk_of(tiles, k)
        cols = pl.ds(low * lanes, (high - low) * lanes)
        copies.append([
            pltpu.make_async_copy(ref.at[:, cols], buf.at[:, cols], sems.at[i, k])
            for i, (ref, buf) in enumerate(zip(refs, scratch))
        ])
    return copies


def smooth_first_kernel(
    dir_in, kap_in, mask_in, nbr_ref, got_a_ref, got_b_ref, corner_ref,
    out_ref, fn_out, fw_out,
    dir_ref, kap_ref, mask_ref, done, own_ref, fn_ref, fw_ref, fe_ref, u0, u1, kbuf,
    load_sems, sems,
):
    tiles, _, lanes = u0.shape
    loads = column_chunks(
        (dir_in, kap_in, mask_in), (dir_ref, kap_ref, mask_ref), load_sems, tiles - 1, lanes
    )
    for load in sum(loads, []):
        load.start()
    own = dir_ref.shape[0]
    rows = own + 2 * HALO
    edge = (HALO, lanes)
    zero = jnp.zeros(edge, jnp.float32)
    even = lax.rem(lax.axis_index("slab"), 2) == 0
    low = row_iota(edge) < HALO // 2

    def edges(c, got_a, got_b):
        top = jnp.where(even, got_b, got_a)
        bot = jnp.where(even, got_a, got_b)
        u0[c, pl.ds(HALO, HALO), :] = jnp.where(low, 0.0, pltpu.roll(top, HALO // 2, 0))
        kbuf[c, pl.ds(HALO, HALO), :] = jnp.where(low, 0.0, 0.5 * top)
        u0[c, pl.ds(PAD + own, HALO), :] = jnp.where(low, bot, 0.0)
        kbuf[c, pl.ds(PAD + own, HALO), :] = jnp.where(
            low, 0.5 * pltpu.roll(bot, HALO // 2, 0), 0.0
        )
        for part in (pl.ds(0, HALO), pl.ds(PAD + own + HALO, HALO)):
            u0[c, part, :] = zero
            u1[c, part, :] = zero
            kbuf[c, part, :] = zero
        fn_ref[c, pl.ds(PAD + own + HALO, HALO), :] = zero

    def fill(c, carry):
        cols = pl.ds(pl.multiple_of(c * lanes, lanes), lanes)
        maskf = mask_ref[:, cols].astype(jnp.float32)
        u0[c, pl.ds(PAD, own), :] = dir_ref[:, cols] * maskf
        kbuf[c, pl.ds(PAD, own), :] = kap_ref[:, cols] * (0.5 * maskf)
        edges(c, got_a_ref[:, cols], got_b_ref[:, cols])
        return carry

    u0[tiles - 1, pl.ds(PAD, own), :] = nbr_ref[0]
    kbuf[tiles - 1, pl.ds(PAD, own), :] = 0.5 * nbr_ref[1]
    edges(tiles - 1, corner_ref[0], corner_ref[1])
    lane = lane_iota((rows, lanes))
    near = jnp.where(lax.axis_index("col") == 0, lanes - 1 - lane, lane) >= lanes - SWEEPS
    body = pl.ds(HALO, rows)
    kbuf[tiles - 1, body, :] = jnp.where(near, kbuf[tiles - 1, body, :], 0.0)

    def faces(c, k_left):
        body = pl.ds(HALO, rows)
        k = kbuf[c, body, :]
        fn_ref[c, body, :] = face(k, kbuf[c, pl.ds(HALO - 1, rows), :])
        fw_ref[c, body, :] = face(k, from_left(k, k_left))
        return k

    k_left = kbuf[tiles - 1, pl.ds(HALO, rows), :]
    for k in range(CHUNKS):
        for load in loads[k]:
            load.wait()
        low_tile, high_tile = chunk_of(tiles - 1, k)
        lax.fori_loop(low_tile, high_tile, fill, 0, unroll=True)
        k_left = lax.fori_loop(low_tile, high_tile, faces, k_left, unroll=True)
    faces(tiles - 1, k_left)
    copies = [
        pltpu.make_async_copy(ref, out, sems.at[i])
        for i, (ref, out) in enumerate(((fn_ref, fn_out), (fw_ref, fw_out)))
    ]
    for copy in copies:
        copy.start()
    derive(tiles, rows, own_ref, fn_ref, fw_ref, fe_ref)

    def finish(c, row, value):
        done[c, pl.ds(row, value.shape[0]), :] = value.astype(jnp.bfloat16)

    def part_done(row, length):
        part = pl.ds(row, length)
        copy = pltpu.make_async_copy(
            done.at[:, part, :], out_ref.at[:, part, :], sems.at[len(copies)]
        )
        copies.append(copy)
        copy.start()

    sweeps(tiles, rows, (u0, u1), own_ref, fn_ref, fw_ref, fe_ref, finish, part_done=part_done)
    for copy in copies:
        copy.wait()


def smooth_last_kernel(
    ret_ref, nbr_ref, fn_ref, fw_ref, dir_in, mask_in, out_ref,
    own_ref, fe_ref, dir_ref, mask_ref, u0, u1, load_sems,
):
    tiles, _, lanes = u0.shape
    loads = sum(
        column_chunks((dir_in, mask_in), (dir_ref, mask_ref), load_sems, tiles - 1, lanes), []
    )
    for load in loads:
        load.start()
    own, chunk = dir_ref.shape[0], ret_ref.shape[1]
    rows = own + 2 * HALO
    zero = jnp.zeros((PAD, lanes), jnp.float32)

    def put(c, value):
        for part in (pl.ds(0, PAD), pl.ds(PAD + own, PAD)):
            u0[c, part, :] = zero
            u1[c, part, :] = zero
        u0[c, pl.ds(PAD - (chunk - own) // 2, chunk), :] = value.astype(jnp.float32)

    def fill(c, carry):
        put(c, ret_ref[c])
        return carry

    lax.fori_loop(0, tiles - 1, fill, 0)
    put(tiles - 1, nbr_ref[...])
    derive(tiles, rows, own_ref, fn_ref, fw_ref, fe_ref)

    def finish(c, row, value):
        cols = pl.ds(pl.multiple_of(c * lanes, lanes), lanes)
        part = pl.ds(row, value.shape[0])
        maskf = mask_ref[part, cols].astype(jnp.float32)
        out_ref[part, cols] = maskf * (dir_ref[part, cols] * maskf + value)

    def before_last():
        for load in loads:
            load.wait()

    sweeps(tiles, rows, (u0, u1), own_ref, fn_ref, fw_ref, fe_ref, finish, before_last)


def prepare_kernel(
    dir_in, kap_in, mask_in, owned_in, anchor_in, scale_in,
    edge_ref, send_a_ref, send_b_ref, out_ref,
    edges, edge_mask, tops, top_mask, bottoms, bottom_mask, owned_ref, anchor_ref, scale_ref,
    sems, *, seg_tiles, col_tiles, span,
):
    rows, cols = dir_in.shape
    lanes = edge_ref.shape[-1]
    is_low = lax.axis_index("col") == 0
    at = pl.ds(pl.multiple_of(jnp.where(is_low, cols - lanes, 0), lanes), lanes)
    low, high = pl.ds(0, HALO), pl.ds(rows - HALO, HALO)
    pairs = [(owned_in, owned_ref), (anchor_in, anchor_ref), (scale_in, scale_ref)]
    for i, source in enumerate((dir_in, kap_in)):
        pairs.append((source.at[:, at], edges.at[i]))
        pairs.append((source.at[low, :], tops.at[i]))
        pairs.append((source.at[high, :], bottoms.at[i]))
    pairs.append((mask_in.at[:, at], edge_mask))
    pairs.append((mask_in.at[low, :], top_mask))
    pairs.append((mask_in.at[high, :], bottom_mask))
    copies = [pltpu.make_async_copy(a, b, sems.at[i]) for i, (a, b) in enumerate(pairs)]
    for copy in copies:
        copy.start()
    for copy in copies:
        copy.wait()

    maskf = edge_mask[...].astype(jnp.float32)
    edge_ref[0] = edges[0] * maskf
    edge_ref[1] = edges[1] * maskf
    upper = row_iota((HALO, cols)) < HALO // 2
    maskf = top_mask[...].astype(jnp.float32)
    first = jnp.where(upper, tops[0] * maskf, pltpu.roll(tops[1] * maskf, HALO // 2, 0))
    maskf = bottom_mask[...].astype(jnp.float32)
    last = jnp.where(upper, pltpu.roll(bottoms[0] * maskf, HALO // 2, 0), bottoms[1] * maskf)
    even = lax.rem(lax.axis_index("slab"), 2) == 0
    send_a_ref[...] = jnp.where(even, last, first)
    send_b_ref[...] = jnp.where(even, first, last)

    seg_max = scale_ref.shape[0]
    me = lax.axis_index("slab") * lax.axis_size("col") + lax.axis_index("col")
    owners = []
    for i in range(seg_max):
        seg = owned_ref[me * seg_max + i]
        safe = jnp.maximum(seg, 0)
        lane = anchor_ref[0, safe] // seg_tiles
        owner = lane * span + lax.rem(anchor_ref[1, safe], col_tiles)
        owner = jnp.where(seg >= 0, owner, -1)
        place = jnp.int32(0)
        for other in owners:
            place = place + jnp.where(other == owner, 1, 0)
        owners.append(owner)

        @pl.when((seg >= 0) & (place < CAP))
        def _(i=i, owner=owner, place=place):
            out_ref[owner * CAP + place] = scale_ref[i : i + 1, :]


def segments_kernel(
    count_ref, seg_ref, second_ref, row_ref, index_ref, x_ref, table_ref,
    prec_in, few_ref, all_ref, out_ref,
    prec_ref, ahead_ref, behind_ref, turned, weighted, zbuf, scale_row, adj, grid,
    prec_sem, scale_sem, *, width, sizes,
):
    parts, chunk, lanes = out_ref.shape
    order = prec_ref.shape[0]
    blocks = order // lanes
    pieces = order // width
    batch = sizes[-1]
    count = count_ref[0]

    def prec_copy(i):
        cols = pl.ds(pl.multiple_of(i * width, width), width)
        return pltpu.make_async_copy(prec_in.at[:, cols], prec_ref.at[:, cols], prec_sem.at[i])

    def scale_copy(source, row, j):
        return pltpu.make_async_copy(source.at[row], scale_row.at[j], scale_sem.at[j])

    def fetch(g):
        for j in range(batch):
            e = g * batch + j

            second = second_ref[jnp.minimum(e, seg_ref.shape[0] - 1)]

            @pl.when((e < count) & (second == 0))
            def _(e=e, j=j):
                scale_copy(few_ref, row_ref[e], j).start()

            @pl.when((e < count) & (second != 0))
            def _(e=e, j=j):
                scale_copy(all_ref, row_ref[e], j).start()

            @pl.when(e >= count)
            def _(j=j):
                scale_row[j] = jnp.zeros((1, order), jnp.float32)

    prec_copy(0).start()
    fetch(0)
    prec_copy(1).start()

    def side(b, carry):
        block = table_ref[b].astype(jnp.float32)
        blank = jnp.zeros_like(block)
        for ref, value in ((ahead_ref, block.T), (behind_ref, block)):
            ref[0, b] = jnp.concatenate([value, blank], axis=1).astype(jnp.bfloat16)
            ref[1, b] = jnp.concatenate([blank, value], axis=1).astype(jnp.bfloat16)
        return carry

    lax.fori_loop(0, table_ref.shape[0], side, 0, unroll=4)

    def turn(q, carry):
        part = pl.ds(pl.multiple_of(q * lanes, lanes), lanes)
        turned[:, part] = x_ref[part, :].astype(jnp.float32).T.astype(jnp.bfloat16)
        adj[:, part] = jnp.zeros((lanes, lanes), jnp.float32)
        return carry

    lax.fori_loop(0, blocks, turn, 0, unroll=4)

    def work(g, size, live):
        ids = []
        for j in range(size):
            e = g * batch + j
            ids.append(seg_ref[jnp.minimum(e, count - 1)])

            @pl.when(j < live)
            def _(j=j):
                scale_copy(few_ref, 0, j).wait()

        def pair_of(table, q):
            sides = []
            for j in range(size):
                low = table[0, index_ref[2 * q, ids[j]]]
                high = table[1, index_ref[2 * q + 1, ids[j]]]
                sides.append(jnp.concatenate([low, high], axis=0))
            return sides

        def interp(q, carry):
            part = pl.ds(pl.multiple_of(q * lanes, lanes), lanes)
            right = jnp.concatenate(pair_of(ahead_ref, q), axis=1)
            seg = jnp.dot(turned[:, part], right, preferred_element_type=jnp.float32)
            seg = seg.astype(jnp.bfloat16).astype(jnp.float32)
            for j in range(size):
                value = seg[:, j * lanes : (j + 1) * lanes] * scale_row[j, :, part]
                weighted[j * lanes : (j + 1) * lanes, part] = value.astype(jnp.bfloat16)
            return carry

        lax.fori_loop(0, blocks, interp, 0, unroll=4)

        def product(i, carry):
            cols = pl.ds(pl.multiple_of(i * width, width), width)

            @pl.when(g == 0)
            def _():
                prec_copy(i).wait()

            @pl.when((g == 0) & (i + 2 < pieces))
            def _():
                prec_copy(i + 2).start()

            cuts = (0, size) if size <= 8 else (0, size // 2, size)
            for low, high in zip(cuts, cuts[1:]):
                prod = jnp.dot(
                    weighted[low * lanes : high * lanes, :], prec_ref[:, cols],
                    preferred_element_type=jnp.float32,
                )
                for j in range(low, high):
                    value = prod[(j - low) * lanes : (j - low + 1) * lanes]
                    rows = slice(j * lanes, (j + 1) * lanes)
                    zbuf[rows, cols] = (value * scale_row[j, :, cols]).astype(jnp.bfloat16)
            return carry

        lax.fori_loop(0, pieces, product, 0)

        def back(q, carry):
            part = pl.ds(pl.multiple_of(q * lanes, lanes), lanes)
            left = jnp.concatenate(
                [zbuf[j * lanes : (j + 1) * lanes, part] for j in range(size)], axis=1
            )
            right = jnp.concatenate(pair_of(behind_ref, q), axis=0)
            adj[:, part] = adj[:, part] + jnp.dot(left, right, preferred_element_type=jnp.float32)
            return carry

        lax.fori_loop(0, blocks, back, 0, unroll=4)

    def whole_group(g, carry):
        work(g, batch, batch)
        fetch(g + 1)
        return carry

    lax.fori_loop(0, count // batch, whole_group, 0)
    rest = lax.rem(count, batch)
    smaller = 0
    for size in sizes:

        @pl.when((rest > smaller) & (rest <= size))
        def _(size=size):
            work(count // batch, size, rest)

        smaller = size

    @pl.when(count == 0)
    def _():
        for i in range(2):
            prec_copy(i).wait()

    zero = jnp.zeros((HALO, lanes), jnp.float32)
    grid[pl.ds(0, HALO), :] = zero
    grid[pl.ds(order + HALO, HALO), :] = zero

    def unturn(q, carry):
        part = pl.ds(pl.multiple_of(q * lanes, lanes), lanes)
        grid[pl.ds(pl.multiple_of(q * lanes + HALO, HALO), lanes), :] = adj[:, part].T
        return carry

    lax.fori_loop(0, blocks, unturn, 0, unroll=4)
    own = order // parts
    first = HALO - (chunk - own) // 2
    for s in range(parts):
        out_ref[s] = grid[pl.ds(s * own + first, chunk), :].astype(jnp.bfloat16)


def vmem_spec():
    return pl.BlockSpec(memory_space=pltpu.VMEM)


def hbm_spec():
    return pl.BlockSpec(memory_space=pltpu.HBM)


def smem_spec():
    return pl.BlockSpec(memory_space=pltpu.SMEM)


def owner_tables(
    owned_segments, seg_anchor, seg_tiles, seg_max, dev_count, col_count, span, col_tiles, my_device
):
    segs = seg_anchor.shape[0]
    slots = dev_count * seg_max
    slot_ids = jnp.arange(slots, dtype=jnp.int32)
    used = owned_segments >= 0
    seg_hot = owned_segments[:, None] == jnp.arange(segs, dtype=jnp.int32)[None, :]
    anchor_row = jnp.sum(jnp.where(seg_hot, seg_anchor[None, :, 0], 0), axis=1)
    anchor_col = jnp.sum(jnp.where(seg_hot, seg_anchor[None, :, 1], 0), axis=1)
    owner_slab = anchor_row // seg_tiles * span + anchor_col % col_tiles
    owner = owner_slab * col_count + anchor_col // col_tiles
    owner = jnp.where(used, owner, -1)
    by_dev = owner.reshape(dev_count, seg_max)
    slot_in = jnp.arange(seg_max, dtype=jnp.int32)
    before = slot_in[None, :] < slot_in[:, None]
    same = (by_dev[:, :, None] == by_dev[:, None, :]) & before[None]
    place = jnp.sum(same.astype(jnp.int32), axis=2).reshape(slots)
    worst = jnp.max(jnp.where(used, place, 0))
    mode = (worst >= CAP).astype(jnp.int32) + (worst > CAP).astype(jnp.int32)
    mine = owner == my_device
    rank = jnp.cumsum(mine.astype(jnp.int32)) - 1
    count = jnp.sum(mine.astype(jnp.int32))
    longest = segs
    pick = mine[None, :] & (rank[None, :] == jnp.arange(longest, dtype=jnp.int32)[:, None])
    src_slab = slot_ids // (seg_max * col_count)
    second = (mode == 2) | ((mode == 1) & (place >= CAP))
    whole = src_slab * seg_max + slot_ids % seg_max
    row = jnp.where(mode == 2, whole, src_slab)
    row = jnp.where(second, row, src_slab * CAP + jnp.minimum(place, CAP - 1))
    columns = [owned_segments, second.astype(jnp.int32), row]
    listed = [jnp.sum(jnp.where(pick, col[None, :], 0), axis=1) for col in columns]
    return count, listed, mode, owner_slab, used, place, slot_in


def per_device(
    direction, kappa, land_mask, owned_segments, seg_anchor,
    interp_index, interp_table, precision, obs_scale,
):
    rows_dev, cols_dev = direction.shape
    blocks, tile_r, _ = interp_table.shape
    order = precision.shape[0]
    _, seg_tiles = interp_index.shape
    seg_max = obs_scale.shape[0]
    lanes = TILE_C
    col_tiles = cols_dev // lanes
    slab_count = lax.axis_size("slab")
    col_count = lax.axis_size("col")
    dev_count = slab_count * col_count
    span = order // rows_dev
    assert span == col_tiles and col_count == 2 and slab_count % span == 0
    groups = [list(range(i, i + span)) for i in range(0, slab_count, span)]
    if len(groups) == 1:
        groups = None
    my_slab = lax.axis_index("slab")
    my_col = lax.axis_index("col")
    my_device = my_slab * col_count + my_col
    is_low = my_col == 0

    def swap(array, groups=None):
        return lax.all_to_all(
            array, "slab", split_axis=0, concat_axis=0, tiled=True, axis_index_groups=groups
        )

    vm = pltpu.VMEM
    edge, send_a, send_b, scales_out = pl.pallas_call(
        functools.partial(
            prepare_kernel, seg_tiles=seg_tiles, col_tiles=col_tiles, span=span
        ),
        out_shape=(
            jax.ShapeDtypeStruct((2, rows_dev, lanes), jnp.float32),
            jax.ShapeDtypeStruct((HALO, cols_dev), jnp.float32),
            jax.ShapeDtypeStruct((HALO, cols_dev), jnp.float32),
            jax.ShapeDtypeStruct((slab_count * CAP, 1, order), jnp.float32),
        ),
        in_specs=[hbm_spec()] * 6,
        out_specs=(vmem_spec(),) * 4,
        scratch_shapes=[
            vm((2, rows_dev, lanes), jnp.float32), vm((rows_dev, lanes), jnp.int32),
            vm((2, HALO, cols_dev), jnp.float32), vm((HALO, cols_dev), jnp.int32),
            vm((2, HALO, cols_dev), jnp.float32), vm((HALO, cols_dev), jnp.int32),
            pltpu.SMEM(owned_segments.shape, jnp.int32),
            pltpu.SMEM(seg_anchor.shape[::-1], jnp.int32),
            vm(obs_scale.shape, jnp.float32),
            pltpu.SemaphoreType.DMA((12,)),
        ],
        compiler_params=pltpu.CompilerParams(vmem_limit_bytes=60 << 20),
        name="prepare",
    )(direction, kappa, land_mask, owned_segments, seg_anchor.T, obs_scale)
    nbr = lax.ppermute(edge, "col", [(0, 1), (1, 0)])
    pairs_a = [(i, i ^ 1) for i in range(slab_count)]
    pairs_b = [(i, i + 1) for i in range(1, slab_count - 1, 2)]
    pairs_b = pairs_b + [(j, i) for i, j in pairs_b]
    got_b = lax.ppermute(send_b, "slab", pairs_b)
    got_a = lax.ppermute(send_a, "slab", pairs_a)

    corners = jnp.stack([got_a, got_b])
    corners = jnp.where(is_low, corners[:, :, cols_dev - lanes :], corners[:, :, :lanes])
    corners = lax.ppermute(corners, "col", [(0, 1), (1, 0)])
    few = swap(scales_out)

    tiles = col_tiles + 1
    height = rows_dev + 2 * PAD
    buf = pltpu.VMEM((tiles, height, lanes), jnp.float32)
    own_float = pltpu.VMEM((rows_dev, cols_dev), jnp.float32)
    own_int = pltpu.VMEM((rows_dev, cols_dev), jnp.int32)
    face_shape = jax.ShapeDtypeStruct((tiles, height, lanes), jnp.float32)
    smoothed, fn, fw = pl.pallas_call(
        smooth_first_kernel,
        out_shape=(
            jax.ShapeDtypeStruct((col_tiles, rows_dev, lanes), jnp.bfloat16),
            face_shape, face_shape,
        ),
        in_specs=[hbm_spec()] * 3 + [vmem_spec()] * 4,
        out_specs=(hbm_spec(),) * 3,
        scratch_shapes=[own_float, own_float, own_int]
        + [pltpu.VMEM((col_tiles, rows_dev, lanes), jnp.bfloat16)]
        + [buf] * 7
        + [pltpu.SemaphoreType.DMA((3, CHUNKS)), pltpu.SemaphoreType.DMA((6,))],
        compiler_params=pltpu.CompilerParams(vmem_limit_bytes=52 << 20),
        cost_estimate=pl.CostEstimate(flops=40000000, bytes_accessed=8 << 20, transcendentals=0),
        name="smooth_first",
    )(direction, kappa, land_mask, nbr, got_a, got_b, corners)

    smoothed, owned_segments, seg_anchor, obs_scale = lax.optimization_barrier(
        (smoothed, owned_segments, seg_anchor, obs_scale)
    )
    gathered = swap(smoothed, groups)

    count, listed, mode, owner_slab, used, place, slot_in = owner_tables(
        owned_segments, seg_anchor, seg_tiles, seg_max, dev_count, col_count, span,
        col_tiles, my_device,
    )

    my_owner = lax.dynamic_slice_in_dim(owner_slab, my_device * seg_max, seg_max)
    my_used = lax.dynamic_slice_in_dim(used, my_device * seg_max, seg_max)
    my_place = lax.dynamic_slice_in_dim(place, my_device * seg_max, seg_max)

    def outbox(cap, position):
        target = jnp.arange(slab_count * cap, dtype=jnp.int32)
        hit = (my_owner * cap + position)[None, :] == target[:, None]
        hit = hit & (my_used & (position >= 0) & (position < cap))[None, :]
        slot = jnp.sum(jnp.where(hit, slot_in[None, :], 0), axis=1)
        return obs_scale[slot].reshape(slab_count * cap, 1, order)

    many = (slab_count * seg_max, 1, order)

    def one_more():
        extra = swap(outbox(1, my_place - CAP))
        return lax.pad(extra, jnp.float32(0), ((0, many[0] - slab_count, 0), (0, 0, 0), (0, 0, 0)))

    def no_more():
        return pl.pallas_call(
            lambda out_ref: None,
            out_shape=jax.ShapeDtypeStruct(many, jnp.float32),
            out_specs=hbm_spec(),
            name="unread",
        )()

    everything = lax.switch(
        mode, [no_more, one_more, lambda: swap(outbox(seg_max, slot_in))]
    )

    chunk = rows_dev + 2 * SWEEPS
    width = order // 4
    sizes = tuple(range(1, 11))
    batch = sizes[-1]

    returning = pl.pallas_call(
        functools.partial(segments_kernel, width=width, sizes=sizes),
        out_shape=jax.ShapeDtypeStruct((span, chunk, lanes), jnp.bfloat16),
        in_specs=[smem_spec()] * 5 + [vmem_spec()] * 2 + [hbm_spec()] * 3,
        out_specs=vmem_spec(),
        scratch_shapes=[
            pltpu.VMEM((order, order), jnp.bfloat16),
            pltpu.VMEM((2, blocks, tile_r, 2 * tile_r), jnp.bfloat16),
            pltpu.VMEM((2, blocks, tile_r, 2 * tile_r), jnp.bfloat16),
            pltpu.VMEM((lanes, order), jnp.bfloat16),
            pltpu.VMEM((batch * lanes, order), jnp.bfloat16),
            pltpu.VMEM((batch * lanes, order), jnp.bfloat16),
            pltpu.VMEM((batch, 1, order), jnp.float32),
            pltpu.VMEM((lanes, order), jnp.float32),
            pltpu.VMEM((order + 2 * HALO, lanes), jnp.float32),
            pltpu.SemaphoreType.DMA((order // width,)),
            pltpu.SemaphoreType.DMA((batch,)),
        ],
        compiler_params=pltpu.CompilerParams(vmem_limit_bytes=45 << 20),
        cost_estimate=pl.CostEstimate(
            flops=8 * 2 * order * order * lanes, bytes_accessed=12 << 20, transcendentals=0
        ),
        name="segments",
    )(
        count.reshape(1), *listed, interp_index.T,
        gathered.reshape(order, lanes), interp_table, precision, few, everything,
    )

    returned = swap(returning, groups)

    if groups is not None:
        returned = lane_edges(returned, slab_count, span, my_slab, rows_dev)

    border = jnp.where(is_low, returned[col_tiles - 1], returned[0])
    border = lax.ppermute(border, "col", [(0, 1), (1, 0)])
    return pl.pallas_call(
        smooth_last_kernel,
        out_shape=jax.ShapeDtypeStruct((rows_dev, cols_dev), jnp.float32),
        in_specs=[vmem_spec()] * 4 + [hbm_spec()] * 2,
        out_specs=vmem_spec(),
        scratch_shapes=[buf] * 2
        + [own_float, own_int, buf, buf]
        + [pltpu.SemaphoreType.DMA((2, CHUNKS))],
        compiler_params=pltpu.CompilerParams(vmem_limit_bytes=45 << 20),
        cost_estimate=pl.CostEstimate(flops=40000000, bytes_accessed=8 << 20, transcendentals=0),
        name="smooth_last",
    )(returned, border, fn, fw, direction, land_mask)


def lane_edges(returned, slab_count, span, my_slab, rows_dev):
    halo = SWEEPS
    up = [(i, i + 1) for i in range(span - 1, slab_count - 1, span)]
    down = [(j, i) for i, j in up]
    own = returned[:, halo : halo + rows_dev]
    above = lax.ppermute(own[:, rows_dev - halo :], "slab", up)
    below = lax.ppermute(own[:, :halo], "slab", down)
    first = my_slab % span == 0
    last = my_slab % span == span - 1
    head = jnp.where(first, above, returned[:, :halo])
    tail = jnp.where(last, below, returned[:, halo + rows_dev :])
    return jnp.concatenate([head, own, tail], axis=1)


def solution(mesh):
    in_specs = (
        P("slab", "col"),
        P("slab", "col"),
        P("slab", "col"),
        P(),
        P(),
        P(),
        P(),
        P(),
        P(("slab", "col"), None),
    )

    return jax.shard_map(
        per_device, mesh=mesh, in_specs=in_specs, out_specs=P("slab", "col"), check_vma=False
    )
```
